128 devices in a mesh: gx: 8 (over z_lo, y), gy: 16 (over z_hi, x, core).
Axes of the slice: x: 4, y: 4, z: 4 (z_hi: 2, z_lo: 2; z = z_hi * 2 + z_lo), core: 2. Of those that a mesh axis runs over, the one named last changes fastest.
Arguments:
- ice_displacement: float32 [2, 64, 128, 128], P(None, 'gx', 'gy'), may hold values from -1.8 to 1.8
- ice_velocity: float32 [2, 64, 128, 128], P(None, 'gx', 'gy'), may hold values from -6 to 6
- jitter: float32 [2, 64, 128, 128], P(None, 'gx', 'gy'), may hold values from -0.2 to 0.2
- bond_mask: int32 [64, 128, 9], P('gx', 'gy'), may hold values from -2147483648 to 2147483647, as said below
- contact_node: int32 [128, 128], P('gy'), may hold values from 0 to 8388607, as said below
- intersection: float32 [128, 128], P('gy'), may hold values from -0.5 to 1
- shell_deflection: float32 [1024, 8192], P('gx', 'gy'), may hold values from -1.8 to 1.8
- shell_velocity: float32 [1024, 8192], P('gx', 'gy'), may hold values from -6 to 6
Outputs:
- ice_moved: float32 [2, 64, 128, 128], P(None, 'gx', 'gy')
- ice_speed: float32 [2, 64, 128, 128], P(None, 'gx', 'gy')
- shell_moved: float32 [1024, 8192], P('gx', 'gy')
- shell_speed: float32 [1024, 8192], P('gx', 'gy')
The draws below stay inside these ranges and needn't reach their ends.
Inputs may be any that keep to these rules, and one draw needn't show every extreme that they name: Bit 4 * i + k of bond_mask[a, b, s] (bit 31 being the sign bit) is 1 where the bonds from the points of lengthwise row i of tile (a, b) to the points q with 4 q // 128 == k of neighbouring tile s are intact. contact_node = r * 8192 + c for shell row r and column c; for point q of tile column t, c // 4 == t * 16 + q % 16 and r // 128 == q // 16.
All inputs are finite; a program needn't handle non-finite values.
Results may differ from the reference program's by a relative error of at most 0.0001.
Values sent between devices are 32-bit elements; how exact they have to be, the bound alone decides.
A program may use at most 64 MiB of HBM per device.

```python
import jax
import jax.numpy as jnp
from jax import lax

TILE_X = 8
TILE_Y = 16
PTS = 128
STEPS = 2
GX_T = 64
GY_T = 128
SH_H = 1024
SH_C = 8192
SHELL_NODES = 8388608


def draw_bond_mask(key, part):
    pieces = jax.random.randint(jax.random.fold_in(key, 3), (32, GX_T, GY_T, 9), 0, 5)
    intact = (pieces > 0).astype(jnp.int32)
    packed = jnp.zeros((GX_T, GY_T, 9), jnp.int32)
    for bit_place in range(31):
        packed = packed + intact[bit_place] * 2 ** bit_place
    return packed + intact[31] * jnp.int32(-2147483648)


def draw_contact_node(key, part):
    key_rows, key_cols = jax.random.split(jax.random.fold_in(key, 7), 2)
    band_rows = SH_H // TILE_X
    point_ids = jnp.arange(PTS, dtype=jnp.int32)
    tile_ids = jnp.arange(GY_T, dtype=jnp.int32)
    depth_row = (point_ids // TILE_Y)[None, :]
    lateral = tile_ids[:, None] * TILE_Y + (point_ids % TILE_Y)[None, :]
    row_ids = depth_row * band_rows + jax.random.randint(key_rows, (GY_T, PTS), 0, band_rows)
    col_ids = 4 * lateral + jax.random.randint(key_cols, (GY_T, PTS), 0, 4)
    return (row_ids * SH_C + col_ids).astype(jnp.int32)


def level_of(rng, extent, shards, low, top_value):
    def one(position, shards_of):
        steps = jax.random.uniform(jax.random.fold_in(jax.random.fold_in(rng, 6), position), (shards_of,), jnp.float32, low / len(shards), top_value / len(shards))
        return jnp.repeat(jnp.exp(steps), extent[position] // shards_of).reshape((-1,) + (1,) * (len(extent) - position - 1))

    factor_of = one(*shards[0])
    for cut in shards[1:]:
        factor_of = factor_of * one(*cut)
    return factor_of


def noise(rng, shape, width, limit, shards=(), held_as=jnp.bfloat16):
    factor_of = level_of(rng, shape, shards, -0.22, 0.18) if shards else 1.0
    result = jax.random.normal(rng, shape, jnp.float32) * width * factor_of
    return jnp.minimum(jnp.maximum(result, -limit), limit).astype(held_as)


def setup_inputs(seed: int = 0) -> dict:
    key_of = jax.random.split(jax.random.key(seed), 9)
    ice_displacement = noise(key_of[0], (2, GX_T, GY_T, PTS), 0.3, 1.8, ((1, 8), (2, 16)), jnp.float32)
    ice_velocity = noise(key_of[1], (2, GX_T, GY_T, PTS), 1.0, 6.0, ((1, 8), (2, 16)), jnp.float32)
    jitter = jnp.clip(jax.random.uniform(key_of[2], (2, GX_T, GY_T, PTS), jnp.float32, -0.2, 0.2) * level_of(key_of[2], (2, GX_T, GY_T, PTS), ((1, 8), (2, 16)), -0.4, 0.0), -0.2, 0.2)
    bond_mask = draw_bond_mask(jax.random.fold_in(key_of[8], 71), 0)
    contact_node = draw_contact_node(jax.random.fold_in(key_of[8], 71), 0)
    intersection = jnp.clip(-0.5 + 1.5 * jax.random.uniform(key_of[5], (GY_T, PTS), jnp.float32) ** level_of(key_of[5], (GY_T, PTS), ((0, 16),), -0.2, 0.2), -0.5, 1.0)
    shell_deflection = noise(key_of[6], (SH_H, SH_C), 0.3, 1.8, ((0, 8), (1, 16)), jnp.float32)
    shell_velocity = noise(key_of[7], (SH_H, SH_C), 1.0, 6.0, ((0, 8), (1, 16)), jnp.float32)
    return {"ice_displacement": ice_displacement, "ice_velocity": ice_velocity, "jitter": jitter, "bond_mask": bond_mask, "contact_node": contact_node, "intersection": intersection, "shell_deflection": shell_deflection, "shell_velocity": shell_velocity}


BOND_C = 1.0
HORIZON = 3.5
DELTA_SQ = 0.25
PENALTY = 4.0
BEND = 0.5
STEP_DT = 0.2

def pair_force(center, nearby, words, shift_x, shift_y):
    points = jnp.arange(TILE_X * TILE_Y, dtype=jnp.int32)
    bit_index = 4 * (points // TILE_Y)[:, None] + (4 * points // PTS)[None, :]
    intact = jnp.right_shift(words[..., None, None], bit_index) & 1
    lengthwise = (points // TILE_Y).astype(jnp.float32)
    sideways = (points % TILE_Y).astype(jnp.float32)
    base_x = shift_x * TILE_X + lengthwise[None, :] - lengthwise[:, None]
    base_y = shift_y * TILE_Y + sideways[None, :] - sideways[:, None]
    rest_x = base_x + (nearby[2][..., None, :] - center[2][..., :, None])
    rest_y = base_y + (nearby[3][..., None, :] - center[3][..., :, None])
    now_x = rest_x + (nearby[0][..., None, :] - center[0][..., :, None])
    now_y = rest_y + (nearby[1][..., None, :] - center[1][..., :, None])
    radius = jnp.sqrt(rest_x * rest_x + rest_y * rest_y + DELTA_SQ)
    stretched = jnp.sqrt(now_x * now_x + now_y * now_y + DELTA_SQ)
    reach = jnp.maximum(1.0 - radius / HORIZON, 0.0)
    factor = BOND_C * intact.astype(jnp.float32) * reach * reach * (stretched - radius) / (radius * stretched)
    return jnp.stack([lax.optimization_barrier(jnp.sum(factor * now_x, axis=-1)), lax.optimization_barrier(jnp.sum(factor * now_y, axis=-1))])

def ice_forces(displacement, jitter, bond_mask):
    rows = displacement.shape[1]
    columns = displacement.shape[2]
    fields = jnp.concatenate([displacement, jitter], axis=0)
    padded = jnp.pad(fields, ((0, 0), (1, 1), (1, 1), (0, 0)))
    inside = jnp.pad(jnp.ones((rows, columns), jnp.float32), 1)

    def one_row(index):
        window = lax.dynamic_slice_in_dim(padded, index, 3, axis=1)
        present = lax.dynamic_slice_in_dim(inside, index, 3, axis=0)
        masks = lax.dynamic_index_in_dim(bond_mask, index, axis=0, keepdims=False)
        center = window[:, 1, 1:1 + columns]
        totals = jnp.zeros((2, columns, TILE_X * TILE_Y), jnp.float32)
        for offset in range(9):
            shift_x = offset // 3 - 1
            shift_y = offset % 3 - 1
            nearby = window[:, 1 + shift_x, 1 + shift_y:1 + shift_y + columns]
            weight = present[1 + shift_x, 1 + shift_y:1 + shift_y + columns]
            totals = totals + pair_force(center, nearby, masks[:, offset], shift_x, shift_y) * weight[None, :, None]
        return totals
    forces = lax.map(one_row, jnp.arange(rows, dtype=jnp.int32))
    return jnp.transpose(forces, (1, 0, 2, 3))

def laplace(field):
    return field[2:, 1:-1] + field[:-2, 1:-1] + field[1:-1, 2:] + field[1:-1, :-2] - 4.0 * field[1:-1, 1:-1]

def reference(ice_displacement, ice_velocity, jitter, bond_mask, contact_node, intersection, shell_deflection, shell_velocity):
    flat_nodes = contact_node.reshape(-1)
    for iteration in range(STEPS):
        forces = ice_forces(ice_displacement, jitter, bond_mask)
        front_gap = ice_displacement[0, GX_T - 1] + intersection
        reached = shell_deflection.reshape(-1)[flat_nodes].reshape(front_gap.shape)
        pushes = PENALTY * jnp.maximum(front_gap - reached, 0.0)
        forces = forces.at[0, GX_T - 1].add(-pushes)
        loading = jax.ops.segment_sum(pushes.reshape(-1), flat_nodes, num_segments=SHELL_NODES).reshape(SH_H, SH_C)
        bending = laplace(laplace(jnp.pad(shell_deflection, 2)))
        ice_velocity = ice_velocity + STEP_DT * forces
        ice_displacement = ice_displacement + STEP_DT * ice_velocity
        shell_velocity = shell_velocity + STEP_DT * (loading - BEND * bending)
        shell_deflection = shell_deflection + STEP_DT * shell_velocity
    return (ice_displacement, ice_velocity, shell_deflection, shell_velocity)
```

```python
import functools

import jax
import jax.numpy as jnp
from jax import lax
from jax.experimental import pallas as pl
from jax.experimental.pallas import tpu as pltpu
from jax.sharding import PartitionSpec as P

MESH = pl.DeviceIdType.MESH

HORIZON = 3.5
DELTA_SQ = 0.25
PENALTY = 4.0
BEND = 0.5
STEP_DT = 0.2
FAR = 100.0

OFFSETS = [
    (u, v)
    for u in range(-3, 4)
    for v in range(-3, 4)
    if (u, v) != (0, 0) and max(abs(u) - 0.4, 0) ** 2 + max(abs(v) - 0.4, 0) ** 2 < HORIZON**2 - DELTA_SQ
]
SIDES = [(dx, dy) for dx in (-1, 0, 1) for dy in (-1, 0, 1) if (dx, dy) != (0, 0)]


def iota(axis):
    return lax.broadcasted_iota(jnp.int32, (8, 128), axis)


def pick(x, index, axis):
    return jnp.take_along_axis(x, index, axis=axis, mode="promise_in_bounds")


def swap_groups(x):
    sub, group = iota(0), iota(1) // 16
    x = pltpu.roll(x, 0, 1, stride=16, stride_axis=0)
    x = pick(x, (group - sub) & 7, 0)
    return pick(x, ((group + sub) & 7) * 16 + (iota(1) & 15), 1)


def turn(x, shift):
    shift = shift % 128
    return pltpu.roll(x, shift, 1) if shift else x


def kernel(
    n_x, n_y, width,
    d_hbm, v_hbm, j_hbm, bond_hbm, node_hbm, inter_hbm, s_hbm, w_hbm,
    d_out, v_out, s_out, w_out,
    d_in, v_in, j_in, bond, node, inter, shell_v,
    field1, field2, disp, vel, shift_j, shift_p, words, coef,
    shell1, shell2, h1, cen,
    pack_s1, pack_r1, pack_s2, pack_r2,
    gap_s, gap_r, reach_s, reach_r, push,
    in_sem, send_sem, recv_sem, row_send, row_recv, con_send, con_recv,
):
    gx, gy = lax.axis_index("gx"), lax.axis_index("gy")
    front = n_x - 1
    is_front = gx == front
    sub, lane = iota(0), iota(1)

    def peer(dx, dy):
        return (lax.rem(gx + dx + n_x, n_x), lax.rem(gy + dy + n_y, n_y))

    barrier = pltpu.get_barrier_semaphore()
    for dx, dy in SIDES:
        pl.semaphore_signal(barrier, inc=1, device_id=peer(dx, dy), device_id_type=MESH)

    @pl.when(is_front)
    def _():
        for i in range(1, n_x - 2):
            pl.semaphore_signal(barrier, inc=1, device_id=(i, gy), device_id_type=MESH)

    @pl.when((gx > 0) & (gx < n_x - 2))
    def _():
        pl.semaphore_signal(barrier, inc=1, device_id=(front, gy), device_id_type=MESH)

    loads = [
        pltpu.make_async_copy(src, dst, in_sem.at[k])
        for k, (src, dst) in enumerate(
            [
                (j_hbm, j_in), (d_hbm, d_in), (node_hbm, node), (inter_hbm, inter),
                (s_hbm, shell1.at[8:136, 128:640]), (bond_hbm, bond), (v_hbm, v_in), (w_hbm, shell_v),
            ]
        )
    ]
    for copy in loads:
        copy.start()

    loads[0].wait()
    loads[1].wait()
    for a in range(8):
        rows = pl.ds(8 + 8 * a, 8)
        for c in range(2):
            jit = swap_groups(j_in[c, a])
            dis = swap_groups(d_in[c, a])
            field1[c, rows, :] = jit
            field1[2 + c, rows, :] = jit + dis
            disp[c, pl.ds(8 * a, 8), :] = dis
    loads[2].wait()
    loads[3].wait()
    inter[...] = swap_groups(inter[...])
    node[...] = swap_groups(node[...])
    gap_s[0] = disp[0, 56:64, :] + inter[...]

    def pack_ice(field, count):
        left = right = jnp.zeros((8, 128), jnp.float32)
        for f in range(count):
            for b in range(8):
                g = 8 * f + b
                x = field[4 - count + f, pl.ds(8 + 8 * b, 8), :]
                here = lane // 4 == g
                left = jnp.where(here, turn(x, 4 * g), left)
                right = jnp.where(here, turn(x, 4 * g + 4), right)
        return left, right

    def pack_shell(field, start, left, right):
        for b in range(16):
            here = lane // 2 == start // 2 + b
            x = field[pl.ds(8 + 8 * b, 8), 128:256]
            left = jnp.where(here, turn(x, start + 2 * b), left)
            x = field[pl.ds(8 + 8 * b, 8), 512:640]
            right = jnp.where(here, turn(x, start + 2 * b + 2), right)
        return left, right

    zero = jnp.zeros((8, 128), jnp.float32)
    left, right = pack_ice(field1, 4)
    pack_s1[0, 0] = left
    pack_s1[1, 0] = right

    mine = jnp.broadcast_to(node[pl.ds(gx, 1), :], (8, 128))
    targets = []
    for k in range(4):
        n = pick(mine, 32 * k + lane // 4, 1)
        row = lax.shift_right_logical(n, width.bit_length() - 1) & 127
        targets.append(jnp.where((n & 3) == (lane & 3), row, -1))

    def touched(field):
        own = []
        points = zero
        for k in range(4):
            total = zero
            for b in range(16):
                x = field[pl.ds(8 + 8 * b, 8), 128 + 128 * k : 256 + 128 * k]
                total = total + jnp.where(sub + 8 * b == targets[k], x, 0.0)
            for s in (4, 2, 1):
                total = total + pltpu.roll(total, s, 0)
            own.append(total)
            total = total + turn(total, -1)
            total = total + turn(total, -2)
            points = jnp.where(lane // 32 == k, pick(total, (lane & 31) * 4, 1), points)
        return own, points

    loads[4].wait()
    own, points = touched(shell1)
    reach_s[0] = points
    left, right = pack_shell(shell1, 0, zero, zero)
    pack_s1[0, 1] = left
    pack_s1[1, 1] = right

    extra = jnp.where(is_front, n_x - 3, jnp.where((gx > 0) & (gx < n_x - 2), 1, 0))
    pl.semaphore_wait(barrier, 8 + extra)

    def row_copies(step, field, shell, base):
        copies = []
        for k, dx in enumerate((-1, 1)):
            src = 8 if dx < 0 else 64
            dst = 72 if dx < 0 else 0
            copies.append(
                pltpu.make_async_remote_copy(
                    field.at[base:4, src : src + 8, :], field.at[base:4, dst : dst + 8, :],
                    row_send.at[step, 0, k], row_recv.at[step, 0, k], device_id=peer(dx, 0), device_id_type=MESH,
                )
            )
        for k, dx in enumerate((-1, 1)):
            src = 8 if dx < 0 else 128
            dst = 136 if dx < 0 else 0
            copies.append(
                pltpu.make_async_remote_copy(
                    shell.at[src : src + 8, 128:640], shell.at[dst : dst + 8, 128:640],
                    row_send.at[step, 1, k], row_recv.at[step, 1, k], device_id=peer(dx, 0), device_id_type=MESH,
                )
            )
        return copies[:2], copies[2:]

    def pack_copies(step, part, send, recv):
        copies = []
        for dy in (-1, 1):
            for dx in (-1, 0, 1):
                side = 0 if dy < 0 else 1
                copies.append(
                    pltpu.make_async_remote_copy(
                        send.at[side, part], recv.at[1 - dx, 1 - side, part],
                        send_sem.at[step, part, side, dx + 1], recv_sem.at[step, part, side, dx + 1],
                        device_id=peer(dx, dy), device_id_type=MESH,
                    )
                )
        return copies

    def gap_copies(step, count=n_x - 1):
        return [
            pltpu.make_async_remote_copy(
                gap_s.at[step], gap_r.at[step], con_send.at[step, i], con_recv.at[step, 0],
                device_id=(i, gy), device_id_type=MESH,
            )
            for i in range(count)
        ]

    def reach_copy(step):
        return pltpu.make_async_remote_copy(
            reach_s.at[step], reach_r.at[step, gx], con_send.at[step, 0], con_recv.at[step, gx],
            device_id=(front, gy), device_id_type=MESH,
        )

    def reach_arrival(step, i):
        return pltpu.make_async_remote_copy(
            reach_s.at[step], reach_r.at[step, i], con_send.at[step, 0], con_recv.at[step, i],
            device_id=(front, gy), device_id_type=MESH,
        )

    def start_gap(step):
        @pl.when(is_front)
        def _():
            for copy in gap_copies(step):
                copy.start()
            gap_r[step] = gap_s[step]

    def start_reach(step):
        @pl.when(is_front)
        def _():
            reach_r[step, front] = reach_s[step]

        @pl.when(jnp.logical_not(is_front))
        def _():
            reach_copy(step).start()

    def end_contact(step):
        @pl.when(is_front)
        def _():
            reached = reach_r[step, front]
            for i in range(n_x - 1):
                reach_arrival(step, i).wait_recv()
                reached = jnp.where(sub == i, reach_r[step, i], reached)
            push[...] = PENALTY * jnp.maximum(gap_s[step] - reached, 0.0)

        @pl.when(jnp.logical_not(is_front))
        def _():
            gap_copies(step, 1)[0].wait_recv()
            push[...] = jnp.zeros((8, 128), jnp.float32)

    def drain_contact(step):
        @pl.when(is_front)
        def _():
            for copy in gap_copies(step):
                copy.wait_send()

        @pl.when(jnp.logical_not(is_front))
        def _():
            reach_copy(step).wait_send()

    ice_rows1, shell_rows1 = row_copies(0, field1, shell1, 0)
    ice_packs1 = pack_copies(0, 0, pack_s1, pack_r1)
    shell_packs1 = pack_copies(0, 1, pack_s1, pack_r1)
    for copy in ice_packs1 + ice_rows1:
        copy.start()
    start_gap(0)
    start_reach(0)
    for copy in shell_packs1 + shell_rows1:
        copy.start()

    loads[5].wait()
    for a in range(8):
        for s in range(9):
            word = jnp.broadcast_to(bond[a, :, s : s + 1], (8, 128))
            words[s, pl.ds(8 * a, 8), :] = pick(word, lane // 16, 0)
    loads[6].wait()
    for a in range(8):
        for c in range(2):
            vel[c, pl.ds(8 * a, 8), :] = swap_groups(v_in[c, a])

    def spread_field(field, index, recv, part, group0, out, missing):
        for b in range(10):
            slot = 0 if b == 0 else 2 if b == 9 else 1
            block = 7 if b == 0 else 0 if b == 9 else b - 1
            g = group0 + block
            lo = turn(recv[slot, 0, part], 124 - 4 * g)
            hi = turn(recv[slot, 1, part], -4 * g)
            if missing is not None:
                lo = jnp.where(gy > 0, lo, missing)
                hi = jnp.where(gy < n_y - 1, hi, missing)
            x = field[index, pl.ds(8 * b, 8), :]
            if missing is not None and b == 0:
                lo, hi, x = (jnp.where(gx > 0, z, missing) for z in (lo, hi, x))
            if missing is not None and b == 9:
                lo, hi, x = (jnp.where(gx < n_x - 1, z, missing) for z in (lo, hi, x))
            for v in range(-3, 4):
                y = x
                if v > 0:
                    y = jnp.where(lane < v, hi, x)
                if v < 0:
                    y = jnp.where(lane >= 128 + v, lo, x)
                out[v + 3, pl.ds(8 * b, 8), :] = turn(y, -v)

    def ice_step(step, field):
        last = step == 1

        def body(a, carry):
            base = pl.multiple_of(8 * a, 8)
            rows = pl.ds(base, 8)
            own = pl.ds(pl.multiple_of(base + 8, 8), 8)
            px, py = field[2, own, :], field[3, own, :]
            if not last:
                jx, jy = field[0, own, :], field[1, own, :]
            fx = fy = jnp.zeros((8, 128), jnp.float32)
            seen = None
            for n, (u, v) in enumerate(OFFSETS):
                there = pl.ds(base + (8 + u), 8)
                if not last:
                    if u != seen:
                        seen = u
                        shift = 4 * sub + (((sub + u) & 7) >> 1)
                        bits = []
                        for dy in range(3):
                            word = words[3 + dy, rows, :]
                            if u < 0:
                                word = jnp.where(sub + u < 0, words[dy, rows, :], word)
                            if u > 0:
                                word = jnp.where(sub + u > 7, words[6 + dy, rows, :], word)
                            bits.append((jnp.right_shift(word, shift) & 1).astype(jnp.float32))
                    intact = bits[1]
                    if v < 0:
                        intact = jnp.where((lane & 15) + v < 0, bits[0], intact)
                    if v > 0:
                        intact = jnp.where((lane & 15) + v > 15, bits[2], intact)
                    rx = (shift_j[0, v + 3, there, :] - jx) + float(u)
                    ry = (shift_j[1, v + 3, there, :] - jy) + float(v)
                    square = rx * rx + ry * ry + DELTA_SQ
                    inverse = lax.rsqrt(square)
                    reach = jnp.maximum(1.0 - square * inverse * (1.0 / HORIZON), 0.0)
                    near = intact * (reach * reach)
                    far = near * inverse
                    coef[n, 0, rows, :] = near
                    coef[n, 1, rows, :] = far
                else:
                    near = coef[n, 0, rows, :]
                    far = coef[n, 1, rows, :]
                nx = (shift_p[0, v + 3, there, :] - px) + float(u)
                ny = (shift_p[1, v + 3, there, :] - py) + float(v)
                factor = far - near * lax.rsqrt(nx * nx + ny * ny + DELTA_SQ)
                fx = fx + factor * nx
                fy = fy + factor * ny
            fx = fx - jnp.where(a == 7, push[...], 0.0)
            for c, force in enumerate((fx, fy)):
                speed = vel[c, rows, :] + STEP_DT * force
                moved = disp[c, rows, :] + STEP_DT * speed
                if last:
                    v_out[c, a] = swap_groups(speed)
                    d_out[c, a] = swap_groups(moved)
                else:
                    vel[c, rows, :] = speed
                    disp[c, rows, :] = moved
                    field2[2 + c, own, :] = field1[c, own, :] + moved
            return carry

        lax.fori_loop(0, 8, body, 0)

    def shell_edges(field, recv, part, start):
        @pl.when(gx == 0)
        def _():
            field[0:8, :] = jnp.zeros((8, 768), jnp.float32)

        @pl.when(gx == n_x - 1)
        def _():
            field[136:144, :] = jnp.zeros((8, 768), jnp.float32)

        for b in range(18):
            slot = 0 if b == 0 else 2 if b == 17 else 1
            block = 15 if b == 0 else 0 if b == 17 else b - 1
            g = start + 2 * block
            keep_lo, keep_hi = gy > 0, gy < n_y - 1
            if b == 0:
                keep_lo, keep_hi = keep_lo & (gx > 0), keep_hi & (gx > 0)
            if b == 17:
                keep_lo, keep_hi = keep_lo & (gx < n_x - 1), keep_hi & (gx < n_x - 1)
            lo = jnp.where(keep_lo, turn(recv[slot, 0, part], 126 - g), 0.0)
            hi = jnp.where(keep_hi, turn(recv[slot, 1, part], -g), 0.0)
            field[pl.ds(8 * b, 8), 0:128] = lo
            field[pl.ds(8 * b, 8), 640:768] = hi

    def shell_step(step, field, own):
        last = step == 1
        gaps = jnp.broadcast_to(gap_r[step, pl.ds(gx, 1), :], (8, 128))
        loads_of = []
        for k in range(4):
            gap = pick(gaps, 32 * k + lane // 4, 1)
            loads_of.append(PENALTY * jnp.maximum(gap - own[k], 0.0))
        load = jnp.concatenate(loads_of, axis=1)
        target = jnp.concatenate(targets, axis=1)
        row = lax.broadcasted_iota(jnp.int32, (8, 512), 0)
        for b in range(18):
            r = pl.ds(8 * b, 8)
            f = field[r, 128:640]
            pair = field[r, 127:639] + field[r, 129:641]
            h1[r, :] = pair
            cen[r, :] = 20.0 * f - 8.0 * pair + (field[r, 126:638] + field[r, 130:642])
        for b in range(16):
            i = 8 + 8 * b
            r = pl.ds(8 * b, 8)
            far = field[i - 2 : i + 6, 128:640] + field[i + 2 : i + 10, 128:640]
            near = field[i - 1 : i + 7, 128:640] + field[i + 1 : i + 9, 128:640]
            diagonal = h1[i - 1 : i + 7, :] + h1[i + 1 : i + 9, :]
            bending = (cen[i : i + 8, :] + far) - 8.0 * near + 2.0 * diagonal
            loading = jnp.where(row + 8 * b == target, load, 0.0)
            speed = shell_v[r, :] + STEP_DT * (loading - BEND * bending)
            moved = field[i : i + 8, 128:640] + STEP_DT * speed
            if last:
                w_out[r, :] = speed
                s_out[r, :] = moved
            else:
                shell_v[r, :] = speed
                shell2[i : i + 8, 128:640] = moved

    for copy in ice_packs1 + ice_rows1:
        copy.wait_recv()
    for c in range(2):
        spread_field(field1, c, pack_r1, 0, 8 * c, shift_j.at[c], FAR)
        spread_field(field1, 2 + c, pack_r1, 0, 16 + 8 * c, shift_p.at[c], None)
    end_contact(0)
    ice_step(0, field1)
    gap_s[1] = disp[0, 56:64, :] + inter[...]
    left, right = pack_ice(field2, 2)
    pack_s2[0, 0] = left
    pack_s2[1, 0] = right
    ice_rows2, shell_rows2 = row_copies(1, field2, shell2, 2)
    ice_packs2 = pack_copies(1, 0, pack_s2, pack_r2)
    shell_packs2 = pack_copies(1, 1, pack_s2, pack_r2)
    for copy in ice_packs2 + ice_rows2:
        copy.start()
    start_gap(1)

    loads[7].wait()
    for copy in shell_packs1 + shell_rows1:
        copy.wait_recv()
    shell_edges(shell1, pack_r1, 1, 0)
    shell_step(0, shell1, own)
    own, points = touched(shell2)
    reach_s[1] = points
    start_reach(1)
    left, right = pack_shell(shell2, 0, zero, zero)
    pack_s2[0, 1] = left
    pack_s2[1, 1] = right
    for copy in shell_packs2 + shell_rows2:
        copy.start()

    for copy in ice_packs2 + ice_rows2:
        copy.wait_recv()
    for c in range(2):
        spread_field(field2, 2 + c, pack_r2, 0, 8 * c, shift_p.at[c], None)
    end_contact(1)
    ice_step(1, field2)
    for copy in shell_packs2 + shell_rows2:
        copy.wait_recv()
    shell_edges(shell2, pack_r2, 1, 0)
    shell_step(1, shell2, own)

    for copy in ice_packs1 + ice_rows1 + shell_packs1 + shell_rows1:
        copy.wait_send()
    for copy in ice_packs2 + ice_rows2 + shell_packs2 + shell_rows2:
        copy.wait_send()
    for step in range(2):
        drain_contact(step)


def on_device(n_x, n_y, width, d, v, j, bond, node, inter, shell, speed):
    f32, i32 = jnp.float32, jnp.int32
    vmem = pltpu.VMEM
    dma = pltpu.SemaphoreType.DMA
    return pl.pallas_call(
        functools.partial(kernel, n_x, n_y, width),
        out_shape=[jax.ShapeDtypeStruct(x.shape, f32) for x in (d, v, shell, speed)],
        in_specs=[pl.BlockSpec(memory_space=pl.ANY)] * 8,
        out_specs=[pl.BlockSpec(memory_space=vmem)] * 4,
        scratch_shapes=[
            vmem(d.shape, f32), vmem(v.shape, f32), vmem(j.shape, f32), vmem(bond.shape, i32),
            vmem(node.shape, i32), vmem(inter.shape, f32), vmem(speed.shape, f32),
            vmem((4, 80, 128), f32), vmem((4, 80, 128), f32), vmem((2, 64, 128), f32), vmem((2, 64, 128), f32),
            vmem((2, 7, 80, 128), f32), vmem((2, 7, 80, 128), f32), vmem((9, 64, 128), i32),
            vmem((len(OFFSETS), 2, 64, 128), f32),
            vmem((144, 768), f32), vmem((144, 768), f32), vmem((144, 512), f32), vmem((144, 512), f32),
            vmem((2, 2, 8, 128), f32), vmem((3, 2, 2, 8, 128), f32),
            vmem((2, 2, 8, 128), f32), vmem((3, 2, 2, 8, 128), f32),
            vmem((2, 8, 128), f32), vmem((2, 8, 128), f32), vmem((2, 8, 128), f32), vmem((2, n_x, 8, 128), f32),
            vmem((8, 128), f32),
            dma((8,)), dma((2, 2, 2, 3)), dma((2, 2, 2, 3)), dma((2, 2, 2)), dma((2, 2, 2)),
            dma((2, n_x)), dma((2, n_x)),
        ],
        compiler_params=pltpu.CompilerParams(collective_id=0, has_side_effects=True),
    )(d, v, j, bond, node, inter, shell, speed)


def solution(mesh):
    n_x, n_y = mesh.shape["gx"], mesh.shape["gy"]
    ice, plate = P(None, "gx", "gy", None), P("gx", "gy")

    def step(*args):
        return on_device(n_x, n_y, args[6].shape[1] * n_y, *args)

    return jax.shard_map(
        step,
        mesh=mesh,
        in_specs=(ice, ice, ice, P("gx", "gy", None), P("gy", None), P("gy", None), plate, plate),
        out_specs=(ice, ice, plate, plate),
        check_vma=False,
    )
```

```python
import functools

import jax
import jax.numpy as jnp
from jax import lax
from jax.experimental import pallas as pl
from jax.experimental.pallas import tpu as pltpu
from jax.sharding import PartitionSpec as P

MESH = pl.DeviceIdType.MESH

HORIZON = 3.5
DELTA_SQ = 0.25
PENALTY = 4.0
BEND = 0.5
STEP_DT = 0.2
FAR = 100.0

OFFSETS = [
    (u, v)
    for u in range(-3, 4)
    for v in range(-3, 4)
    if (u, v) != (0, 0) and max(abs(u) - 0.4, 0) ** 2 + max(abs(v) - 0.4, 0) ** 2 < HORIZON**2 - DELTA_SQ
]
ROW_OFFSETS = [(u, v) for u, v in OFFSETS if u > 0]
SIDES = [(dx, dy) for dx in (-1, 0, 1) for dy in (-1, 0, 1) if (dx, dy) != (0, 0)]


def iota(axis):
    return lax.broadcasted_iota(jnp.int32, (8, 128), axis)


def pick(x, index, axis):
    return jnp.take_along_axis(x, index, axis=axis, mode="promise_in_bounds")


def swap_groups(x):
    sub, group = iota(0), iota(1) // 16
    x = pltpu.roll(x, 0, 1, stride=16, stride_axis=0)
    x = pick(x, (group - sub) & 7, 0)
    return pick(x, ((group + sub) & 7) * 16 + (iota(1) & 15), 1)


def turn(x, shift):
    shift = shift % 128
    return pltpu.roll(x, shift, 1) if shift else x


def slide(x, shift):
    return pltpu.roll(x, shift % 8, 0)


def bonds(intact, square):
    inverse = lax.rsqrt(square)
    reach = jnp.maximum(1.0 - square * inverse * (1.0 / HORIZON), 0.0)
    near = intact * (reach * reach)
    return near, near * inverse


def bits_of(word, shift):
    return (jnp.right_shift(word, shift) & 1).astype(jnp.float32)


def kernel(
    n_x, n_y, width,
    d_hbm, v_hbm, j_hbm, bond_hbm, node_hbm, inter_hbm, s_hbm, w_hbm,
    d_out, v_out, s_out, shell_v,
    d_in, v_in, j_in, bond, node, inter,
    field1, field2, disp, vel, force, shift_j, shift_p, words, coef, row_coef, col_coef,
    shell1, shell2, h1, cen, square,
    edge_s1, edge_r1, edge_s2, edge_r2, rows_r1, rows_r2,
    rim_s, rim_r, slab_r, gap_s, gap_r, reach_s, reach_r, push,
    in_sem, send_sem, ice_sem, shell_sem, con_send, con_recv,
):
    f32 = jnp.float32
    gx, gy = lax.axis_index("gx"), lax.axis_index("gy")
    front = n_x - 1
    is_front = gx == front
    has_up, has_down, has_left, has_right = gx > 0, gx < n_x - 1, gy > 0, gy < n_y - 1
    sub, lane = iota(0), iota(1)
    zero = jnp.zeros((8, 128), f32)

    def peer(dx, dy):
        return (lax.rem(gx + dx + n_x, n_x), lax.rem(gy + dy + n_y, n_y))

    barrier = pltpu.get_barrier_semaphore()
    for dx, dy in SIDES:
        pl.semaphore_signal(barrier, inc=1, device_id=peer(dx, dy), device_id_type=MESH)

    @pl.when(is_front)
    def _():
        for i in range(1, n_x - 2):
            pl.semaphore_signal(barrier, inc=1, device_id=(i, gy), device_id_type=MESH)

    @pl.when((gx > 0) & (gx < n_x - 2))
    def _():
        pl.semaphore_signal(barrier, inc=1, device_id=(front, gy), device_id_type=MESH)

    loads = [
        pltpu.make_async_copy(src, dst, in_sem.at[k])
        for k, (src, dst) in enumerate(
            [
                (j_hbm, j_in), (d_hbm, d_in), (node_hbm, node), (inter_hbm, inter),
                (s_hbm, shell1.at[8:136, 128:640]), (bond_hbm, bond), (v_hbm, v_in), (w_hbm, shell_v),
            ]
        )
    ]
    for copy in loads:
        copy.start()

    for c in range(2):
        for v in range(7):
            for r in (0, 72):
                shift_j[c, v, r : r + 8, :] = zero + FAR
                shift_p[c, v, r : r + 8, :] = zero
    for field in (shell1, shell2):
        for r in (0, 136):
            field[r : r + 8, :] = jnp.zeros((8, 768), f32)
        for b in range(16):
            for c in (0, 640):
                field[8 + 8 * b : 16 + 8 * b, c : c + 128] = zero
    for b in range(1, 15):
        square[8 * b : 8 * b + 8, :] = zero

    loads[0].wait()
    loads[1].wait()
    for a in range(8):
        rows = pl.ds(8 + 8 * a, 8)
        for c in range(2):
            jit = swap_groups(j_in[c, a])
            dis = swap_groups(d_in[c, a])
            field1[c, rows, :] = jit
            field1[2 + c, rows, :] = jit + dis
            disp[c, pl.ds(8 * a, 8), :] = dis

    def edges(field, base):
        stack = jnp.concatenate([field[base, 8:72, :], field[base + 1, 8:72, :]], axis=0)
        across = jnp.transpose(stack)
        return across[0:8, :], across[120:128, :]

    for part, base in enumerate((0, 2)):
        left, right = edges(field1, base)
        edge_s1[0, part] = left
        edge_s1[1, part] = right
    loads[2].wait()
    loads[3].wait()
    inter[...] = swap_groups(inter[...])
    node[...] = swap_groups(node[...])
    gap_s[0] = disp[0, 56:64, :] + inter[...]

    mine = jnp.broadcast_to(node[pl.ds(gx, 1), :], (8, 128))
    targets = []
    for k in range(4):
        n = pick(mine, 32 * k + lane // 4, 1)
        row = lax.shift_right_logical(n, width.bit_length() - 1) & 127
        targets.append(jnp.where((n & 3) == (lane & 3), row, -1))

    def gather_points(totals):
        own = []
        points = zero
        for k, total in enumerate(totals):
            for s in (4, 2, 1):
                total = total + slide(total, s)
            own.append(total)
            total = total + turn(total, -1)
            total = total + turn(total, -2)
            points = jnp.where(lane // 32 == k, pick(total, (lane & 31) * 4, 1), points)
        return own, points

    def pack_rim(field):
        left = right = zero
        for b in range(16):
            here = lane // 2 == b
            left = jnp.where(here, turn(field[8 + 8 * b : 16 + 8 * b, 128:256], 2 * b), left)
            right = jnp.where(here, turn(field[8 + 8 * b : 16 + 8 * b, 512:640], 2 * b + 2), right)
        return left, right

    loads[4].wait()
    totals = []
    for k in range(4):
        total = zero
        for b in range(16):
            x = shell1[8 + 8 * b : 16 + 8 * b, 128 + 128 * k : 256 + 128 * k]
            total = total + jnp.where(sub + 8 * b == targets[k], x, 0.0)
        totals.append(total)
    own, points = gather_points(totals)
    reach_s[0] = points
    left, right = pack_rim(shell1)
    rim_s[0, 0] = left
    rim_s[0, 1] = right

    extra = jnp.where(is_front, n_x - 3, jnp.where((gx > 0) & (gx < n_x - 2), 1, 0))
    pl.semaphore_wait(barrier, 8 + extra)

    def send(src, dst, recv_sem, where):
        pltpu.make_async_remote_copy(
            src, dst, send_sem.at[0], recv_sem, device_id=where, device_id_type=MESH
        ).start()

    def span(kib):
        return coef.at[0 : kib // 8, 0, 0:16, :]

    def arrived(kib, recv_sem):
        pltpu.make_async_remote_copy(
            span(kib), span(kib), send_sem.at[0], recv_sem, device_id=peer(0, 1), device_id_type=MESH
        ).wait_recv()

    def send_ice(step, field, base, edge_s, edge_r, rows_r):
        for dy in (-1, 1):
            side = 0 if dy < 0 else 1
            for dx in (-1, 0, 1):
                send(edge_s.at[side], edge_r.at[1 - dx, 1 - side], ice_sem.at[step], peer(dx, dy))
        for k, dx in enumerate((-1, 1)):
            src = 8 if dx < 0 else 64
            send(field.at[base:4, src : src + 8, :], rows_r.at[1 - k], ice_sem.at[step], peer(dx, 0))

    def send_shell(step, field):
        for dy in (-1, 1):
            side = 0 if dy < 0 else 1
            for dx in (-1, 0, 1):
                send(rim_s.at[step, side], rim_r.at[step, 1 - dx, 1 - side], shell_sem.at[step], peer(dx, dy))
        for k, dx in enumerate((-1, 1)):
            src = 8 if dx < 0 else 128
            send(field.at[src : src + 8, 128:640], slab_r.at[step, 1 - k], shell_sem.at[step], peer(dx, 0))

    def gap_copy(step, i):
        return pltpu.make_async_remote_copy(
            gap_s.at[step], gap_r.at[step], con_send.at[0], con_recv.at[step],
            device_id=(i, gy), device_id_type=MESH,
        )

    def reach_copy(step):
        return pltpu.make_async_remote_copy(
            reach_s.at[step], reach_r.at[step, gx], con_send.at[0], con_recv.at[step],
            device_id=(front, gy), device_id_type=MESH,
        )

    def start_gap(step):
        @pl.when(is_front)
        def _():
            for i in range(n_x - 1):
                gap_copy(step, i).start()
            gap_r[step] = gap_s[step]

    def start_reach(step):
        @pl.when(is_front)
        def _():
            reach_r[step, front] = reach_s[step]

        @pl.when(jnp.logical_not(is_front))
        def _():
            reach_copy(step).start()

    def end_contact(step):
        @pl.when(is_front)
        def _():
            slots = reach_r.at[step, 0 : n_x - 1]
            pltpu.make_async_remote_copy(
                slots, slots, con_send.at[0], con_recv.at[step], device_id=(0, gy), device_id_type=MESH
            ).wait_recv()
            reached = reach_r[step, front]
            for i in range(n_x - 1):
                reached = jnp.where(sub == i, reach_r[step, i], reached)
            push[...] = PENALTY * jnp.maximum(gap_s[step] - reached, 0.0)

        @pl.when(jnp.logical_not(is_front))
        def _():
            gap_copy(step, 0).wait_recv()
            push[...] = jnp.zeros((8, 128), f32)

    send_ice(0, field1, 0, edge_s1, edge_r1, rows_r1)
    start_gap(0)
    start_reach(0)
    send_shell(0, shell1)

    loads[5].wait()
    for a in range(8):
        for s in range(9):
            word = jnp.broadcast_to(bond[a, :, s : s + 1], (8, 128))
            words[s, pl.ds(8 * a, 8), :] = pick(word, lane // 16, 0)
    col_words = []
    for side in range(2):
        for dx in range(3):
            total = jnp.zeros((8, 128), jnp.int32)
            for a in range(8):
                s = 3 * dx + 2 * side
                word = jnp.broadcast_to(bond[a, 7 * side : 7 * side + 1, s : s + 1], (8, 128))
                total = jnp.where((lane & 63) // 8 == a, word, total)
            col_words.append(total)
    loads[6].wait()
    for a in range(8):
        for c in range(2):
            vel[c, pl.ds(8 * a, 8), :] = swap_groups(v_in[c, a])

    def spread_field(field, index, out, missing):
        for b in range(1, 9):
            x = field[index, pl.ds(8 * b, 8), :]
            for v in range(-3, 4):
                y = x
                if missing is not None and v > 0:
                    y = jnp.where(lane < v, missing, x)
                if missing is not None and v < 0:
                    y = jnp.where(lane >= 128 + v, missing, x)
                out[v + 3, pl.ds(8 * b, 8), :] = turn(y, -v)

    def ice_inside(step, field):
        last = step == 1

        def body(a, carry):
            base = pl.multiple_of(8 * a, 8)
            rows = pl.ds(base, 8)
            own = pl.ds(pl.multiple_of(base + 8, 8), 8)
            px, py = field[2, own, :], field[3, own, :]
            if not last:
                jx, jy = field[0, own, :], field[1, own, :]
            fx = fy = zero
            seen = None
            for n, (u, v) in enumerate(OFFSETS):
                there = pl.ds(base + (8 + u), 8)
                if not last:
                    if u != seen:
                        seen = u
                        shift = 4 * sub + (((sub + u) & 7) >> 1)
                        bits = []
                        for dy in range(3):
                            word = words[3 + dy, rows, :]
                            if u < 0:
                                word = jnp.where(sub + u < 0, words[dy, rows, :], word)
                            if u > 0:
                                word = jnp.where(sub + u > 7, words[6 + dy, rows, :], word)
                            bits.append(bits_of(word, shift))
                    intact = bits[1]
                    if v < 0:
                        intact = jnp.where((lane & 15) + v < 0, bits[0], intact)
                    if v > 0:
                        intact = jnp.where((lane & 15) + v > 15, bits[2], intact)
                    rx = (shift_j[0, v + 3, there, :] - jx) + float(u)
                    ry = (shift_j[1, v + 3, there, :] - jy) + float(v)
                    near, far = bonds(intact, rx * rx + ry * ry + DELTA_SQ)
                    coef[n, 0, rows, :] = near
                    coef[n, 1, rows, :] = far
                else:
                    near = coef[n, 0, rows, :]
                    far = coef[n, 1, rows, :]
                nx = (shift_p[0, v + 3, there, :] - px) + float(u)
                ny = (shift_p[1, v + 3, there, :] - py) + float(v)
                factor = far - near * lax.rsqrt(nx * nx + ny * ny + DELTA_SQ)
                fx = fx + factor * nx
                fy = fy + factor * ny
            force[0, rows, :] = fx
            force[1, rows, :] = fy
            return carry

        lax.fori_loop(0, 8, body, 0)

    top = sub < 4

    def ice_rows(step, field, rows_r):
        last = step == 1
        base = 2 if last else 0
        mine = [jnp.where(top, field[c, 8:16, :], field[c, 64:72, :]) for c in range(base, 4)]
        fx = fy = zero
        if not last:
            word = [jnp.where(top, words[dy, 0:8, :], words[6 + dy, 56:64, :]) for dy in range(3)]
        seen = None
        for n, (u, v) in enumerate(ROW_OFFSETS):
            if u != seen:
                seen = u
                beyond = [
                    jnp.where(top, slide(rows_r[0, c], u), slide(rows_r[1, c], -u)) for c in range(4 - base)
                ]
                along = jnp.where(top, -float(u), float(u))
                if not last:
                    inside = ((sub < u) & has_up) | ((sub >= 8 - u) & has_down)
                    shift = 4 * sub + (((sub + jnp.where(top, -u, u)) & 7) >> 1)
                    bits = [jnp.where(inside, bits_of(w, shift), 0.0) for w in word]
            if not last:
                intact = bits[1]
                if v < 0:
                    intact = jnp.where((lane & 15) + v < 0, bits[0], intact)
                    intact = jnp.where(lane + v < 0, 0.0, intact)
                if v > 0:
                    intact = jnp.where((lane & 15) + v > 15, bits[2], intact)
                    intact = jnp.where(lane + v > 127, 0.0, intact)
                rx = (turn(beyond[0], -v) - mine[0]) + along
                ry = (turn(beyond[1], -v) - mine[1]) + float(v)
                near, far = bonds(intact, rx * rx + ry * ry + DELTA_SQ)
                row_coef[n, 0] = near
                row_coef[n, 1] = far
            else:
                near, far = row_coef[n, 0], row_coef[n, 1]
            nx = (turn(beyond[2 - base], -v) - mine[2 - base]) + along
            ny = (turn(beyond[3 - base], -v) - mine[3 - base]) + float(v)
            factor = far - near * lax.rsqrt(nx * nx + ny * ny + DELTA_SQ)
            fx = fx + factor * nx
            fy = fy + factor * ny
        return fx, fy

    near_col = jnp.where(sub < 3, 0, jnp.where(sub < 5, 1, 2))
    far_col = jnp.where(sub < 3, sub + 1, jnp.where(sub < 5, sub - 2, 1))
    point_row = lane & 63

    def ice_columns(step, edge_s, edge_r):
        last = step == 1
        parts = (0,) if last else (0, 1)
        whole = []
        for side in range(2):
            sign = 1.0 if side else -1.0
            mine_at = 7 - near_col if side else near_col
            beyond_at = far_col - 1 if side else 8 - far_col
            mine = [pick(edge_s[side, p], mine_at, 0) for p in parts]
            beyond = [[pick(edge_r[slot, side, p], beyond_at, 0) for slot in range(3)] for p in parts]
            across = (near_col + far_col).astype(f32) * sign
            total = zero
            for u in range(-3, 4):
                def moved(p):
                    if u == 0:
                        return beyond[p][1]
                    inside = point_row + u >= 0 if u < 0 else point_row + u <= 63
                    return jnp.where(inside, turn(beyond[p][1], -u), turn(beyond[p][0 if u < 0 else 2], 64 - u))

                offset = jnp.where(lane < 64, float(u), across)
                if not last:
                    word = col_words[3 * side + 1]
                    if u < 0:
                        word = jnp.where((lane & 7) + u < 0, col_words[3 * side], word)
                    if u > 0:
                        word = jnp.where((lane & 7) + u > 7, col_words[3 * side + 2], word)
                    intact = bits_of(word, 4 * (lane & 7) + ((((lane & 7) + u) & 7) >> 1))
                    there = (sub < 6) & (has_right if side else has_left)
                    if u < 0:
                        there = there & ((point_row + u >= 0) | has_up)
                    if u > 0:
                        there = there & ((point_row + u <= 63) | has_down)
                    intact = jnp.where(there, intact, 0.0)
                    rest = (moved(0) - mine[0]) + offset
                    square_of = rest * rest
                    near, far = bonds(intact, square_of + turn(square_of, 64) + DELTA_SQ)
                    col_coef[side, u + 3, 0] = near
                    col_coef[side, u + 3, 1] = far
                else:
                    near, far = col_coef[side, u + 3, 0], col_coef[side, u + 3, 1]
                now = (moved(len(parts) - 1) - mine[-1]) + offset
                square_of = now * now
                factor = far - near * lax.rsqrt(square_of + turn(square_of, 64) + DELTA_SQ)
                total = total + factor * now
            at = 7 - sub if side else sub
            whole.append(
                jnp.where(at < 3, pick(total, jnp.where(at == 0, 0, jnp.where(at == 1, 3, 5)), 0), 0.0)
                + jnp.where(at < 2, pick(total, jnp.where(at == 0, 1, 4), 0), 0.0)
                + jnp.where(at == 0, pick(total, jnp.full((8, 128), 2, jnp.int32), 0), 0.0)
            )
        square[0:8, :] = whole[0]
        square[120:128, :] = whole[1]
        return jnp.transpose(square[...])

    def ice_finish(step, rows_force, columns_force):
        last = step == 1
        for a in range(8):
            rows = pl.ds(8 * a, 8)
            for c in range(2):
                total = force[c, rows, :] + columns_force[64 * c + 8 * a : 64 * c + 8 * a + 8, :]
                if a == 0:
                    total = total + jnp.where(top, rows_force[c], 0.0)
                if a == 7:
                    total = total + jnp.where(top, 0.0, rows_force[c])
                    if c == 0:
                        total = total - push[...]
                speed = vel[c, rows, :] + STEP_DT * total
                moved = disp[c, rows, :] + STEP_DT * speed
                if last:
                    v_out[c, a] = swap_groups(speed)
                    d_out[c, a] = swap_groups(moved)
                else:
                    vel[c, rows, :] = speed
                    disp[c, rows, :] = moved
                    field2[2 + c, 8 + 8 * a : 16 + 8 * a, :] = field1[c, 8 + 8 * a : 16 + 8 * a, :] + moved

    def shell_inside(field, put):
        for b in range(18):
            r = pl.ds(8 * b, 8)
            f = field[r, 128:640]
            pair = field[r, 127:639] + field[r, 129:641]
            h1[r, :] = pair
            cen[r, :] = 20.0 * f - 8.0 * pair + (field[r, 126:638] + field[r, 130:642])
        for b in range(16):
            i = 8 + 8 * b
            r = pl.ds(8 * b, 8)
            far = field[i - 2 : i + 6, 128:640] + field[i + 2 : i + 10, 128:640]
            near = field[i - 1 : i + 7, 128:640] + field[i + 1 : i + 9, 128:640]
            diagonal = h1[i - 1 : i + 7, :] + h1[i + 1 : i + 9, :]
            bending = (cen[i : i + 8, :] + far) - 8.0 * near + 2.0 * diagonal
            speed = shell_v[r, :] - (STEP_DT * BEND) * bending
            shell_v[r, :] = speed
            put(b, field[i : i + 8, 128:640] + STEP_DT * speed)

    def rim_terms(step, side):
        above, level, below = (rim_r[step, slot, side] for slot in range(3))
        level = jnp.where(lane < 2, jnp.where(has_up, turn(above, -30), 0.0), turn(level, 2))
        rim = jnp.where(lane >= 34, jnp.where(has_down, turn(below, 34), 0.0), level)
        rim = jnp.where(has_right if side else has_left, rim, 0.0)
        first = turn(rim, 1 if side else -1)
        up, down = slide(first, 1), slide(first, -1)
        up = jnp.where(sub == 0, turn(up, 2), up)
        down = jnp.where(sub == 7, turn(down, -2), down)
        full = rim - 8.0 * first + 2.0 * (up + down)
        return jnp.where((lane & 1) == side, full, rim)

    def slab_terms(step):
        sub_w = lax.broadcasted_iota(jnp.int32, (8, 512), 0)
        lane_w = lax.broadcasted_iota(jnp.int32, (8, 512), 1)
        terms = []
        for k in range(2):
            slab = jnp.where(has_down if k else has_up, slab_r[step, k], 0.0)
            sign = -1 if k else 1
            outer = pltpu.roll(slab, (2 * sign) % 8, 0)
            inner = pltpu.roll(slab, sign % 8, 0)
            pair = jnp.where(lane_w == 0, 0.0, pltpu.roll(inner, 1, 1)) + jnp.where(
                lane_w == 511, 0.0, pltpu.roll(inner, 511, 1)
            )
            at = 7 - sub_w if k else sub_w
            terms.append(
                jnp.where(at < 2, outer, 0.0) + jnp.where(at == 0, 2.0 * pair - 8.0 * inner, 0.0)
            )
        return terms

    def shell_finish(step, own, put, get):
        gaps = jnp.broadcast_to(gap_r[step, pl.ds(gx, 1), :], (8, 128))
        slabs = slab_terms(step)
        rims = [rim_terms(step, side) for side in range(2)]
        totals = []
        for k in range(4):
            gap = pick(gaps, 32 * k + lane // 4, 1)
            load = (STEP_DT * PENALTY) * jnp.maximum(gap - own[k], 0.0)
            total = zero
            for b in range(16):
                here = sub + 8 * b == targets[k]
                change = jnp.where(here, load, 0.0)
                beyond = None
                if b == 0:
                    beyond = slabs[0][:, 128 * k : 128 * k + 128]
                if b == 15:
                    beyond = slabs[1][:, 128 * k : 128 * k + 128]
                if k == 0 or k == 3:
                    rim = turn(rims[k // 3], (124 if k else -2) - 2 * b)
                    rim = jnp.where(lane >= 126 if k else lane < 2, rim, 0.0)
                    beyond = rim if beyond is None else beyond + rim
                if beyond is not None:
                    change = change - (STEP_DT * BEND) * beyond
                at = (pl.ds(8 * b, 8), slice(128 * k, 128 * k + 128))
                shell_v[at] = shell_v[at] + change
                moved = get(b, k) + STEP_DT * change
                put(b, k, moved)
                total = total + jnp.where(here, moved, 0.0)
            totals.append(total)
        return totals

    def put_rows(b, moved):
        shell2[8 + 8 * b : 16 + 8 * b, 128:640] = moved

    def put_block(b, k, moved):
        shell2[8 + 8 * b : 16 + 8 * b, 128 + 128 * k : 256 + 128 * k] = moved

    def get_block(b, k):
        return shell2[8 + 8 * b : 16 + 8 * b, 128 + 128 * k : 256 + 128 * k]

    def out_rows(b, moved):
        s_out[pl.ds(8 * b, 8), :] = moved

    def out_block(b, k, moved):
        s_out[pl.ds(8 * b, 8), 128 * k : 128 * k + 128] = moved

    def out_get(b, k):
        return s_out[pl.ds(8 * b, 8), 128 * k : 128 * k + 128]

    for c in range(2):
        spread_field(field1, c, shift_j.at[c], FAR)
        spread_field(field1, 2 + c, shift_p.at[c], None)
    ice_inside(0, field1)
    loads[7].wait()
    shell_inside(shell1, put_rows)

    arrived(80, ice_sem.at[0])
    columns_force = ice_columns(0, edge_s1, edge_r1)
    rows_force = ice_rows(0, field1, rows_r1)
    end_contact(0)
    ice_finish(0, rows_force, columns_force)
    gap_s[1] = disp[0, 56:64, :] + inter[...]
    left, right = edges(field2, 2)
    edge_s2[0, 0] = left
    edge_s2[1, 0] = right
    send_ice(1, field2, 2, edge_s2, edge_r2, rows_r2)
    start_gap(1)

    arrived(56, shell_sem.at[0])
    totals = shell_finish(0, own, put_block, get_block)
    own, points = gather_points(totals)
    reach_s[1] = points
    start_reach(1)
    left, right = pack_rim(shell2)
    rim_s[1, 0] = left
    rim_s[1, 1] = right
    send_shell(1, shell2)

    for c in range(2):
        spread_field(field2, 2 + c, shift_p.at[c], None)
    ice_inside(1, field2)
    shell_inside(shell2, out_rows)

    arrived(40, ice_sem.at[1])
    columns_force = ice_columns(1, edge_s2, edge_r2)
    rows_force = ice_rows(1, field2, rows_r2)
    end_contact(1)
    ice_finish(1, rows_force, columns_force)
    arrived(56, shell_sem.at[1])
    shell_finish(1, own, out_block, out_get)

    pltpu.make_async_remote_copy(
        span(232), span(232), send_sem.at[0], ice_sem.at[0], device_id=peer(0, 1), device_id_type=MESH
    ).wait_send()

    @pl.when(is_front)
    def _():
        slots = reach_r.at[:, 0 : n_x - 1]
        pltpu.make_async_remote_copy(
            slots, slots, con_send.at[0], con_recv.at[0], device_id=(0, gy), device_id_type=MESH
        ).wait_send()

    @pl.when(jnp.logical_not(is_front))
    def _():
        pltpu.make_async_remote_copy(
            gap_r, gap_r, con_send.at[0], con_recv.at[0], device_id=(front, gy), device_id_type=MESH
        ).wait_send()


def write_out(*refs):
    copies = [pltpu.make_async_copy(refs[k], refs[4 + k], refs[8].at[k]) for k in range(4)]
    for copy in copies:
        copy.start()
    for copy in copies:
        copy.wait()


def on_device(n_x, n_y, width, d, v, j, bond, node, inter, shell, speed):
    f32, i32 = jnp.float32, jnp.int32
    vmem = pltpu.VMEM
    dma = pltpu.SemaphoreType.DMA
    shapes = [x.shape for x in (d, v, shell, speed)]
    held = pl.pallas_call(
        functools.partial(kernel, n_x, n_y, width),
        out_shape=[vmem(s, f32) for s in shapes],
        in_specs=[pl.BlockSpec(memory_space=pl.ANY)] * 8,
        out_specs=[pl.BlockSpec(memory_space=vmem)] * 4,
        scratch_shapes=[
            vmem(d.shape, f32), vmem(v.shape, f32), vmem(j.shape, f32), vmem(bond.shape, i32),
            vmem(node.shape, i32), vmem(inter.shape, f32),
            vmem((4, 80, 128), f32), vmem((4, 80, 128), f32), vmem((2, 64, 128), f32), vmem((2, 64, 128), f32),
            vmem((2, 64, 128), f32),
            vmem((2, 7, 80, 128), f32), vmem((2, 7, 80, 128), f32), vmem((9, 64, 128), i32),
            vmem((len(OFFSETS), 2, 64, 128), f32), vmem((len(ROW_OFFSETS), 2, 8, 128), f32),
            vmem((2, 7, 2, 8, 128), f32),
            vmem((144, 768), f32), vmem((144, 768), f32), vmem((144, 512), f32), vmem((144, 512), f32),
            vmem((128, 128), f32),
            vmem((2, 2, 8, 128), f32), vmem((3, 2, 2, 8, 128), f32),
            vmem((2, 1, 8, 128), f32), vmem((3, 2, 1, 8, 128), f32),
            vmem((2, 4, 8, 128), f32), vmem((2, 2, 8, 128), f32),
            vmem((2, 2, 8, 128), f32), vmem((2, 3, 2, 8, 128), f32), vmem((2, 2, 8, 512), f32),
            vmem((2, 8, 128), f32), vmem((2, 8, 128), f32), vmem((2, 8, 128), f32), vmem((2, n_x, 8, 128), f32),
            vmem((8, 128), f32),
            dma((8,)), dma((1,)), dma((2,)), dma((2,)), dma((1,)), dma((2,)),
        ],
        compiler_params=pltpu.CompilerParams(collective_id=0, has_side_effects=True),
    )(d, v, j, bond, node, inter, shell, speed)
    return pl.pallas_call(
        write_out,
        out_shape=[jax.ShapeDtypeStruct(s, f32) for s in shapes],
        in_specs=[pl.BlockSpec(memory_space=vmem)] * 4,
        out_specs=[pl.BlockSpec(memory_space=pl.ANY)] * 4,
        scratch_shapes=[dma((4,))],
    )(*[pltpu.with_memory_space_constraint(x, vmem) for x in held])


def solution(mesh):
    n_x, n_y = mesh.shape["gx"], mesh.shape["gy"]
    ice, plate = P(None, "gx", "gy", None), P("gx", "gy")

    def step(*args):
        return on_device(n_x, n_y, args[6].shape[1] * n_y, *args)

    return jax.shard_map(
        step,
        mesh=mesh,
        in_specs=(ice, ice, ice, P("gx", "gy", None), P("gy", None), P("gy", None), plate, plate),
        out_specs=(ice, ice, plate, plate),
        check_vma=False,
    )
```

```python
import functools

import jax
import jax.numpy as jnp
from jax import lax
from jax.experimental import pallas as pl
from jax.experimental.pallas import tpu as pltpu
from jax.sharding import PartitionSpec as P

MESH = pl.DeviceIdType.MESH

HORIZON = 3.5
DELTA_SQ = 0.25
PENALTY = 4.0
BEND = 0.5
STEP_DT = 0.2
RUN = 32

OFFSETS = [
    (u, v)
    for u in range(-3, 4)
    for v in range(-3, 4)
    if (u, v) != (0, 0) and max(abs(u) - 0.4, 0) ** 2 + max(abs(v) - 0.4, 0) ** 2 < HORIZON**2 - DELTA_SQ
]
ROW_OFFSETS = [(u, v) for u, v in OFFSETS if u > 0]
SIDES = [(dx, dy) for dx in (-1, 0, 1) for dy in (-1, 0, 1) if (dx, dy) != (0, 0)]


def iota(axis):
    return lax.broadcasted_iota(jnp.int32, (8, 128), axis)


def pick(x, index, axis):
    return jnp.take_along_axis(x, index, axis=axis, mode="promise_in_bounds")


def swap_groups(x):
    sub, group = iota(0), iota(1) // 16
    x = pltpu.roll(x, 0, 1, stride=16, stride_axis=0)
    x = pick(x, (group - sub) & 7, 0)
    return pick(x, ((group + sub) & 7) * 16 + (iota(1) & 15), 1)


def turn(x, shift):
    shift = shift % 128
    return pltpu.roll(x, shift, 1) if shift else x


def slide(x, shift):
    return pltpu.roll(x, shift % 8, 0)


def bonds(intact, square):
    inverse = lax.rsqrt(square)
    reach = jnp.maximum(HORIZON - square * inverse, 0.0)
    near = intact * (reach * reach)
    return near, near * inverse


def intact_of(word, bit):
    return jnp.where((word & bit) != 0, 1.0 / HORIZON**2, 0.0)


def bit_at(row, beyond):
    return jnp.left_shift(1, 4 * (row & 7) + ((beyond & 7) >> 1))


def kernel(
    n_x, n_y, width,
    d_hbm, v_hbm, j_hbm, bond_hbm, node_hbm, inter_hbm, s_hbm, w_hbm,
    d_out, v_out, s_out, shell_v,
    d_in, v_in, j_in, bond, node, inter,
    field1, field2, disp, vel, force, shift_j, shift_p, words, coef, row_coef, col_coef,
    row_words, shell1, shell2, bend1, square,
    edge_s1, edge_r1, edge_s2, edge_r2, rows_r1, rows_r2,
    rim_s, rim_r, slab_r, gap_s, gap_r, reach_s, reach_r, push,
    in_sem, send_sem, ice_sem, shell_sem, con_send, con_recv,
):
    f32 = jnp.float32
    gx, gy = lax.axis_index("gx"), lax.axis_index("gy")
    front = n_x - 1
    is_front = gx == front
    has_up, has_down, has_left, has_right = gx > 0, gx < n_x - 1, gy > 0, gy < n_y - 1
    sub, lane = iota(0), iota(1)
    zero = jnp.zeros((8, 128), f32)

    def peer(dx, dy):
        return (lax.rem(gx + dx + n_x, n_x), lax.rem(gy + dy + n_y, n_y))

    def load(src, dst, k):
        return pltpu.make_async_copy(src, dst, in_sem.at[k])

    def span(kib):
        return coef.at[0 : kib // 8, 0, 0:16, :]

    first = [load(j_hbm, j_in, 0), load(d_hbm, d_in, 1), load(node_hbm, node, 2), load(inter_hbm, inter, 3)]
    plate = [load(s_hbm.at[:, 128 * k : 128 * k + 128], shell1.at[k, 8:136, :], 4) for k in range(4)]
    later = [load(bond_hbm, bond, 5), load(v_hbm, v_in, 6), load(w_hbm, shell_v, 7)]
    for copy in first + plate + later:
        copy.start()

    barrier = pltpu.get_barrier_semaphore()
    for dx, dy in SIDES:
        pl.semaphore_signal(barrier, inc=1, device_id=peer(dx, dy), device_id_type=MESH)

    @pl.when(is_front)
    def _():
        for i in range(1, n_x - 2):
            pl.semaphore_signal(barrier, inc=1, device_id=(i, gy), device_id_type=MESH)

    @pl.when((gx > 0) & (gx < n_x - 2))
    def _():
        pl.semaphore_signal(barrier, inc=1, device_id=(front, gy), device_id_type=MESH)

    for r in (0, 72):
        for c in range(2):
            for v in range(7):
                shift_j[c, v, r : r + 8, :] = zero
                shift_p[c, v, r : r + 8, :] = zero
        for c in range(4):
            field1[c, r : r + 8, :] = zero
            field2[c, r : r + 8, :] = zero
    for field in (shell1, shell2):
        for r in (0, 136):
            for k in range(4):
                field[k, r : r + 8, :] = zero
    for b in range(1, 15):
        square[8 * b : 8 * b + 8, :] = zero

    first[0].wait()
    first[1].wait()
    for a in range(8):
        rows = pl.ds(8 + 8 * a, 8)
        for c in range(2):
            jit = swap_groups(j_in[c, a])
            dis = swap_groups(d_in[c, a])
            field1[c, rows, :] = jit
            field1[2 + c, rows, :] = jit + dis
            disp[c, pl.ds(8 * a, 8), :] = dis

    def edges(field, base):
        stack = jnp.concatenate([field[base, 8:72, :], field[base + 1, 8:72, :]], axis=0)
        across = jnp.transpose(stack)
        return across[0:8, :], across[120:128, :]

    for part, base in enumerate((0, 2)):
        left, right = edges(field1, base)
        edge_s1[0, part] = left
        edge_s1[1, part] = right
    first[2].wait()
    first[3].wait()
    inter[...] = swap_groups(inter[...])
    node[...] = swap_groups(node[...])
    gap_s[0] = disp[0, 56:64, :] + inter[...]

    mine = jnp.broadcast_to(node[pl.ds(gx, 1), :], (8, 128))
    targets = []
    for k in range(4):
        n = pick(mine, 32 * k + lane // 4, 1)
        row = lax.shift_right_logical(n, width.bit_length() - 1) & 127
        targets.append(jnp.where((n & 3) == (lane & 3), row, -1))

    def gather_points(totals):
        own = []
        points = zero
        for k, total in enumerate(totals):
            for s in (4, 2, 1):
                total = total + slide(total, s)
            own.append(total)
            total = total + turn(total, -1)
            total = total + turn(total, -2)
            points = jnp.where(lane // 32 == k, pick(total, (lane & 31) * 4, 1), points)
        return own, points

    def pack_rim(field):
        left = right = zero
        for b in range(16):
            here = lane // 2 == b
            left = jnp.where(here, turn(field[0, 8 + 8 * b : 16 + 8 * b, :], 2 * b), left)
            right = jnp.where(here, turn(field[3, 8 + 8 * b : 16 + 8 * b, :], 2 * b + 2), right)
        return left, right

    load(span(256), span(256), 4).wait()
    totals = []
    for k in range(4):
        total = zero
        for b in range(16):
            x = shell1[k, 8 + 8 * b : 16 + 8 * b, :]
            total = total + jnp.where(sub + 8 * b == targets[k], x, 0.0)
        totals.append(total)
    own, points = gather_points(totals)
    reach_s[0] = points
    left, right = pack_rim(shell1)
    edge_s1[0, 2] = left
    edge_s1[1, 2] = right

    extra = jnp.where(is_front, n_x - 3, jnp.where((gx > 0) & (gx < n_x - 2), 1, 0))
    pl.semaphore_wait(barrier, 8 + extra)

    def send(src, dst, recv_sem, where):
        pltpu.make_async_remote_copy(
            src, dst, send_sem.at[0], recv_sem, device_id=where, device_id_type=MESH
        ).start()

    def arrived(kib, recv_sem):
        pltpu.make_async_remote_copy(
            span(kib), span(kib), send_sem.at[0], recv_sem, device_id=peer(0, 1), device_id_type=MESH
        ).wait_recv()

    def send_ice(step, field, base, edge_s, edge_r, rows_r):
        for dy in (-1, 1):
            side = 0 if dy < 0 else 1
            for dx in (-1, 0, 1):
                send(edge_s.at[side], edge_r.at[1 - dx, 1 - side], ice_sem.at[step], peer(dx, dy))
        for k, dx in enumerate((-1, 1)):
            src = 8 if dx < 0 else 64
            send(field.at[base:4, src : src + 8, :], rows_r.at[1 - k], ice_sem.at[step], peer(dx, 0))

    def send_rims():
        for dy in (-1, 1):
            side = 0 if dy < 0 else 1
            for dx in (-1, 0, 1):
                send(rim_s.at[side], rim_r.at[1 - dx, 1 - side], shell_sem.at[1], peer(dx, dy))

    def send_slabs(step, field):
        for k, dx in enumerate((-1, 1)):
            src = 8 if dx < 0 else 128
            send(field.at[:, src : src + 8, :], slab_r.at[step, 1 - k], shell_sem.at[step], peer(dx, 0))

    def gap_copy(step, i):
        return pltpu.make_async_remote_copy(
            gap_s.at[step], gap_r.at[step], con_send.at[0], con_recv.at[step],
            device_id=(i, gy), device_id_type=MESH,
        )

    def reach_copy(step):
        return pltpu.make_async_remote_copy(
            reach_s.at[step], reach_r.at[step, gx], con_send.at[0], con_recv.at[step],
            device_id=(front, gy), device_id_type=MESH,
        )

    def start_gap(step):
        @pl.when(is_front)
        def _():
            for i in range(n_x - 1):
                gap_copy(step, i).start()
            gap_r[step] = gap_s[step]

    def start_reach(step):
        @pl.when(is_front)
        def _():
            reach_r[step, front] = reach_s[step]

        @pl.when(jnp.logical_not(is_front))
        def _():
            reach_copy(step).start()

    def end_contact(step):
        @pl.when(is_front)
        def _():
            slots = reach_r.at[step, 0 : n_x - 1]
            pltpu.make_async_remote_copy(
                slots, slots, con_send.at[0], con_recv.at[step], device_id=(0, gy), device_id_type=MESH
            ).wait_recv()
            reached = reach_r[step, front]
            for i in range(n_x - 1):
                reached = jnp.where(sub == i, reach_r[step, i], reached)
            push[...] = PENALTY * jnp.maximum(gap_s[step] - reached, 0.0)

        @pl.when(jnp.logical_not(is_front))
        def _():
            gap_copy(step, 0).wait_recv()
            push[...] = jnp.zeros((8, 128), f32)

    send_ice(0, field1, 0, edge_s1, edge_r1, rows_r1)
    start_gap(0)
    start_reach(0)
    send_slabs(0, shell1)

    later[0].wait()
    none = jnp.zeros((8, 128), jnp.int32)
    for s in range(9):
        for a in range(8):
            word = pick(jnp.broadcast_to(bond[8 * a : 8 * a + 8, s : s + 1], (8, 128)), lane // 16, 0)
            if s % 3 == 0:
                word = jnp.where(lane < 16, 0, word)
            if s % 3 == 2:
                word = jnp.where(lane >= 112, 0, word)
            if a == 0 and s < 3:
                row_words[0, s] = word
                word = none
            if a == 7 and s > 5:
                row_words[1, s - 6] = word
                word = none
            words[s, 8 * a : 8 * a + 8, :] = word
    col_words = []
    for side in range(2):
        tiles = bond[pl.ds(7 * side, 8, stride=8), :]
        for dx in range(3):
            s = 3 * dx + 2 * side
            word = jnp.broadcast_to(tiles[:, s : s + 1], (8, 128))
            col_words.append(pick(word, (lane & 63) // 8, 0))
    later[1].wait()
    for a in range(8):
        for c in range(2):
            vel[c, pl.ds(8 * a, 8), :] = swap_groups(v_in[c, a])

    def spread_field(field, index, out):
        for b in range(1, 9):
            x = field[index, 8 * b : 8 * b + 8, :]
            for v in range(-3, 4):
                if v:
                    out[v + 3, 8 * b : 8 * b + 8, :] = turn(x, -v)

    def ice_inside(step, field):
        last = step == 1
        sub_r = lax.broadcasted_iota(jnp.int32, (RUN, 128), 0)
        lane_r = lax.broadcasted_iota(jnp.int32, (RUN, 128), 1)
        tile_row, tile_col = sub_r & 7, lane_r & 15

        def body(a, carry):
            base = pl.multiple_of(RUN * a, RUN)
            rows = pl.ds(base, RUN)
            own = pl.ds(pl.multiple_of(base + 8, 8), RUN)

            def partner(shifted, c, u, v):
                there = pl.ds(base + (8 + u), RUN)
                if v == 0:
                    return field[(0 if shifted is shift_j else 2) + c, there, :]
                return shifted[c, v + 3, there, :]

            px = field[2, own, :]
            py = [field[3, own, :] - float(v) for v in range(-3, 4)]
            if not last:
                jx = field[0, own, :]
                jy = [field[1, own, :] - float(v) for v in range(-3, 4)]
            fx = fy = jnp.zeros((RUN, 128), f32)
            seen = None
            for n, (u, v) in enumerate(OFFSETS):
                if u != seen:
                    seen = u
                    px_u = px - float(u)
                    if not last:
                        jx_u = jx - float(u)
                        bit = bit_at(tile_row, tile_row + u)
                        flags = []
                        for dy in range(3):
                            word = words[3 + dy, rows, :]
                            if u < 0:
                                word = jnp.where(tile_row + u < 0, words[dy, rows, :], word)
                            if u > 0:
                                word = jnp.where(tile_row + u > 7, words[6 + dy, rows, :], word)
                            flags.append(intact_of(word, bit))
                if not last:
                    intact = flags[1]
                    if v < 0:
                        intact = jnp.where(tile_col + v < 0, flags[0], intact)
                    if v > 0:
                        intact = jnp.where(tile_col + v > 15, flags[2], intact)
                    rx = partner(shift_j, 0, u, v) - jx_u
                    ry = partner(shift_j, 1, u, v) - jy[v + 3]
                    near, far = bonds(intact, rx * rx + ry * ry + DELTA_SQ)
                    coef[n, 0, rows, :] = near
                    coef[n, 1, rows, :] = far
                else:
                    near = coef[n, 0, rows, :]
                    far = coef[n, 1, rows, :]
                nx = partner(shift_p, 0, u, v) - px_u
                ny = partner(shift_p, 1, u, v) - py[v + 3]
                factor = far - near * lax.rsqrt(nx * nx + ny * ny + DELTA_SQ)
                fx = fx + factor * nx
                fy = fy + factor * ny
            force[0, rows, :] = fx
            force[1, rows, :] = fy
            return carry

        lax.fori_loop(0, 64 // RUN, body, 0)

    top = sub < 4

    def ice_rows(step, field, rows_r):
        last = step == 1
        base = 2 if last else 0
        mine = [jnp.where(top, field[c, 8:16, :], field[c, 64:72, :]) for c in range(base, 4)]
        mine_y = [[mine[c] - float(v) for v in range(-3, 4)] for c in range(1, 4 - base, 2)]
        fx = fy = zero
        if not last:
            word = [jnp.where(top, row_words[0, dy], row_words[1, dy]) for dy in range(3)]
        seen = None
        for n, (u, v) in enumerate(ROW_OFFSETS):
            if u != seen:
                seen = u
                beyond = [
                    jnp.where(top, slide(rows_r[0, c], u), slide(rows_r[1, c], -u)) for c in range(4 - base)
                ]
                along = jnp.where(top, -float(u), float(u))
                mine_x = [mine[c] - along for c in range(0, 4 - base, 2)]
                if not last:
                    inside = ((sub < u) & has_up) | ((sub >= 8 - u) & has_down)
                    bit = bit_at(sub, sub + jnp.where(top, -u, u))
                    flags = [jnp.where(inside, intact_of(w, bit), 0.0) for w in word]
            if not last:
                intact = flags[1]
                if v < 0:
                    intact = jnp.where((lane & 15) + v < 0, flags[0], intact)
                if v > 0:
                    intact = jnp.where((lane & 15) + v > 15, flags[2], intact)
                rx = turn(beyond[0], -v) - mine_x[0]
                ry = turn(beyond[1], -v) - mine_y[0][v + 3]
                near, far = bonds(intact, rx * rx + ry * ry + DELTA_SQ)
                row_coef[n, 0] = near
                row_coef[n, 1] = far
            else:
                near, far = row_coef[n, 0], row_coef[n, 1]
            nx = turn(beyond[2 - base], -v) - mine_x[-1]
            ny = turn(beyond[3 - base], -v) - mine_y[-1][v + 3]
            factor = far - near * lax.rsqrt(nx * nx + ny * ny + DELTA_SQ)
            fx = fx + factor * nx
            fy = fy + factor * ny
        return fx, fy

    near_col = jnp.where(sub < 3, 0, jnp.where(sub < 5, 1, 2))
    far_col = jnp.where(sub < 3, sub + 1, jnp.where(sub < 5, sub - 2, 1))
    point_row = lane & 63

    def ice_columns(step, edge_s, edge_r):
        last = step == 1
        parts = (0,) if last else (0, 1)
        whole = []
        for side in range(2):
            sign = 1.0 if side else -1.0
            mine_at = 7 - near_col if side else near_col
            beyond_at = far_col - 1 if side else 8 - far_col
            mine = [pick(edge_s[side, p], mine_at, 0) for p in parts]
            beyond = [[pick(edge_r[slot, side, p], beyond_at, 0) for slot in range(3)] for p in parts]
            across = (near_col + far_col).astype(f32) * sign
            total = zero
            for u in range(-3, 4):
                def moved(p):
                    if u == 0:
                        return beyond[p][1]
                    inside = point_row + u >= 0 if u < 0 else point_row + u <= 63
                    return jnp.where(inside, turn(beyond[p][1], -u), turn(beyond[p][0 if u < 0 else 2], 64 - u))

                offset = jnp.where(lane < 64, float(u), across)
                if not last:
                    word = col_words[3 * side + 1]
                    if u < 0:
                        word = jnp.where((lane & 7) + u < 0, col_words[3 * side], word)
                    if u > 0:
                        word = jnp.where((lane & 7) + u > 7, col_words[3 * side + 2], word)
                    intact = intact_of(word, bit_at(lane, lane + u))
                    there = (sub < 6) & (has_right if side else has_left)
                    if u < 0:
                        there = there & ((point_row + u >= 0) | has_up)
                    if u > 0:
                        there = there & ((point_row + u <= 63) | has_down)
                    intact = jnp.where(there, intact, 0.0)
                    rest = (moved(0) - mine[0]) + offset
                    square_of = rest * rest
                    near, far = bonds(intact, square_of + turn(square_of, 64) + DELTA_SQ)
                    col_coef[side, u + 3, 0] = near
                    col_coef[side, u + 3, 1] = far
                else:
                    near, far = col_coef[side, u + 3, 0], col_coef[side, u + 3, 1]
                now = (moved(len(parts) - 1) - mine[-1]) + offset
                square_of = now * now
                factor = far - near * lax.rsqrt(square_of + turn(square_of, 64) + DELTA_SQ)
                total = total + factor * now
            at = 7 - sub if side else sub
            whole.append(
                jnp.where(at < 3, pick(total, jnp.where(at == 0, 0, jnp.where(at == 1, 3, 5)), 0), 0.0)
                + jnp.where(at < 2, pick(total, jnp.where(at == 0, 1, 4), 0), 0.0)
                + jnp.where(at == 0, pick(total, jnp.full((8, 128), 2, jnp.int32), 0), 0.0)
            )
        square[0:8, :] = whole[0]
        square[120:128, :] = whole[1]
        return jnp.transpose(square[...])

    def ice_finish(step, rows_force, columns_force):
        last = step == 1
        for a in range(8):
            rows = pl.ds(8 * a, 8)
            for c in range(2):
                total = force[c, rows, :] + columns_force[64 * c + 8 * a : 64 * c + 8 * a + 8, :]
                if a == 0:
                    total = total + jnp.where(top, rows_force[c], 0.0)
                if a == 7:
                    total = total + jnp.where(top, 0.0, rows_force[c])
                    if c == 0:
                        total = total - push[...]
                speed = vel[c, rows, :] + STEP_DT * total
                moved = disp[c, rows, :] + STEP_DT * speed
                if last:
                    v_out[c, a] = swap_groups(speed)
                    d_out[c, a] = swap_groups(moved)
                else:
                    vel[c, rows, :] = speed
                    disp[c, rows, :] = moved
                    field2[2 + c, 8 + 8 * a : 16 + 8 * a, :] = field1[c, 8 + 8 * a : 16 + 8 * a, :] + moved

    def sideways(x, first, last):
        up = [turn(c, 1) for c in x]
        down = [turn(c, -1) for c in x]
        return [
            jnp.where(lane == 0, up[k - 1] if k else first, up[k])
            + jnp.where(lane == 127, down[k + 1] if k < 3 else last, down[k])
            for k in range(4)
        ]

    def shell_inside(field, put):
        def chunks(ref, start):
            return [ref[k, pl.ds(start, 8), :] for k in range(4)]

        def once(b, carry):
            for h in range(4):
                i = pl.multiple_of(32 * b + 8 * h + 8, 8)
                f, up, down = chunks(field, i), chunks(field, i - 1), chunks(field, i + 1)
                for k, side in enumerate(sideways(f, 0.0, 0.0)):
                    bend1[k, pl.ds(i, 8), :] = (up[k] + down[k]) + side - 4.0 * f[k]
            return carry

        def twice(b, carry):
            for h in range(4):
                base = pl.multiple_of(32 * b + 8 * h, 8)
                i = pl.multiple_of(base + 8, 8)
                f, g = chunks(field, i), chunks(bend1, i)
                up, down = chunks(bend1, i - 1), chunks(bend1, i + 1)
                for k, side in enumerate(sideways(g, f[0], f[3])):
                    at = (pl.ds(base, 8), slice(128 * k, 128 * k + 128))
                    bending = (up[k] + down[k]) + side - 4.0 * g[k]
                    speed = shell_v[at] - (STEP_DT * BEND) * bending
                    shell_v[at] = speed
                    put(base, k, f[k] + STEP_DT * speed)
            return carry

        lax.fori_loop(0, 4, once, 0)
        for k in range(4):
            bend1[k, 7:8, :] = field[k, 8:9, :]
            bend1[k, 136:137, :] = field[k, 135:136, :]
        lax.fori_loop(0, 4, twice, 0)

    def rim_terms(step, side):
        above, level, below = (edge_r1[t, side, 2] if step == 0 else rim_r[t, side] for t in range(3))
        level = jnp.where(lane < 2, jnp.where(has_up, turn(above, -30), 0.0), turn(level, 2))
        rim = jnp.where(lane >= 34, jnp.where(has_down, turn(below, 34), 0.0), level)
        rim = jnp.where(has_right if side else has_left, rim, 0.0)
        first = turn(rim, 1 if side else -1)
        up, down = slide(first, 1), slide(first, -1)
        up = jnp.where(sub == 0, turn(up, 2), up)
        down = jnp.where(sub == 7, turn(down, -2), down)
        full = rim - 8.0 * first + 2.0 * (up + down)
        return jnp.where((lane & 1) == side, full, rim)

    def slab_terms(step):
        terms = []
        for k in range(2):
            slab = [jnp.where(has_down if k else has_up, slab_r[step, k, c], 0.0) for c in range(4)]
            sign = -1 if k else 1
            outer = [slide(x, 2 * sign) for x in slab]
            inner = [slide(x, sign) for x in slab]
            at = 7 - sub if k else sub
            terms.append(
                [
                    jnp.where(at < 2, o, 0.0) + jnp.where(at == 0, 2.0 * pair - 8.0 * x, 0.0)
                    for o, x, pair in zip(outer, inner, sideways(inner, 0.0, 0.0))
                ]
            )
        return terms

    def shell_finish(step, own, put, get):
        gaps = jnp.broadcast_to(gap_r[step, pl.ds(gx, 1), :], (8, 128))
        slabs = slab_terms(step)
        rims = [rim_terms(step, side) for side in range(2)]
        totals = []
        for k in range(4):
            gap = pick(gaps, 32 * k + lane // 4, 1)
            load = (STEP_DT * PENALTY) * jnp.maximum(gap - own[k], 0.0)
            total = zero
            for b in range(16):
                here = sub + 8 * b == targets[k]
                change = jnp.where(here, load, 0.0)
                beyond = None
                if b == 0:
                    beyond = slabs[0][k]
                if b == 15:
                    beyond = slabs[1][k]
                if k == 0 or k == 3:
                    rim = turn(rims[k // 3], (124 if k else -2) - 2 * b)
                    rim = jnp.where(lane >= 126 if k else lane < 2, rim, 0.0)
                    beyond = rim if beyond is None else beyond + rim
                if beyond is not None:
                    change = change - (STEP_DT * BEND) * beyond
                at = (pl.ds(8 * b, 8), slice(128 * k, 128 * k + 128))
                shell_v[at] = shell_v[at] + change
                moved = get(8 * b, k) + STEP_DT * change
                put(8 * b, k, moved)
                total = total + jnp.where(here, moved, 0.0)
            totals.append(total)
        return totals

    def put_block(base, k, moved):
        shell2[k, pl.ds(base + 8, 8), :] = moved

    def get_block(base, k):
        return shell2[k, pl.ds(base + 8, 8), :]

    def out_block(base, k, moved):
        s_out[pl.ds(base, 8), 128 * k : 128 * k + 128] = moved

    def out_get(base, k):
        return s_out[pl.ds(base, 8), 128 * k : 128 * k + 128]

    for c in range(2):
        spread_field(field1, c, shift_j.at[c])
        spread_field(field1, 2 + c, shift_p.at[c])
    ice_inside(0, field1)
    later[2].wait()
    shell_inside(shell1, put_block)

    arrived(104, ice_sem.at[0])
    columns_force = ice_columns(0, edge_s1, edge_r1)
    rows_force = ice_rows(0, field1, rows_r1)
    end_contact(0)
    ice_finish(0, rows_force, columns_force)
    gap_s[1] = disp[0, 56:64, :] + inter[...]
    left, right = edges(field2, 2)
    edge_s2[0, 0] = left
    edge_s2[1, 0] = right
    send_ice(1, field2, 2, edge_s2, edge_r2, rows_r2)
    start_gap(1)

    arrived(32, shell_sem.at[0])
    totals = shell_finish(0, own, put_block, get_block)
    own, points = gather_points(totals)
    reach_s[1] = points
    start_reach(1)
    left, right = pack_rim(shell2)
    rim_s[0] = left
    rim_s[1] = right
    send_rims()
    send_slabs(1, shell2)

    for c in range(2):
        spread_field(field2, 2 + c, shift_p.at[c])
    ice_inside(1, field2)
    shell_inside(shell2, out_block)

    arrived(40, ice_sem.at[1])
    columns_force = ice_columns(1, edge_s2, edge_r2)
    rows_force = ice_rows(1, field2, rows_r2)
    end_contact(1)
    ice_finish(1, rows_force, columns_force)
    arrived(56, shell_sem.at[1])
    shell_finish(1, own, out_block, out_get)

    pltpu.make_async_remote_copy(
        span(232), span(232), send_sem.at[0], ice_sem.at[0], device_id=peer(0, 1), device_id_type=MESH
    ).wait_send()

    @pl.when(is_front)
    def _():
        slots = reach_r.at[:, 0 : n_x - 1]
        pltpu.make_async_remote_copy(
            slots, slots, con_send.at[0], con_recv.at[0], device_id=(0, gy), device_id_type=MESH
        ).wait_send()

    @pl.when(jnp.logical_not(is_front))
    def _():
        pltpu.make_async_remote_copy(
            gap_r, gap_r, con_send.at[0], con_recv.at[0], device_id=(front, gy), device_id_type=MESH
        ).wait_send()


def write_out(*refs):
    copies = [pltpu.make_async_copy(refs[k], refs[4 + k], refs[8].at[k]) for k in range(4)]
    for copy in copies:
        copy.start()
    for copy in copies:
        copy.wait()


def on_device(n_x, n_y, width, d, v, j, bond, node, inter, shell, speed):
    f32, i32 = jnp.float32, jnp.int32
    vmem = pltpu.VMEM
    dma = pltpu.SemaphoreType.DMA
    shapes = [x.shape for x in (d, v, shell, speed)]
    held = pl.pallas_call(
        functools.partial(kernel, n_x, n_y, width),
        out_shape=[vmem(s, f32) for s in shapes],
        in_specs=[pl.BlockSpec(memory_space=pl.ANY)] * 8,
        out_specs=[pl.BlockSpec(memory_space=vmem)] * 4,
        scratch_shapes=[
            vmem(d.shape, f32), vmem(v.shape, f32), vmem(j.shape, f32), vmem(bond.shape, i32),
            vmem(node.shape, i32), vmem(inter.shape, f32),
            vmem((4, 80, 128), f32), vmem((4, 80, 128), f32), vmem((2, 64, 128), f32), vmem((2, 64, 128), f32),
            vmem((2, 64, 128), f32),
            vmem((2, 7, 80, 128), f32), vmem((2, 7, 80, 128), f32), vmem((9, 64, 128), i32),
            vmem((len(OFFSETS), 2, 64, 128), f32), vmem((len(ROW_OFFSETS), 2, 8, 128), f32),
            vmem((2, 7, 2, 8, 128), f32),
            vmem((2, 3, 8, 128), i32), vmem((4, 144, 128), f32), vmem((4, 144, 128), f32), vmem((4, 144, 128), f32),
            vmem((128, 128), f32),
            vmem((2, 3, 8, 128), f32), vmem((3, 2, 3, 8, 128), f32),
            vmem((2, 1, 8, 128), f32), vmem((3, 2, 1, 8, 128), f32),
            vmem((2, 4, 8, 128), f32), vmem((2, 2, 8, 128), f32),
            vmem((2, 8, 128), f32), vmem((3, 2, 8, 128), f32), vmem((2, 2, 4, 8, 128), f32),
            vmem((2, 8, 128), f32), vmem((2, 8, 128), f32), vmem((2, 8, 128), f32), vmem((2, n_x, 8, 128), f32),
            vmem((8, 128), f32),
            dma((8,)), dma((1,)), dma((2,)), dma((2,)), dma((1,)), dma((2,)),
        ],
        compiler_params=pltpu.CompilerParams(collective_id=0, has_side_effects=True),
    )(d, v, j, bond, node, inter, shell, speed)
    return pl.pallas_call(
        write_out,
        out_shape=[jax.ShapeDtypeStruct(s, f32) for s in shapes],
        in_specs=[pl.BlockSpec(memory_space=vmem)] * 4,
        out_specs=[pl.BlockSpec(memory_space=pl.ANY)] * 4,
        scratch_shapes=[dma((4,))],
    )(*[pltpu.with_memory_space_constraint(x, vmem) for x in held])


def solution(mesh):
    n_x, n_y = mesh.shape["gx"], mesh.shape["gy"]
    ice, plate = P(None, "gx", "gy", None), P("gx", "gy")

    def step(d, v, j, bond, *rest):
        width = rest[2].shape[1] * n_y
        return on_device(n_x, n_y, width, d, v, j, bond.reshape(-1, bond.shape[2]), *rest)

    return jax.shard_map(
        step,
        mesh=mesh,
        in_specs=(ice, ice, ice, P("gx", "gy", None), P("gy", None), P("gy", None), plate, plate),
        out_specs=(ice, ice, plate, plate),
        check_vma=False,
    )
```

```python
import functools

import jax
import jax.numpy as jnp
from jax import lax
from jax.experimental import pallas as pl
from jax.experimental.pallas import tpu as pltpu
from jax.sharding import PartitionSpec as P

MESH = pl.DeviceIdType.MESH

HORIZON = 3.5
DELTA_SQ = 0.25
PENALTY = 4.0
BEND = 0.5
STEP_DT = 0.2
RUN = 32

OFFSETS = [
    (u, v)
    for u in range(-3, 4)
    for v in range(-3, 4)
    if (u, v) != (0, 0) and max(abs(u) - 0.4, 0) ** 2 + max(abs(v) - 0.4, 0) ** 2 < HORIZON**2 - DELTA_SQ
]
ROW_OFFSETS = [(u, v) for u, v in OFFSETS if u > 0]
SIDES = [(dx, dy) for dx in (-1, 0, 1) for dy in (-1, 0, 1) if (dx, dy) != (0, 0)]


def iota(axis):
    return lax.broadcasted_iota(jnp.int32, (8, 128), axis)


def pick(x, index, axis):
    return jnp.take_along_axis(x, index, axis=axis, mode="promise_in_bounds")


def swap_groups(x):
    sub, group = iota(0), iota(1) // 16
    x = pltpu.roll(x, 0, 1, stride=16, stride_axis=0)
    x = pick(x, (group - sub) & 7, 0)
    return pick(x, ((group + sub) & 7) * 16 + (iota(1) & 15), 1)


def turn(x, shift):
    shift = shift % 128
    return pltpu.roll(x, shift, 1) if shift else x


def slide(x, shift):
    return pltpu.roll(x, shift % 8, 0)


def bonds(intact, square):
    inverse = lax.rsqrt(square)
    reach = jnp.maximum(HORIZON - square * inverse, 0.0)
    near = intact * (reach * reach)
    return near, near * inverse


def intact_of(word, bit):
    return jnp.where((word & bit) != 0, 1.0 / HORIZON**2, 0.0)


def bit_at(row, beyond):
    return jnp.left_shift(1, 4 * (row & 7) + ((beyond & 7) >> 1))


def kernel(
    n_x, n_y, width,
    d_hbm, v_hbm, j_hbm, bond_hbm, node_hbm, inter_hbm, s_hbm, w_hbm,
    d_out, v_out, s_out, shell_v,
    d_in, v_in, j_in, bond, node, inter,
    field1, field2, disp, vel, force, shift_j, shift_p, words, coef, row_coef, col_coef,
    row_words, shell1, shell2, bend1, square,
    edge_s1, edge_r1, edge_s2, edge_r2, rows_s1, rows_r1, rows_s2, rows_r2,
    rim_s, rim_r, slab_s, slab_r, gap_all, gap_s, gap_r, reach_s, reach_r, push,
    in_sem, send_sem, recv_sem, con_send, con_recv,
):
    f32 = jnp.float32
    gx, gy = lax.axis_index("gx"), lax.axis_index("gy")
    front = n_x - 1
    is_front = gx == front
    has_up, has_down, has_left, has_right = gx > 0, gx < n_x - 1, gy > 0, gy < n_y - 1
    sub, lane = iota(0), iota(1)
    zero = jnp.zeros((8, 128), f32)

    x_of = {-1: lax.rem(gx + (n_x - 1), n_x), 0: gx, 1: lax.rem(gx + 1, n_x)}
    across = ((-1, has_left), (1, has_right))

    def peer(dx, dy):
        return (x_of[dx], gy + dy)

    barrier = pltpu.get_barrier_semaphore()

    def greet(where):
        pl.semaphore_signal(barrier, inc=1, device_id=where, device_id_type=MESH)

    for dy, there in across:
        @pl.when(there)
        def _(dy=dy):
            for dx in (-1, 1, 0):
                greet(peer(dx, dy))

    for dx in (-1, 1):
        greet(peer(dx, 0))

    @pl.when(is_front)
    def _():
        for i in range(1, n_x - 2):
            greet((i, gy))

    @pl.when((gx > 0) & (gx < n_x - 2))
    def _():
        greet((front, gy))

    def load(src, dst, k):
        return pltpu.make_async_copy(src, dst, in_sem.at[k])

    def span(kib):
        return coef.at[0 : kib // 4, 0, 0:8, :]

    first = [load(j_hbm, j_in, 0), load(d_hbm, d_in, 1), load(node_hbm, node, 2), load(inter_hbm, inter, 3)]
    plate = [load(s_hbm.at[:, 128 * k : 128 * k + 128], shell1.at[k, 8:136, :], 4) for k in range(4)]
    later = [load(bond_hbm, bond, 5), load(v_hbm, v_in, 6), load(w_hbm, shell_v, 7)]
    for copy in first + plate + later:
        copy.start()

    for r in (0, 72):
        for c in range(2):
            for v in range(7):
                shift_j[c, v, r : r + 8, :] = zero
                shift_p[c, v, r : r + 8, :] = zero
        for c in range(4):
            field1[c, r : r + 8, :] = zero
            field2[c, r : r + 8, :] = zero
    for field in (shell1, shell2):
        for r in (0, 136):
            for k in range(4):
                field[k, r : r + 8, :] = zero
    for b in range(1, 15):
        square[8 * b : 8 * b + 8, :] = zero

    first[0].wait()
    first[1].wait()
    for a in range(8):
        rows = pl.ds(8 + 8 * a, 8)
        for c in range(2):
            jit = swap_groups(j_in[c, a])
            dis = swap_groups(d_in[c, a])
            field1[c, rows, :] = jit
            field1[2 + c, rows, :] = jit + dis
            disp[c, pl.ds(8 * a, 8), :] = dis

    def edges(field, base):
        stack = jnp.concatenate([field[base, 8:72, :], field[base + 1, 8:72, :]], axis=0)
        across = jnp.transpose(stack)
        return across[0:8, :], across[120:128, :]

    jit_left, jit_right = edges(field1, 0)
    pos_left, pos_right = edges(field1, 2)
    edge_s1[0, 0] = jnp.where(sub < 3, jit_left, slide(pos_left, 3))
    edge_s1[1, 0] = jnp.where(sub > 4, jit_right, slide(pos_right, -3))

    def pack_rows(field, base):
        x, y = field[base, 8:16, :], field[base + 1, 8:16, :]
        first_rows = jnp.where(sub < 3, x, slide(y, 3))
        x, y = field[base, 64:72, :], field[base + 1, 64:72, :]
        return first_rows, jnp.where(sub > 4, x, slide(y, -3))

    for part, base in enumerate((0, 2)):
        rows_s1[0, part], rows_s1[1, part] = pack_rows(field1, base)

    def pack_slab(field):
        ends = []
        for start, at in ((8, 0), (128, 6)):
            total = zero
            for c in range(4):
                total = jnp.where(sub // 2 == c, slide(field[c, start : start + 8, :], 2 * c - at), total)
            ends.append(total)
        return ends

    first[2].wait()
    first[3].wait()
    inter[...] = swap_groups(inter[...])
    node[...] = swap_groups(node[...])

    def put_gap(step):
        gap = disp[0, 56:64, :] + inter[...]
        gap_all[...] = gap
        for i in range(8):
            gap_s[step, i] = gap[i : i + 1, :]

    put_gap(0)

    mine = jnp.broadcast_to(node[pl.ds(gx, 1), :], (8, 128))
    targets = []
    for k in range(4):
        n = pick(mine, 32 * k + lane // 4, 1)
        row = lax.shift_right_logical(n, width.bit_length() - 1) & 127
        targets.append(jnp.where((n & 3) == (lane & 3), row, -1))

    def gather_points(totals):
        own = []
        points = zero
        for k, total in enumerate(totals):
            for s in (4, 2, 1):
                total = total + slide(total, s)
            own.append(total)
            total = total + turn(total, -1)
            total = total + turn(total, -2)
            points = jnp.where(lane // 32 == k, pick(total, (lane & 31) * 4, 1), points)
        return own, points

    def pack_rim(field):
        left = right = zero
        for b in range(16):
            here = lane // 2 == b
            left = jnp.where(here, turn(field[0, 8 + 8 * b : 16 + 8 * b, :], 2 * b), left)
            right = jnp.where(here, turn(field[3, 8 + 8 * b : 16 + 8 * b, :], 2 * b + 2), right)
        return left, right

    load(shell1.at[:, 8:136, :], shell1.at[:, 8:136, :], 4).wait()
    totals = []
    for k in range(4):
        total = zero
        for b in range(16):
            x = shell1[k, 8 + 8 * b : 16 + 8 * b, :]
            total = total + jnp.where(sub + 8 * b == targets[k], x, 0.0)
        totals.append(total)
    own, points = gather_points(totals)
    reach_s[0] = points[0:1, :]
    left, right = pack_rim(shell1)
    edge_s1[0, 1] = left
    edge_s1[1, 1] = right
    rows_s1[0, 2], rows_s1[1, 2] = pack_slab(shell1)

    extra = jnp.where(is_front, n_x - 3, jnp.where((gx > 0) & (gx < n_x - 2), 1, 0))
    pl.semaphore_wait(barrier, 2 + 3 * has_left + 3 * has_right + extra)

    def send(src, dst, group, phase, where):
        pltpu.make_async_remote_copy(
            src, dst, send_sem.at[group], recv_sem.at[phase, group], device_id=where, device_id_type=MESH
        ).start()

    def send_columns(phase, src, dst):
        for side, (dy, there) in enumerate(across):
            @pl.when(there)
            def _(side=side, dy=dy):
                for dx in (-1, 1, 0):
                    send(src.at[side], dst.at[1 - dx, 1 - side], 2 - side, phase, peer(dx, dy))

    def send_rows(phase, src, dst):
        for k, dx in enumerate((-1, 1)):
            send(src.at[k], dst.at[1 - k], 0, phase, peer(dx, 0))

    def group_wait(kib, group, phase):
        return pltpu.make_async_remote_copy(
            span(kib), span(kib), send_sem.at[group], recv_sem.at[phase, group],
            device_id=peer(1, 0), device_id_type=MESH,
        )

    def arrived(phase, rows_kib, columns_kib):
        for side, (_, there) in enumerate(across):
            @pl.when(there)
            def _(side=side):
                group_wait(columns_kib, 1 + side, phase).wait_recv()

        group_wait(rows_kib, 0, phase).wait_recv()

    def gap_copy(step, i):
        return pltpu.make_async_remote_copy(
            gap_s.at[step, i], gap_r.at[step], con_send.at[0], con_recv.at[step],
            device_id=(i, gy), device_id_type=MESH,
        )

    def reach_copy(step):
        return pltpu.make_async_remote_copy(
            reach_s.at[step], reach_r.at[step, gx], con_send.at[0], con_recv.at[step],
            device_id=(front, gy), device_id_type=MESH,
        )

    def start_gap(step):
        @pl.when(is_front)
        def _():
            for i in range(n_x - 1):
                gap_copy(step, i).start()
            gap_r[step] = gap_s[step, n_x - 1]

    def start_reach(step):
        @pl.when(is_front)
        def _():
            reach_r[step, front] = reach_s[step]

        @pl.when(jnp.logical_not(is_front))
        def _():
            reach_copy(step).start()

    def end_contact(step):
        @pl.when(is_front)
        def _():
            slots = reach_r.at[step, 0 : n_x - 1]
            pltpu.make_async_remote_copy(
                slots, slots, con_send.at[0], con_recv.at[step], device_id=(0, gy), device_id_type=MESH
            ).wait_recv()
            reached = jnp.broadcast_to(reach_r[step, front], (8, 128))
            for i in range(n_x - 1):
                reached = jnp.where(sub == i, jnp.broadcast_to(reach_r[step, i], (8, 128)), reached)
            push[...] = PENALTY * jnp.maximum(gap_all[...] - reached, 0.0)

        @pl.when(jnp.logical_not(is_front))
        def _():
            gap_copy(step, 0).wait_recv()
            push[...] = jnp.zeros((8, 128), f32)

    send_columns(0, edge_s1, edge_r1)
    send_rows(0, rows_s1, rows_r1)
    start_gap(0)
    start_reach(0)

    later[0].wait()
    none = jnp.zeros((8, 128), jnp.int32)
    for s in range(9):
        for a in range(8):
            word = pick(jnp.broadcast_to(bond[8 * a : 8 * a + 8, s : s + 1], (8, 128)), lane // 16, 0)
            if s % 3 == 0:
                word = jnp.where(lane < 16, 0, word)
            if s % 3 == 2:
                word = jnp.where(lane >= 112, 0, word)
            if a == 0 and s < 3:
                row_words[0, s] = word
                word = none
            if a == 7 and s > 5:
                row_words[1, s - 6] = word
                word = none
            words[s, 8 * a : 8 * a + 8, :] = word
    col_words = []
    for side in range(2):
        tiles = bond[pl.ds(7 * side, 8, stride=8), :]
        for dx in range(3):
            s = 3 * dx + 2 * side
            word = jnp.broadcast_to(tiles[:, s : s + 1], (8, 128))
            col_words.append(pick(word, (lane & 63) // 8, 0))
    later[1].wait()
    for a in range(8):
        for c in range(2):
            vel[c, pl.ds(8 * a, 8), :] = swap_groups(v_in[c, a])

    def spread_field(field, index, out):
        for b in range(1, 9):
            x = field[index, 8 * b : 8 * b + 8, :]
            for v in range(-3, 4):
                if v:
                    out[v + 3, 8 * b : 8 * b + 8, :] = turn(x, -v)

    def ice_inside(step, field):
        last = step == 1
        sub_r = lax.broadcasted_iota(jnp.int32, (RUN, 128), 0)
        lane_r = lax.broadcasted_iota(jnp.int32, (RUN, 128), 1)
        tile_row, tile_col = sub_r & 7, lane_r & 15

        def body(a, carry):
            base = pl.multiple_of(RUN * a, RUN)
            rows = pl.ds(base, RUN)
            own = pl.ds(pl.multiple_of(base + 8, 8), RUN)

            def partner(shifted, c, u, v):
                there = pl.ds(base + (8 + u), RUN)
                if v == 0:
                    return field[(0 if shifted is shift_j else 2) + c, there, :]
                return shifted[c, v + 3, there, :]

            px = field[2, own, :]
            py = [field[3, own, :] - float(v) for v in range(-3, 4)]
            if not last:
                jx = field[0, own, :]
                jy = [field[1, own, :] - float(v) for v in range(-3, 4)]
            fx = fy = jnp.zeros((RUN, 128), f32)
            seen = None
            for n, (u, v) in enumerate(OFFSETS):
                if u != seen:
                    seen = u
                    px_u = px - float(u)
                    if not last:
                        jx_u = jx - float(u)
                        bit = bit_at(tile_row, tile_row + u)
                        flags = []
                        for dy in range(3):
                            word = words[3 + dy, rows, :]
                            if u < 0:
                                word = jnp.where(tile_row + u < 0, words[dy, rows, :], word)
                            if u > 0:
                                word = jnp.where(tile_row + u > 7, words[6 + dy, rows, :], word)
                            flags.append(intact_of(word, bit))
                if not last:
                    intact = flags[1]
                    if v < 0:
                        intact = jnp.where(tile_col + v < 0, flags[0], intact)
                    if v > 0:
                        intact = jnp.where(tile_col + v > 15, flags[2], intact)
                    rx = partner(shift_j, 0, u, v) - jx_u
                    ry = partner(shift_j, 1, u, v) - jy[v + 3]
                    near, far = bonds(intact, rx * rx + ry * ry + DELTA_SQ)
                    coef[n, 0, rows, :] = near
                    coef[n, 1, rows, :] = far
                else:
                    near = coef[n, 0, rows, :]
                    far = coef[n, 1, rows, :]
                nx = partner(shift_p, 0, u, v) - px_u
                ny = partner(shift_p, 1, u, v) - py[v + 3]
                factor = far - near * lax.rsqrt(nx * nx + ny * ny + DELTA_SQ)
                fx = fx + factor * nx
                fy = fy + factor * ny
            force[0, rows, :] = fx
            force[1, rows, :] = fy
            return carry

        lax.fori_loop(0, 64 // RUN, body, 0)

    top = sub < 4

    def ice_rows(step, field, rows_r):
        last = step == 1
        base = 2 if last else 0
        mine = [jnp.where(top, field[c, 8:16, :], field[c, 64:72, :]) for c in range(base, 4)]
        mine_y = [[mine[c] - float(v) for v in range(-3, 4)] for c in range(1, 4 - base, 2)]
        fx = fy = zero
        if not last:
            word = [jnp.where(top, row_words[0, dy], row_words[1, dy]) for dy in range(3)]
        seen = None
        for n, (u, v) in enumerate(ROW_OFFSETS):
            if u != seen:
                seen = u
                beyond = [
                    jnp.where(top, slide(rows_r[0, c // 2], u + 3 * (c % 2)), slide(rows_r[1, c // 2], -u - 3 * (c % 2)))
                    for c in range(4 - base)
                ]
                along = jnp.where(top, -float(u), float(u))
                mine_x = [mine[c] - along for c in range(0, 4 - base, 2)]
                if not last:
                    inside = ((sub < u) & has_up) | ((sub >= 8 - u) & has_down)
                    bit = bit_at(sub, sub + jnp.where(top, -u, u))
                    flags = [jnp.where(inside, intact_of(w, bit), 0.0) for w in word]
            if not last:
                intact = flags[1]
                if v < 0:
                    intact = jnp.where((lane & 15) + v < 0, flags[0], intact)
                if v > 0:
                    intact = jnp.where((lane & 15) + v > 15, flags[2], intact)
                rx = turn(beyond[0], -v) - mine_x[0]
                ry = turn(beyond[1], -v) - mine_y[0][v + 3]
                near, far = bonds(intact, rx * rx + ry * ry + DELTA_SQ)
                row_coef[n, 0] = near
                row_coef[n, 1] = far
            else:
                near, far = row_coef[n, 0], row_coef[n, 1]
            nx = turn(beyond[2 - base], -v) - mine_x[-1]
            ny = turn(beyond[3 - base], -v) - mine_y[-1][v + 3]
            factor = far - near * lax.rsqrt(nx * nx + ny * ny + DELTA_SQ)
            fx = fx + factor * nx
            fy = fy + factor * ny
        return fx, fy

    near_col = jnp.where(sub < 3, 0, jnp.where(sub < 5, 1, 2))
    far_col = jnp.where(sub < 3, sub + 1, jnp.where(sub < 5, sub - 2, 1))
    point_row = lane & 63

    def ice_columns(step, edge_s, edge_r):
        last = step == 1
        parts = (0,) if last else (0, 1)
        whole = []
        for side in range(2):
            sign = 1.0 if side else -1.0
            mine_at = 7 - near_col if side else near_col
            beyond_at = far_col - 1 if side else 8 - far_col
            shifts = [3 * p for p in parts]
            mine = [pick(edge_s[side, 0], mine_at - h if side else mine_at + h, 0) for h in shifts]
            beyond = [
                [pick(edge_r[slot, side, 0], beyond_at + h if side else beyond_at - h, 0) for slot in range(3)]
                for h in shifts
            ]
            across = (near_col + far_col).astype(f32) * sign
            total = zero
            for u in range(-3, 4):
                def moved(p):
                    if u == 0:
                        return beyond[p][1]
                    inside = point_row + u >= 0 if u < 0 else point_row + u <= 63
                    return jnp.where(inside, turn(beyond[p][1], -u), turn(beyond[p][0 if u < 0 else 2], 64 - u))

                offset = jnp.where(lane < 64, float(u), across)
                if not last:
                    word = col_words[3 * side + 1]
                    if u < 0:
                        word = jnp.where((lane & 7) + u < 0, col_words[3 * side], word)
                    if u > 0:
                        word = jnp.where((lane & 7) + u > 7, col_words[3 * side + 2], word)
                    intact = intact_of(word, bit_at(lane, lane + u))
                    there = (sub < 6) & (has_right if side else has_left)
                    if u < 0:
                        there = there & ((point_row + u >= 0) | has_up)
                    if u > 0:
                        there = there & ((point_row + u <= 63) | has_down)
                    intact = jnp.where(there, intact, 0.0)
                    rest = (moved(0) - mine[0]) + offset
                    square_of = rest * rest
                    near, far = bonds(intact, square_of + turn(square_of, 64) + DELTA_SQ)
                    col_coef[side, u + 3, 0] = near
                    col_coef[side, u + 3, 1] = far
                else:
                    near, far = col_coef[side, u + 3, 0], col_coef[side, u + 3, 1]
                now = (moved(len(parts) - 1) - mine[-1]) + offset
                square_of = now * now
                factor = far - near * lax.rsqrt(square_of + turn(square_of, 64) + DELTA_SQ)
                total = total + factor * now
            at = 7 - sub if side else sub
            total = jnp.where(has_right if side else has_left, total, 0.0)
            whole.append(
                jnp.where(at < 3, pick(total, jnp.where(at == 0, 0, jnp.where(at == 1, 3, 5)), 0), 0.0)
                + jnp.where(at < 2, pick(total, jnp.where(at == 0, 1, 4), 0), 0.0)
                + jnp.where(at == 0, pick(total, jnp.full((8, 128), 2, jnp.int32), 0), 0.0)
            )
        square[0:8, :] = whole[0]
        square[120:128, :] = whole[1]
        return jnp.transpose(square[...])

    def ice_finish(step, rows_force, columns_force):
        last = step == 1
        for a in range(8):
            rows = pl.ds(8 * a, 8)
            for c in range(2):
                total = force[c, rows, :] + columns_force[64 * c + 8 * a : 64 * c + 8 * a + 8, :]
                if a == 0:
                    total = total + jnp.where(top, rows_force[c], 0.0)
                if a == 7:
                    total = total + jnp.where(top, 0.0, rows_force[c])
                    if c == 0:
                        total = total - push[...]
                speed = vel[c, rows, :] + STEP_DT * total
                moved = disp[c, rows, :] + STEP_DT * speed
                if last:
                    v_out[c, a] = swap_groups(speed)
                    d_out[c, a] = swap_groups(moved)
                else:
                    vel[c, rows, :] = speed
                    disp[c, rows, :] = moved
                    field2[2 + c, 8 + 8 * a : 16 + 8 * a, :] = field1[c, 8 + 8 * a : 16 + 8 * a, :] + moved

    def sideways(x, first, last):
        up = [turn(c, 1) for c in x]
        down = [turn(c, -1) for c in x]
        return [
            jnp.where(lane == 0, up[k - 1] if k else first, up[k])
            + jnp.where(lane == 127, down[k + 1] if k < 3 else last, down[k])
            for k in range(4)
        ]

    def shell_inside(field, put):
        def chunks(ref, start):
            return [ref[k, pl.ds(start, 8), :] for k in range(4)]

        def once(b, carry):
            for h in range(4):
                i = pl.multiple_of(32 * b + 8 * h + 8, 8)
                f, up, down = chunks(field, i), chunks(field, i - 1), chunks(field, i + 1)
                for k, side in enumerate(sideways(f, 0.0, 0.0)):
                    bend1[k, pl.ds(i, 8), :] = (up[k] + down[k]) + side - 4.0 * f[k]
            return carry

        def twice(b, carry):
            for h in range(4):
                base = pl.multiple_of(32 * b + 8 * h, 8)
                i = pl.multiple_of(base + 8, 8)
                f, g = chunks(field, i), chunks(bend1, i)
                up, down = chunks(bend1, i - 1), chunks(bend1, i + 1)
                for k, side in enumerate(sideways(g, f[0], f[3])):
                    at = (pl.ds(base, 8), slice(128 * k, 128 * k + 128))
                    bending = (up[k] + down[k]) + side - 4.0 * g[k]
                    speed = shell_v[at] - (STEP_DT * BEND) * bending
                    shell_v[at] = speed
                    put(base, k, f[k] + STEP_DT * speed)
            return carry

        lax.fori_loop(0, 4, once, 0)
        for k in range(4):
            bend1[k, 7:8, :] = field[k, 8:9, :]
            bend1[k, 136:137, :] = field[k, 135:136, :]
        lax.fori_loop(0, 4, twice, 0)

    def rim_terms(step, side):
        above, level, below = (edge_r1[t, side, 1] if step == 0 else rim_r[t, side] for t in range(3))
        level = jnp.where(lane < 2, jnp.where(has_up, turn(above, -30), 0.0), turn(level, 2))
        rim = jnp.where(lane >= 34, jnp.where(has_down, turn(below, 34), 0.0), level)
        rim = jnp.where(has_right if side else has_left, rim, 0.0)
        first = turn(rim, 1 if side else -1)
        up, down = slide(first, 1), slide(first, -1)
        up = jnp.where(sub == 0, turn(up, 2), up)
        down = jnp.where(sub == 7, turn(down, -2), down)
        full = rim - 8.0 * first + 2.0 * (up + down)
        return jnp.where((lane & 1) == side, full, rim)

    def slab_terms(step):
        terms = []
        for k in range(2):
            slab = rows_r1[k, 2] if step == 0 else slab_r[k]
            slab = jnp.where(has_down if k else has_up, slab, 0.0)
            outer = [slide(slab, (6 if k else 0) - 2 * c) for c in range(4)]
            inner = [slide(slab, (7 if k else -1) - 2 * c) for c in range(4)]
            at = 7 - sub if k else sub
            terms.append(
                [
                    jnp.where(at < 2, o, 0.0) + jnp.where(at == 0, 2.0 * pair - 8.0 * x, 0.0)
                    for o, x, pair in zip(outer, inner, sideways(inner, 0.0, 0.0))
                ]
            )
        return terms

    def shell_finish(step, own, put, get):
        gaps = jnp.broadcast_to(gap_r[step], (8, 128))
        slabs = slab_terms(step)
        rims = [rim_terms(step, side) for side in range(2)]
        totals = []
        for k in range(4):
            gap = pick(gaps, 32 * k + lane // 4, 1)
            load = (STEP_DT * PENALTY) * jnp.maximum(gap - own[k], 0.0)
            total = zero
            for b in range(16):
                here = sub + 8 * b == targets[k]
                change = jnp.where(here, load, 0.0)
                beyond = None
                if b == 0:
                    beyond = slabs[0][k]
                if b == 15:
                    beyond = slabs[1][k]
                if k == 0 or k == 3:
                    rim = turn(rims[k // 3], (124 if k else -2) - 2 * b)
                    rim = jnp.where(lane >= 126 if k else lane < 2, rim, 0.0)
                    beyond = rim if beyond is None else beyond + rim
                if beyond is not None:
                    change = change - (STEP_DT * BEND) * beyond
                at = (pl.ds(8 * b, 8), slice(128 * k, 128 * k + 128))
                shell_v[at] = shell_v[at] + change
                moved = get(8 * b, k) + STEP_DT * change
                put(8 * b, k, moved)
                total = total + jnp.where(here, moved, 0.0)
            totals.append(total)
        return totals

    def put_block(base, k, moved):
        shell2[k, pl.ds(base + 8, 8), :] = moved

    def get_block(base, k):
        return shell2[k, pl.ds(base + 8, 8), :]

    def out_block(base, k, moved):
        s_out[pl.ds(base, 8), 128 * k : 128 * k + 128] = moved

    def out_get(base, k):
        return s_out[pl.ds(base, 8), 128 * k : 128 * k + 128]

    for c in range(2):
        spread_field(field1, c, shift_j.at[c])
        spread_field(field1, 2 + c, shift_p.at[c])
    ice_inside(0, field1)
    later[2].wait()
    shell_inside(shell1, put_block)

    arrived(0, 24, 24)
    columns_force = ice_columns(0, edge_s1, edge_r1)
    rows_force = ice_rows(0, field1, rows_r1)
    end_contact(0)
    ice_finish(0, rows_force, columns_force)
    put_gap(1)
    left, right = edges(field2, 2)
    edge_s2[0, 0] = left
    edge_s2[1, 0] = right
    rows_s2[0, 0], rows_s2[1, 0] = pack_rows(field2, 2)
    send_columns(1, edge_s2, edge_r2)
    send_rows(1, rows_s2, rows_r2)
    start_gap(1)

    totals = shell_finish(0, own, put_block, get_block)
    own, points = gather_points(totals)
    reach_s[1] = points[0:1, :]
    start_reach(1)
    left, right = pack_rim(shell2)
    rim_s[0] = left
    rim_s[1] = right
    slab_s[0], slab_s[1] = pack_slab(shell2)
    send_columns(2, rim_s, rim_r)
    send_rows(2, slab_s, slab_r)

    for c in range(2):
        spread_field(field2, 2 + c, shift_p.at[c])
    ice_inside(1, field2)
    shell_inside(shell2, out_block)

    arrived(1, 8, 12)
    columns_force = ice_columns(1, edge_s2, edge_r2)
    rows_force = ice_rows(1, field2, rows_r2)
    end_contact(1)
    ice_finish(1, rows_force, columns_force)
    arrived(2, 8, 12)
    shell_finish(1, own, out_block, out_get)

    for side, (_, there) in enumerate(across):
        @pl.when(there)
        def _(side=side):
            group_wait(48, 2 - side, 0).wait_send()

    group_wait(40, 0, 0).wait_send()

    @pl.when(is_front)
    def _():
        slots = reach_r.at[:, 0 : n_x - 1]
        pltpu.make_async_remote_copy(
            slots, slots, con_send.at[0], con_recv.at[0], device_id=(0, gy), device_id_type=MESH
        ).wait_send()

    @pl.when(jnp.logical_not(is_front))
    def _():
        pltpu.make_async_remote_copy(
            gap_r, gap_r, con_send.at[0], con_recv.at[0], device_id=(front, gy), device_id_type=MESH
        ).wait_send()


def write_out(*refs):
    copies = [pltpu.make_async_copy(refs[k], refs[4 + k], refs[8].at[k]) for k in range(4)]
    for copy in copies:
        copy.start()
    for copy in copies:
        copy.wait()


def on_device(n_x, n_y, width, d, v, j, bond, node, inter, shell, speed):
    f32, i32 = jnp.float32, jnp.int32
    vmem = pltpu.VMEM
    dma = pltpu.SemaphoreType.DMA
    shapes = [x.shape for x in (d, v, shell, speed)]
    held = pl.pallas_call(
        functools.partial(kernel, n_x, n_y, width),
        out_shape=[vmem(s, f32) for s in shapes],
        in_specs=[pl.BlockSpec(memory_space=pl.ANY)] * 8,
        out_specs=[pl.BlockSpec(memory_space=vmem)] * 4,
        scratch_shapes=[
            vmem(d.shape, f32), vmem(v.shape, f32), vmem(j.shape, f32), vmem(bond.shape, i32),
            vmem(node.shape, i32), vmem(inter.shape, f32),
            vmem((4, 80, 128), f32), vmem((4, 80, 128), f32), vmem((2, 64, 128), f32), vmem((2, 64, 128), f32),
            vmem((2, 64, 128), f32),
            vmem((2, 7, 80, 128), f32), vmem((2, 7, 80, 128), f32), vmem((9, 64, 128), i32),
            vmem((len(OFFSETS), 2, 64, 128), f32), vmem((len(ROW_OFFSETS), 2, 8, 128), f32),
            vmem((2, 7, 2, 8, 128), f32),
            vmem((2, 3, 8, 128), i32), vmem((4, 144, 128), f32), vmem((4, 144, 128), f32), vmem((4, 144, 128), f32),
            vmem((128, 128), f32),
            vmem((2, 2, 8, 128), f32), vmem((3, 2, 2, 8, 128), f32),
            vmem((2, 1, 8, 128), f32), vmem((3, 2, 1, 8, 128), f32),
            vmem((2, 3, 8, 128), f32), vmem((2, 3, 8, 128), f32), vmem((2, 1, 8, 128), f32), vmem((2, 1, 8, 128), f32),
            vmem((2, 8, 128), f32), vmem((3, 2, 8, 128), f32), vmem((2, 8, 128), f32), vmem((2, 8, 128), f32),
            vmem((8, 128), f32), vmem((2, n_x, 1, 128), f32), vmem((2, 1, 128), f32),
            vmem((2, 1, 128), f32), vmem((2, n_x, 1, 128), f32), vmem((8, 128), f32),
            dma((8,)), dma((3,)), dma((3, 3)), dma((1,)), dma((2,)),
        ],
        compiler_params=pltpu.CompilerParams(collective_id=0, has_side_effects=True),
    )(d, v, j, bond, node, inter, shell, speed)
    return pl.pallas_call(
        write_out,
        out_shape=[jax.ShapeDtypeStruct(s, f32) for s in shapes],
        in_specs=[pl.BlockSpec(memory_space=vmem)] * 4,
        out_specs=[pl.BlockSpec(memory_space=pl.ANY)] * 4,
        scratch_shapes=[dma((4,))],
    )(*[pltpu.with_memory_space_constraint(x, vmem) for x in held])


def solution(mesh):
    n_x, n_y = mesh.shape["gx"], mesh.shape["gy"]
    ice, plate = P(None, "gx", "gy", None), P("gx", "gy")

    def step(d, v, j, bond, *rest):
        width = rest[2].shape[1] * n_y
        return on_device(n_x, n_y, width, d, v, j, bond.reshape(-1, bond.shape[2]), *rest)

    return jax.shard_map(
        step,
        mesh=mesh,
        in_specs=(ice, ice, ice, P("gx", "gy", None), P("gy", None), P("gy", None), plate, plate),
        out_specs=(ice, ice, plate, plate),
        check_vma=False,
    )
```

```python
import functools

import jax
import jax.numpy as jnp
from jax import lax
from jax.experimental import pallas as pl
from jax.experimental.pallas import tpu as pltpu
from jax.sharding import PartitionSpec as P

MESH = pl.DeviceIdType.MESH

HORIZON = 3.5
DELTA_SQ = 0.25
PENALTY = 4.0
BEND = 0.5
STEP_DT = 0.2
RUN = 32

OFFSETS = [
    (u, v)
    for u in range(-3, 4)
    for v in range(-3, 4)
    if (u, v) != (0, 0) and max(abs(u) - 0.4, 0) ** 2 + max(abs(v) - 0.4, 0) ** 2 < HORIZON**2 - DELTA_SQ
]
ROW_OFFSETS = [(u, v) for u, v in OFFSETS if u > 0]
SIDES = [(dx, dy) for dx in (-1, 0, 1) for dy in (-1, 0, 1) if (dx, dy) != (0, 0)]


def iota(axis):
    return lax.broadcasted_iota(jnp.int32, (8, 128), axis)


def pick(x, index, axis):
    return jnp.take_along_axis(x, index, axis=axis, mode="promise_in_bounds")


def swap_groups(x):
    sub, group = iota(0), iota(1) // 16
    x = pltpu.roll(x, 0, 1, stride=16, stride_axis=0)
    x = pick(x, (group - sub) & 7, 0)
    return pick(x, ((group + sub) & 7) * 16 + (iota(1) & 15), 1)


def turn(x, shift):
    shift = shift % 128
    return pltpu.roll(x, shift, 1) if shift else x


def slide(x, shift):
    return pltpu.roll(x, shift % 8, 0)


def bonds(intact, square):
    inverse = lax.rsqrt(square)
    reach = jnp.maximum(HORIZON - square * inverse, 0.0)
    near = intact * (reach * reach)
    return near, near * inverse


def intact_of(word, bit):
    return jnp.where((word & bit) != 0, 1.0 / HORIZON**2, 0.0)


def bit_at(row, beyond):
    return jnp.left_shift(1, 4 * (row & 7) + ((beyond & 7) >> 1))


def kernel(
    n_x, n_y, width,
    d_hbm, v_hbm, j_hbm, bond_hbm, node_hbm, inter_hbm, s_hbm, w_hbm,
    d_out, v_out, s_out, shell_v,
    d_in, v_in, j_in, bond, node, inter,
    field1, field2, disp, vel, force, shift_j, shift_p, words, coef, row_coef, col_coef,
    row_words, shell1, shell2, bend1, square,
    edge_s1, edge_r1, edge_s2, edge_r2, rows_s1, rows_r1, rows_s2, rows_r2,
    rim_s, rim_r, slab_s, slab_r, gap_all, gap_s, gap_r, reach_s, reach_r, push,
    in_sem, send_sem, recv_sem, con_send, con_recv,
):
    f32 = jnp.float32
    gx, gy = lax.axis_index("gx"), lax.axis_index("gy")
    front = n_x - 1
    is_front = gx == front
    has_up, has_down, has_left, has_right = gx > 0, gx < n_x - 1, gy > 0, gy < n_y - 1
    sub, lane = iota(0), iota(1)
    zero = jnp.zeros((8, 128), f32)

    across = {-1: has_left, 1: has_right}
    along = {-1: has_up, 1: has_down}

    def with_peer(dx, dy, run):
        there = along[dx] & across[dy] if dx and dy else along[dx] if dx else across[dy]

        @pl.when(there)
        def _():
            run((gx + dx, gy + dy))

    barrier = pltpu.get_barrier_semaphore()

    def greet(where):
        pl.semaphore_signal(barrier, inc=1, device_id=where, device_id_type=MESH)

    for dx, dy in SIDES:
        with_peer(dx, dy, greet)

    @pl.when(is_front)
    def _():
        for i in range(n_x - 2):
            greet((i, gy))

    @pl.when(gx < n_x - 2)
    def _():
        greet((front, gy))

    def load(src, dst, k):
        return pltpu.make_async_copy(src, dst, in_sem.at[k])

    def span(kib):
        return coef.at[0 : kib // 4, 0, 0:8, :]

    first = [load(j_hbm, j_in, 0), load(d_hbm, d_in, 1), load(node_hbm, node, 2), load(inter_hbm, inter, 3)]
    plate = [load(s_hbm.at[:, 128 * k : 128 * k + 128], shell1.at[k, 8:136, :], 4) for k in range(4)]
    later = [load(bond_hbm, bond, 5), load(v_hbm, v_in, 6), load(w_hbm, shell_v, 7)]
    for copy in first + plate + later:
        copy.start()

    for r in (0, 72):
        for c in range(2):
            for v in range(7):
                shift_j[c, v, r : r + 8, :] = zero
                shift_p[c, v, r : r + 8, :] = zero
        for c in range(4):
            field1[c, r : r + 8, :] = zero
            field2[c, r : r + 8, :] = zero
    for field in (shell1, shell2):
        for r in (0, 136):
            for k in range(4):
                field[k, r : r + 8, :] = zero
    for b in range(1, 15):
        square[8 * b : 8 * b + 8, :] = zero

    first[0].wait()
    first[1].wait()
    for a in range(8):
        rows = pl.ds(8 + 8 * a, 8)
        for c in range(2):
            jit = swap_groups(j_in[c, a])
            dis = swap_groups(d_in[c, a])
            field1[c, rows, :] = jit
            field1[2 + c, rows, :] = jit + dis
            disp[c, pl.ds(8 * a, 8), :] = dis

    def edges(field, base):
        stack = jnp.concatenate([field[base, 8:72, :], field[base + 1, 8:72, :]], axis=0)
        across = jnp.transpose(stack)
        return across[0:8, :], across[120:128, :]

    jit_left, jit_right = edges(field1, 0)
    pos_left, pos_right = edges(field1, 2)
    edge_s1[0, 0] = jnp.where(sub < 3, jit_left, slide(pos_left, 3))
    edge_s1[1, 0] = jnp.where(sub > 4, jit_right, slide(pos_right, -3))

    def pack_rows(field, base):
        x, y = field[base, 8:16, :], field[base + 1, 8:16, :]
        first_rows = jnp.where(sub < 3, x, slide(y, 3))
        x, y = field[base, 64:72, :], field[base + 1, 64:72, :]
        return first_rows, jnp.where(sub > 4, x, slide(y, -3))

    for part, base in enumerate((0, 2)):
        rows_s1[0, part], rows_s1[1, part] = pack_rows(field1, base)

    def pack_slab(field):
        ends = []
        for start, at in ((8, 0), (128, 6)):
            total = zero
            for c in range(4):
                total = jnp.where(sub // 2 == c, slide(field[c, start : start + 8, :], 2 * c - at), total)
            ends.append(total)
        return ends

    first[2].wait()
    first[3].wait()
    inter[...] = swap_groups(inter[...])
    node[...] = swap_groups(node[...])

    def put_gap(step):
        gap = disp[0, 56:64, :] + inter[...]
        gap_all[...] = gap
        for i in range(8):
            gap_s[step, i] = gap[i : i + 1, :]

    put_gap(0)

    mine = jnp.broadcast_to(node[pl.ds(gx, 1), :], (8, 128))
    targets = []
    for k in range(4):
        n = pick(mine, 32 * k + lane // 4, 1)
        row = lax.shift_right_logical(n, width.bit_length() - 1) & 127
        targets.append(jnp.where((n & 3) == (lane & 3), row, -1))

    def gather_points(totals):
        own = []
        points = zero
        for k, total in enumerate(totals):
            for s in (4, 2, 1):
                total = total + slide(total, s)
            own.append(total)
            total = total + turn(total, -1)
            total = total + turn(total, -2)
            points = jnp.where(lane // 32 == k, pick(total, (lane & 31) * 4, 1), points)
        return own, points

    def pack_rim(field):
        left = right = zero
        for b in range(16):
            here = lane // 2 == b
            left = jnp.where(here, turn(field[0, 8 + 8 * b : 16 + 8 * b, :], 2 * b), left)
            right = jnp.where(here, turn(field[3, 8 + 8 * b : 16 + 8 * b, :], 2 * b + 2), right)
        return left, right

    load(shell1.at[:, 8:136, :], shell1.at[:, 8:136, :], 4).wait()
    totals = []
    for k in range(4):
        total = zero
        for b in range(16):
            x = shell1[k, 8 + 8 * b : 16 + 8 * b, :]
            total = total + jnp.where(sub + 8 * b == targets[k], x, 0.0)
        totals.append(total)
    own, points = gather_points(totals)
    reach_s[0] = points[0:1, :]
    left, right = pack_rim(shell1)
    edge_s1[0, 1] = left
    edge_s1[1, 1] = right
    rows_s1[0, 2], rows_s1[1, 2] = pack_slab(shell1)

    n_along = has_up.astype(jnp.int32) + has_down.astype(jnp.int32)
    n_across = has_left.astype(jnp.int32) + has_right.astype(jnp.int32)
    extra = jnp.where(is_front, n_x - 2, jnp.where(gx < n_x - 2, 1, 0))
    pl.semaphore_wait(barrier, n_along + n_across + n_along * n_across + extra)

    def send(src, dst, phase, dx, dy):
        with_peer(dx, dy, lambda where: pltpu.make_async_remote_copy(
            src, dst, send_sem.at[1 - dx, 1 - dy], recv_sem.at[phase, 1 - dx, 1 - dy],
            device_id=where, device_id_type=MESH,
        ).start())

    def send_columns(phase, src, dst):
        for dy in (-1, 1):
            side = (dy + 1) // 2
            for dx in (-1, 1, 0):
                send(src.at[side], dst.at[1 - dx, 1 - side], phase, dx, dy)

    def send_rows(phase, src, dst):
        for k, dx in enumerate((-1, 1)):
            send(src.at[k], dst.at[1 - k], phase, dx, 0)

    def group_wait(kib, dx, dy, phase):
        return pltpu.make_async_remote_copy(
            span(kib), span(kib), send_sem.at[1 - dx, 1 - dy], recv_sem.at[phase, 1 + dx, 1 + dy],
            device_id=(0, 0), device_id_type=MESH,
        )

    def arrived(phase, rows_kib, columns_kib):
        for dx, dy in SIDES:
            kib = columns_kib if dy else rows_kib
            with_peer(dx, dy, lambda where: group_wait(kib, dx, dy, phase).wait_recv())

    def gap_copy(step, i):
        return pltpu.make_async_remote_copy(
            gap_s.at[step, i], gap_r.at[step], con_send.at[0], con_recv.at[step],
            device_id=(i, gy), device_id_type=MESH,
        )

    def reach_copy(step):
        return pltpu.make_async_remote_copy(
            reach_s.at[step], reach_r.at[step, gx], con_send.at[0], con_recv.at[step],
            device_id=(front, gy), device_id_type=MESH,
        )

    def start_gap(step):
        @pl.when(is_front)
        def _():
            for i in range(n_x - 1):
                gap_copy(step, i).start()
            gap_r[step] = gap_s[step, n_x - 1]

    def start_reach(step):
        @pl.when(is_front)
        def _():
            reach_r[step, front] = reach_s[step]

        @pl.when(jnp.logical_not(is_front))
        def _():
            reach_copy(step).start()

    def end_contact(step):
        @pl.when(is_front)
        def _():
            slots = reach_r.at[step, 0 : n_x - 1]
            pltpu.make_async_remote_copy(
                slots, slots, con_send.at[0], con_recv.at[step], device_id=(0, gy), device_id_type=MESH
            ).wait_recv()
            reached = jnp.broadcast_to(reach_r[step, front], (8, 128))
            for i in range(n_x - 1):
                reached = jnp.where(sub == i, jnp.broadcast_to(reach_r[step, i], (8, 128)), reached)
            push[...] = PENALTY * jnp.maximum(gap_all[...] - reached, 0.0)

        @pl.when(jnp.logical_not(is_front))
        def _():
            gap_copy(step, 0).wait_recv()
            push[...] = jnp.zeros((8, 128), f32)

    send_columns(0, edge_s1, edge_r1)
    send_rows(0, rows_s1, rows_r1)
    start_gap(0)
    start_reach(0)

    later[0].wait()
    none = jnp.zeros((8, 128), jnp.int32)
    for s in range(9):
        for a in range(8):
            word = pick(jnp.broadcast_to(bond[8 * a : 8 * a + 8, s : s + 1], (8, 128)), lane // 16, 0)
            if s % 3 == 0:
                word = jnp.where(lane < 16, 0, word)
            if s % 3 == 2:
                word = jnp.where(lane >= 112, 0, word)
            if a == 0 and s < 3:
                row_words[0, s] = word
                word = none
            if a == 7 and s > 5:
                row_words[1, s - 6] = word
                word = none
            words[s, 8 * a : 8 * a + 8, :] = word
    col_words = []
    for side in range(2):
        tiles = bond[pl.ds(7 * side, 8, stride=8), :]
        for dx in range(3):
            s = 3 * dx + 2 * side
            word = jnp.broadcast_to(tiles[:, s : s + 1], (8, 128))
            col_words.append(pick(word, (lane & 63) // 8, 0))
    later[1].wait()
    for a in range(8):
        for c in range(2):
            vel[c, pl.ds(8 * a, 8), :] = swap_groups(v_in[c, a])

    def spread_field(field, index, out):
        for b in range(1, 9):
            x = field[index, 8 * b : 8 * b + 8, :]
            for v in range(-3, 4):
                if v:
                    out[v + 3, 8 * b : 8 * b + 8, :] = turn(x, -v)

    def ice_inside(step, field):
        last = step == 1
        sub_r = lax.broadcasted_iota(jnp.int32, (RUN, 128), 0)
        lane_r = lax.broadcasted_iota(jnp.int32, (RUN, 128), 1)
        tile_row, tile_col = sub_r & 7, lane_r & 15

        def body(a, carry):
            base = pl.multiple_of(RUN * a, RUN)
            rows = pl.ds(base, RUN)
            own = pl.ds(pl.multiple_of(base + 8, 8), RUN)

            def partner(shifted, c, u, v):
                there = pl.ds(base + (8 + u), RUN)
                if v == 0:
                    return field[(0 if shifted is shift_j else 2) + c, there, :]
                return shifted[c, v + 3, there, :]

            px = field[2, own, :]
            py = [field[3, own, :] - float(v) for v in range(-3, 4)]
            if not last:
                jx = field[0, own, :]
                jy = [field[1, own, :] - float(v) for v in range(-3, 4)]
            fx = fy = jnp.zeros((RUN, 128), f32)
            seen = None
            for n, (u, v) in enumerate(OFFSETS):
                if u != seen:
                    seen = u
                    px_u = px - float(u)
                    if not last:
                        jx_u = jx - float(u)
                        bit = bit_at(tile_row, tile_row + u)
                        flags = []
                        for dy in range(3):
                            word = words[3 + dy, rows, :]
                            if u < 0:
                                word = jnp.where(tile_row + u < 0, words[dy, rows, :], word)
                            if u > 0:
                                word = jnp.where(tile_row + u > 7, words[6 + dy, rows, :], word)
                            flags.append(intact_of(word, bit))
                if not last:
                    intact = flags[1]
                    if v < 0:
                        intact = jnp.where(tile_col + v < 0, flags[0], intact)
                    if v > 0:
                        intact = jnp.where(tile_col + v > 15, flags[2], intact)
                    rx = partner(shift_j, 0, u, v) - jx_u
                    ry = partner(shift_j, 1, u, v) - jy[v + 3]
                    near, far = bonds(intact, rx * rx + ry * ry + DELTA_SQ)
                    coef[n, 0, rows, :] = near
                    coef[n, 1, rows, :] = far
                else:
                    near = coef[n, 0, rows, :]
                    far = coef[n, 1, rows, :]
                nx = partner(shift_p, 0, u, v) - px_u
                ny = partner(shift_p, 1, u, v) - py[v + 3]
                factor = far - near * lax.rsqrt(nx * nx + ny * ny + DELTA_SQ)
                fx = fx + factor * nx
                fy = fy + factor * ny
            force[0, rows, :] = fx
            force[1, rows, :] = fy
            return carry

        lax.fori_loop(0, 64 // RUN, body, 0)

    top = sub < 4

    def ice_rows(step, field, rows_r):
        last = step == 1
        base = 2 if last else 0
        mine = [jnp.where(top, field[c, 8:16, :], field[c, 64:72, :]) for c in range(base, 4)]
        mine_y = [[mine[c] - float(v) for v in range(-3, 4)] for c in range(1, 4 - base, 2)]
        fx = fy = zero
        if not last:
            word = [jnp.where(top, row_words[0, dy], row_words[1, dy]) for dy in range(3)]
        seen = None
        for n, (u, v) in enumerate(ROW_OFFSETS):
            if u != seen:
                seen = u
                beyond = [
                    jnp.where(top, slide(rows_r[0, c // 2], u + 3 * (c % 2)), slide(rows_r[1, c // 2], -u - 3 * (c % 2)))
                    for c in range(4 - base)
                ]
                along = jnp.where(top, -float(u), float(u))
                mine_x = [mine[c] - along for c in range(0, 4 - base, 2)]
                if not last:
                    inside = ((sub < u) & has_up) | ((sub >= 8 - u) & has_down)
                    bit = bit_at(sub, sub + jnp.where(top, -u, u))
                    flags = [jnp.where(inside, intact_of(w, bit), 0.0) for w in word]
            if not last:
                intact = flags[1]
                if v < 0:
                    intact = jnp.where((lane & 15) + v < 0, flags[0], intact)
                if v > 0:
                    intact = jnp.where((lane & 15) + v > 15, flags[2], intact)
                rx = turn(beyond[0], -v) - mine_x[0]
                ry = turn(beyond[1], -v) - mine_y[0][v + 3]
                near, far = bonds(intact, rx * rx + ry * ry + DELTA_SQ)
                row_coef[n, 0] = near
                row_coef[n, 1] = far
            else:
                near, far = row_coef[n, 0], row_coef[n, 1]
            nx = turn(beyond[2 - base], -v) - mine_x[-1]
            ny = turn(beyond[3 - base], -v) - mine_y[-1][v + 3]
            factor = far - near * lax.rsqrt(nx * nx + ny * ny + DELTA_SQ)
            fx = fx + factor * nx
            fy = fy + factor * ny
        present = (top & has_up) | (jnp.logical_not(top) & has_down)
        return jnp.where(present, fx, 0.0), jnp.where(present, fy, 0.0)

    near_col = jnp.where(sub < 3, 0, jnp.where(sub < 5, 1, 2))
    far_col = jnp.where(sub < 3, sub + 1, jnp.where(sub < 5, sub - 2, 1))
    point_row = lane & 63

    def ice_columns(step, edge_s, edge_r):
        last = step == 1
        parts = (0,) if last else (0, 1)
        whole = []
        for side in range(2):
            sign = 1.0 if side else -1.0
            mine_at = 7 - near_col if side else near_col
            beyond_at = far_col - 1 if side else 8 - far_col
            shifts = [3 * p for p in parts]
            mine = [pick(edge_s[side, 0], mine_at - h if side else mine_at + h, 0) for h in shifts]
            beyond = [
                [pick(edge_r[slot, side, 0], beyond_at + h if side else beyond_at - h, 0) for slot in range(3)]
                for h in shifts
            ]
            sideways_by = (near_col + far_col).astype(f32) * sign
            total = zero
            for u in range(-3, 4):
                def moved(p):
                    if u == 0:
                        return beyond[p][1]
                    inside = (point_row + u >= 0) | jnp.logical_not(has_up)
                    if u > 0:
                        inside = (point_row + u <= 63) | jnp.logical_not(has_down)
                    return jnp.where(inside, turn(beyond[p][1], -u), turn(beyond[p][0 if u < 0 else 2], 64 - u))

                offset = jnp.where(lane < 64, float(u), sideways_by)
                if not last:
                    word = col_words[3 * side + 1]
                    if u < 0:
                        word = jnp.where((lane & 7) + u < 0, col_words[3 * side], word)
                    if u > 0:
                        word = jnp.where((lane & 7) + u > 7, col_words[3 * side + 2], word)
                    intact = intact_of(word, bit_at(lane, lane + u))
                    there = (sub < 6) & (has_right if side else has_left)
                    if u < 0:
                        there = there & ((point_row + u >= 0) | has_up)
                    if u > 0:
                        there = there & ((point_row + u <= 63) | has_down)
                    intact = jnp.where(there, intact, 0.0)
                    rest = (moved(0) - mine[0]) + offset
                    square_of = rest * rest
                    near, far = bonds(intact, square_of + turn(square_of, 64) + DELTA_SQ)
                    col_coef[side, u + 3, 0] = near
                    col_coef[side, u + 3, 1] = far
                else:
                    near, far = col_coef[side, u + 3, 0], col_coef[side, u + 3, 1]
                now = (moved(len(parts) - 1) - mine[-1]) + offset
                square_of = now * now
                factor = far - near * lax.rsqrt(square_of + turn(square_of, 64) + DELTA_SQ)
                total = total + factor * now
            at = 7 - sub if side else sub
            total = jnp.where(has_right if side else has_left, total, 0.0)
            whole.append(
                jnp.where(at < 3, pick(total, jnp.where(at == 0, 0, jnp.where(at == 1, 3, 5)), 0), 0.0)
                + jnp.where(at < 2, pick(total, jnp.where(at == 0, 1, 4), 0), 0.0)
                + jnp.where(at == 0, pick(total, jnp.full((8, 128), 2, jnp.int32), 0), 0.0)
            )
        square[0:8, :] = whole[0]
        square[120:128, :] = whole[1]
        return jnp.transpose(square[...])

    def ice_finish(step, rows_force, columns_force):
        last = step == 1
        for a in range(8):
            rows = pl.ds(8 * a, 8)
            for c in range(2):
                total = force[c, rows, :] + columns_force[64 * c + 8 * a : 64 * c + 8 * a + 8, :]
                if a == 0:
                    total = total + jnp.where(top, rows_force[c], 0.0)
                if a == 7:
                    total = total + jnp.where(top, 0.0, rows_force[c])
                    if c == 0:
                        total = total - push[...]
                speed = vel[c, rows, :] + STEP_DT * total
                moved = disp[c, rows, :] + STEP_DT * speed
                if last:
                    v_out[c, a] = swap_groups(speed)
                    d_out[c, a] = swap_groups(moved)
                else:
                    vel[c, rows, :] = speed
                    disp[c, rows, :] = moved
                    field2[2 + c, 8 + 8 * a : 16 + 8 * a, :] = field1[c, 8 + 8 * a : 16 + 8 * a, :] + moved

    def sideways(x, first, last):
        up = [turn(c, 1) for c in x]
        down = [turn(c, -1) for c in x]
        return [
            jnp.where(lane == 0, up[k - 1] if k else first, up[k])
            + jnp.where(lane == 127, down[k + 1] if k < 3 else last, down[k])
            for k in range(4)
        ]

    def shell_inside(field, put):
        def chunks(ref, start):
            return [ref[k, pl.ds(start, 8), :] for k in range(4)]

        def once(b, carry):
            for h in range(4):
                i = pl.multiple_of(32 * b + 8 * h + 8, 8)
                f, up, down = chunks(field, i), chunks(field, i - 1), chunks(field, i + 1)
                for k, side in enumerate(sideways(f, 0.0, 0.0)):
                    bend1[k, pl.ds(i, 8), :] = (up[k] + down[k]) + side - 4.0 * f[k]
            return carry

        def twice(b, carry):
            for h in range(4):
                base = pl.multiple_of(32 * b + 8 * h, 8)
                i = pl.multiple_of(base + 8, 8)
                f, g = chunks(field, i), chunks(bend1, i)
                up, down = chunks(bend1, i - 1), chunks(bend1, i + 1)
                for k, side in enumerate(sideways(g, f[0], f[3])):
                    at = (pl.ds(base, 8), slice(128 * k, 128 * k + 128))
                    bending = (up[k] + down[k]) + side - 4.0 * g[k]
                    speed = shell_v[at] - (STEP_DT * BEND) * bending
                    shell_v[at] = speed
                    put(base, k, f[k] + STEP_DT * speed)
            return carry

        lax.fori_loop(0, 4, once, 0)
        for k in range(4):
            bend1[k, 7:8, :] = field[k, 8:9, :]
            bend1[k, 136:137, :] = field[k, 135:136, :]
        lax.fori_loop(0, 4, twice, 0)

    def rim_terms(step, side):
        above, level, below = (edge_r1[t, side, 1] if step == 0 else rim_r[t, side] for t in range(3))
        level = jnp.where(lane < 2, jnp.where(has_up, turn(above, -30), 0.0), turn(level, 2))
        rim = jnp.where(lane >= 34, jnp.where(has_down, turn(below, 34), 0.0), level)
        rim = jnp.where(has_right if side else has_left, rim, 0.0)
        first = turn(rim, 1 if side else -1)
        up, down = slide(first, 1), slide(first, -1)
        up = jnp.where(sub == 0, turn(up, 2), up)
        down = jnp.where(sub == 7, turn(down, -2), down)
        full = rim - 8.0 * first + 2.0 * (up + down)
        return jnp.where((lane & 1) == side, full, rim)

    def slab_terms(step):
        terms = []
        for k in range(2):
            slab = rows_r1[k, 2] if step == 0 else slab_r[k]
            slab = jnp.where(has_down if k else has_up, slab, 0.0)
            outer = [slide(slab, (6 if k else 0) - 2 * c) for c in range(4)]
            inner = [slide(slab, (7 if k else -1) - 2 * c) for c in range(4)]
            at = 7 - sub if k else sub
            terms.append(
                [
                    jnp.where(at < 2, o, 0.0) + jnp.where(at == 0, 2.0 * pair - 8.0 * x, 0.0)
                    for o, x, pair in zip(outer, inner, sideways(inner, 0.0, 0.0))
                ]
            )
        return terms

    def shell_finish(step, own, put, get):
        gaps = jnp.broadcast_to(gap_r[step], (8, 128))
        slabs = slab_terms(step)
        rims = [rim_terms(step, side) for side in range(2)]
        totals = []
        for k in range(4):
            gap = pick(gaps, 32 * k + lane // 4, 1)
            load = (STEP_DT * PENALTY) * jnp.maximum(gap - own[k], 0.0)
            total = zero
            for b in range(16):
                here = sub + 8 * b == targets[k]
                change = jnp.where(here, load, 0.0)
                beyond = None
                if b == 0:
                    beyond = slabs[0][k]
                if b == 15:
                    beyond = slabs[1][k]
                if k == 0 or k == 3:
                    rim = turn(rims[k // 3], (124 if k else -2) - 2 * b)
                    rim = jnp.where(lane >= 126 if k else lane < 2, rim, 0.0)
                    beyond = rim if beyond is None else beyond + rim
                if beyond is not None:
                    change = change - (STEP_DT * BEND) * beyond
                at = (pl.ds(8 * b, 8), slice(128 * k, 128 * k + 128))
                shell_v[at] = shell_v[at] + change
                moved = get(8 * b, k) + STEP_DT * change
                put(8 * b, k, moved)
                total = total + jnp.where(here, moved, 0.0)
            totals.append(total)
        return totals

    def put_block(base, k, moved):
        shell2[k, pl.ds(base + 8, 8), :] = moved

    def get_block(base, k):
        return shell2[k, pl.ds(base + 8, 8), :]

    def out_block(base, k, moved):
        s_out[pl.ds(base, 8), 128 * k : 128 * k + 128] = moved

    def out_get(base, k):
        return s_out[pl.ds(base, 8), 128 * k : 128 * k + 128]

    for c in range(2):
        spread_field(field1, c, shift_j.at[c])
        spread_field(field1, 2 + c, shift_p.at[c])
    ice_inside(0, field1)
    later[2].wait()
    shell_inside(shell1, put_block)

    arrived(0, 12, 8)
    columns_force = ice_columns(0, edge_s1, edge_r1)
    rows_force = ice_rows(0, field1, rows_r1)
    end_contact(0)
    ice_finish(0, rows_force, columns_force)
    put_gap(1)
    left, right = edges(field2, 2)
    edge_s2[0, 0] = left
    edge_s2[1, 0] = right
    rows_s2[0, 0], rows_s2[1, 0] = pack_rows(field2, 2)
    send_columns(1, edge_s2, edge_r2)
    send_rows(1, rows_s2, rows_r2)
    start_gap(1)

    totals = shell_finish(0, own, put_block, get_block)
    own, points = gather_points(totals)
    reach_s[1] = points[0:1, :]
    start_reach(1)
    left, right = pack_rim(shell2)
    rim_s[0] = left
    rim_s[1] = right
    slab_s[0], slab_s[1] = pack_slab(shell2)
    send_columns(2, rim_s, rim_r)
    send_rows(2, slab_s, slab_r)

    for c in range(2):
        spread_field(field2, 2 + c, shift_p.at[c])
    ice_inside(1, field2)
    shell_inside(shell2, out_block)

    arrived(1, 4, 4)
    columns_force = ice_columns(1, edge_s2, edge_r2)
    rows_force = ice_rows(1, field2, rows_r2)
    end_contact(1)
    ice_finish(1, rows_force, columns_force)
    arrived(2, 4, 4)
    shell_finish(1, own, out_block, out_get)

    for dx, dy in SIDES:
        with_peer(dx, dy, lambda where: group_wait(16 if dy else 20, dx, dy, 0).wait_send())

    @pl.when(is_front)
    def _():
        slots = reach_r.at[:, 0 : n_x - 1]
        pltpu.make_async_remote_copy(
            slots, slots, con_send.at[0], con_recv.at[0], device_id=(0, gy), device_id_type=MESH
        ).wait_send()

    @pl.when(jnp.logical_not(is_front))
    def _():
        pltpu.make_async_remote_copy(
            gap_r, gap_r, con_send.at[0], con_recv.at[0], device_id=(front, gy), device_id_type=MESH
        ).wait_send()


def write_out(*refs):
    copies = [pltpu.make_async_copy(refs[k], refs[4 + k], refs[8].at[k]) for k in range(4)]
    for copy in copies:
        copy.start()
    for copy in copies:
        copy.wait()


def on_device(n_x, n_y, width, d, v, j, bond, node, inter, shell, speed):
    f32, i32 = jnp.float32, jnp.int32
    vmem = pltpu.VMEM
    dma = pltpu.SemaphoreType.DMA
    shapes = [x.shape for x in (d, v, shell, speed)]
    held = pl.pallas_call(
        functools.partial(kernel, n_x, n_y, width),
        out_shape=[vmem(s, f32) for s in shapes],
        in_specs=[pl.BlockSpec(memory_space=pl.ANY)] * 8,
        out_specs=[pl.BlockSpec(memory_space=vmem)] * 4,
        scratch_shapes=[
            vmem(d.shape, f32), vmem(v.shape, f32), vmem(j.shape, f32), vmem(bond.shape, i32),
            vmem(node.shape, i32), vmem(inter.shape, f32),
            vmem((4, 80, 128), f32), vmem((4, 80, 128), f32), vmem((2, 64, 128), f32), vmem((2, 64, 128), f32),
            vmem((2, 64, 128), f32),
            vmem((2, 7, 80, 128), f32), vmem((2, 7, 80, 128), f32), vmem((9, 64, 128), i32),
            vmem((len(OFFSETS), 2, 64, 128), f32), vmem((len(ROW_OFFSETS), 2, 8, 128), f32),
            vmem((2, 7, 2, 8, 128), f32),
            vmem((2, 3, 8, 128), i32), vmem((4, 144, 128), f32), vmem((4, 144, 128), f32), vmem((4, 144, 128), f32),
            vmem((128, 128), f32),
            vmem((2, 2, 8, 128), f32), vmem((3, 2, 2, 8, 128), f32),
            vmem((2, 1, 8, 128), f32), vmem((3, 2, 1, 8, 128), f32),
            vmem((2, 3, 8, 128), f32), vmem((2, 3, 8, 128), f32), vmem((2, 1, 8, 128), f32), vmem((2, 1, 8, 128), f32),
            vmem((2, 8, 128), f32), vmem((3, 2, 8, 128), f32), vmem((2, 8, 128), f32), vmem((2, 8, 128), f32),
            vmem((8, 128), f32), vmem((2, n_x, 1, 128), f32), vmem((2, 1, 128), f32),
            vmem((2, 1, 128), f32), vmem((2, n_x, 1, 128), f32), vmem((8, 128), f32),
            dma((8,)), dma((3, 3)), dma((3, 3, 3)), dma((1,)), dma((2,)),
        ],
        compiler_params=pltpu.CompilerParams(collective_id=0, has_side_effects=True),
    )(d, v, j, bond, node, inter, shell, speed)
    return pl.pallas_call(
        write_out,
        out_shape=[jax.ShapeDtypeStruct(s, f32) for s in shapes],
        in_specs=[pl.BlockSpec(memory_space=vmem)] * 4,
        out_specs=[pl.BlockSpec(memory_space=pl.ANY)] * 4,
        scratch_shapes=[dma((4,))],
    )(*[pltpu.with_memory_space_constraint(x, vmem) for x in held])


def solution(mesh):
    n_x, n_y = mesh.shape["gx"], mesh.shape["gy"]
    ice, plate = P(None, "gx", "gy", None), P("gx", "gy")

    def step(d, v, j, bond, *rest):
        width = rest[2].shape[1] * n_y
        return on_device(n_x, n_y, width, d, v, j, bond.reshape(-1, bond.shape[2]), *rest)

    return jax.shard_map(
        step,
        mesh=mesh,
        in_specs=(ice, ice, ice, P("gx", "gy", None), P("gy", None), P("gy", None), plate, plate),
        out_specs=(ice, ice, plate, plate),
        check_vma=False,
    )
```

```python
import functools

import jax
import jax.numpy as jnp
from jax import lax
from jax.experimental import pallas as pl
from jax.experimental.pallas import tpu as pltpu
from jax.sharding import PartitionSpec as P

MESH = pl.DeviceIdType.MESH

HORIZON = 3.5
DELTA_SQ = 0.25
PENALTY = 4.0
BEND = 0.5
STEP_DT = 0.2
RUN = 32

OFFSETS = [
    (u, v)
    for u in range(-3, 4)
    for v in range(-3, 4)
    if (u, v) != (0, 0) and max(abs(u) - 0.4, 0) ** 2 + max(abs(v) - 0.4, 0) ** 2 < HORIZON**2 - DELTA_SQ
]
ROW_OFFSETS = [(u, v) for u, v in OFFSETS if u > 0]
SIDES = [(dx, dy) for dx in (-1, 0, 1) for dy in (-1, 0, 1) if (dx, dy) != (0, 0)]


def iota(axis):
    return lax.broadcasted_iota(jnp.int32, (8, 128), axis)


def pick(x, index, axis):
    return jnp.take_along_axis(x, index, axis=axis, mode="promise_in_bounds")


def swap_groups(x):
    sub, group = iota(0), iota(1) // 16
    x = pltpu.roll(x, 0, 1, stride=16, stride_axis=0)
    x = pick(x, (group - sub) & 7, 0)
    return pick(x, ((group + sub) & 7) * 16 + (iota(1) & 15), 1)


def turn(x, shift):
    shift = shift % 128
    return pltpu.roll(x, shift, 1) if shift else x


def slide(x, shift):
    return pltpu.roll(x, shift % 8, 0)


def bonds(intact, square):
    inverse = lax.rsqrt(square)
    reach = jnp.maximum(HORIZON - square * inverse, 0.0)
    near = intact * (reach * reach)
    return near, near * inverse


def intact_of(word, bit):
    return jnp.where((word & bit) != 0, 1.0 / HORIZON**2, 0.0)


def bit_at(row, beyond):
    return jnp.left_shift(1, 4 * (row & 7) + ((beyond & 7) >> 1))


def kernel(
    n_x, n_y, width,
    d_hbm, v_hbm, j_hbm, bond_hbm, node_hbm, inter_hbm, s_hbm, w_hbm,
    d_out, v_out, s_out, shell_v,
    d_in, v_in, j_in, bond, node, inter,
    field1, field2, disp, vel, force, shift_j, shift_p, words, coef, row_coef, col_coef,
    row_words, shell1, shell2, bend1, square,
    edge_s1, edge_r1, edge_s2, edge_r2, rows_s1, rows_r1, rows_s2, rows_r2,
    rim_s, rim_r, slab_s, slab_r, gap_all, gap_s, gap_r, reach_s, reach_r, push,
    in_sem, send_sem, recv_sem, con_send, con_recv,
):
    f32 = jnp.float32
    gx, gy = lax.axis_index("gx"), lax.axis_index("gy")
    front = n_x - 1
    is_front = gx == front
    has_up, has_down, has_left, has_right = gx > 0, gx < n_x - 1, gy > 0, gy < n_y - 1
    sub, lane = iota(0), iota(1)
    zero = jnp.zeros((8, 128), f32)

    across = {-1: has_left, 1: has_right}
    along = {-1: has_up, 1: has_down}

    def with_peer(dx, dy, run):
        there = along[dx] & across[dy] if dx and dy else along[dx] if dx else across[dy]

        @pl.when(there)
        def _():
            run((gx + dx, gy + dy))

    barrier = pltpu.get_barrier_semaphore()

    def greet(where):
        pl.semaphore_signal(barrier, inc=1, device_id=where, device_id_type=MESH)

    for dx, dy in SIDES:
        with_peer(dx, dy, greet)

    @pl.when(is_front)
    def _():
        for i in range(n_x - 2):
            greet((i, gy))

    @pl.when(gx < n_x - 2)
    def _():
        greet((front, gy))

    def load(src, dst, k):
        return pltpu.make_async_copy(src, dst, in_sem.at[k])

    def span(kib):
        return coef.at[0 : kib // 4, 0, 0:8, :]

    first = [load(j_hbm, j_in, 0), load(d_hbm, d_in, 1), load(node_hbm, node, 2), load(inter_hbm, inter, 3)]
    plate = [load(s_hbm.at[:, 128 * k : 128 * k + 128], shell1.at[k, 8:136, :], 4) for k in range(4)]
    later = [load(bond_hbm, bond, 5), load(v_hbm, v_in, 6), load(w_hbm, shell_v, 7)]
    for copy in first + plate + later:
        copy.start()

    for r in (0, 72):
        for c in range(2):
            for v in range(7):
                shift_j[c, v, r : r + 8, :] = zero
                shift_p[c, v, r : r + 8, :] = zero
        for c in range(4):
            field1[c, r : r + 8, :] = zero
            field2[c, r : r + 8, :] = zero
    for field in (shell1, shell2):
        for r in (0, 136):
            for k in range(4):
                field[k, r : r + 8, :] = zero
    for b in range(1, 15):
        square[8 * b : 8 * b + 8, :] = zero

    first[0].wait()
    first[1].wait()
    for a in range(8):
        rows = pl.ds(8 + 8 * a, 8)
        for c in range(2):
            jit = swap_groups(j_in[c, a])
            dis = swap_groups(d_in[c, a])
            field1[c, rows, :] = jit
            field1[2 + c, rows, :] = jit + dis
            disp[c, pl.ds(8 * a, 8), :] = dis

    def edges(field, base):
        stack = jnp.concatenate([field[base, 8:72, :], field[base + 1, 8:72, :]], axis=0)
        across = jnp.transpose(stack)
        return across[0:8, :], across[120:128, :]

    jit_left, jit_right = edges(field1, 0)
    pos_left, pos_right = edges(field1, 2)
    edge_s1[0, 0] = jnp.where(sub < 3, jit_left, slide(pos_left, 3))
    edge_s1[1, 0] = jnp.where(sub > 4, jit_right, slide(pos_right, -3))

    def pack_rows(field, base):
        x, y = field[base, 8:16, :], field[base + 1, 8:16, :]
        first_rows = jnp.where(sub < 3, x, slide(y, 3))
        x, y = field[base, 64:72, :], field[base + 1, 64:72, :]
        return first_rows, jnp.where(sub > 4, x, slide(y, -3))

    for part, base in enumerate((0, 2)):
        rows_s1[0, part], rows_s1[1, part] = pack_rows(field1, base)

    def pack_slab(field):
        ends = []
        for start, at in ((8, 0), (128, 6)):
            total = zero
            for c in range(4):
                total = jnp.where(sub // 2 == c, slide(field[c, start : start + 8, :], 2 * c - at), total)
            ends.append(total)
        return ends

    first[2].wait()
    first[3].wait()
    inter[...] = swap_groups(inter[...])
    node[...] = swap_groups(node[...])

    def put_gap(step):
        gap = disp[0, 56:64, :] + inter[...]
        gap_all[...] = gap
        for i in range(8):
            gap_s[step, i] = gap[i : i + 1, :]

    put_gap(0)

    mine = jnp.broadcast_to(node[pl.ds(gx, 1), :], (8, 128))
    targets = []
    for k in range(4):
        n = pick(mine, 32 * k + lane // 4, 1)
        row = lax.shift_right_logical(n, width.bit_length() - 1) & 127
        targets.append(jnp.where((n & 3) == (lane & 3), row, -1))

    def gather_points(totals):
        own = []
        points = zero
        for k, total in enumerate(totals):
            for s in (4, 2, 1):
                total = total + slide(total, s)
            own.append(total)
            total = total + turn(total, -1)
            total = total + turn(total, -2)
            points = jnp.where(lane // 32 == k, pick(total, (lane & 31) * 4, 1), points)
        return own, points

    def pack_rim(field):
        left = right = zero
        for b in range(16):
            here = lane // 2 == b
            left = jnp.where(here, turn(field[0, 8 + 8 * b : 16 + 8 * b, :], 2 * b), left)
            right = jnp.where(here, turn(field[3, 8 + 8 * b : 16 + 8 * b, :], 2 * b + 2), right)
        return left, right

    load(shell1.at[:, 8:136, :], shell1.at[:, 8:136, :], 4).wait()
    totals = []
    for k in range(4):
        total = zero
        for b in range(16):
            x = shell1[k, 8 + 8 * b : 16 + 8 * b, :]
            total = total + jnp.where(sub + 8 * b == targets[k], x, 0.0)
        totals.append(total)
    own, points = gather_points(totals)
    reach_s[0] = points[0:1, :]
    left, right = pack_rim(shell1)
    edge_s1[0, 1] = left
    edge_s1[1, 1] = right
    rows_s1[0, 2], rows_s1[1, 2] = pack_slab(shell1)

    n_along = has_up.astype(jnp.int32) + has_down.astype(jnp.int32)
    n_across = has_left.astype(jnp.int32) + has_right.astype(jnp.int32)
    extra = jnp.where(is_front, n_x - 2, jnp.where(gx < n_x - 2, 1, 0))
    pl.semaphore_wait(barrier, n_along + n_across + n_along * n_across + extra)

    def send(src, dst, phase, dx, dy):
        with_peer(dx, dy, lambda where: pltpu.make_async_remote_copy(
            src, dst, send_sem.at[1 - dx, 1 - dy], recv_sem.at[phase, 1 - dx, 1 - dy],
            device_id=where, device_id_type=MESH,
        ).start())

    def send_columns(phase, src, dst):
        for dy in (-1, 1):
            side = (dy + 1) // 2
            for dx in (-1, 1, 0):
                send(src.at[side], dst.at[1 - dx, 1 - side], phase, dx, dy)

    def send_rows(phase, src, dst):
        for k, dx in enumerate((-1, 1)):
            send(src.at[k], dst.at[1 - k], phase, dx, 0)

    def group_wait(kib, dx, dy, phase):
        return pltpu.make_async_remote_copy(
            span(kib), span(kib), send_sem.at[1 - dx, 1 - dy], recv_sem.at[phase, 1 + dx, 1 + dy],
            device_id=(0, 0), device_id_type=MESH,
        )

    def rows_arrived(phase, kib):
        for dx in (-1, 1):
            with_peer(dx, 0, lambda where: group_wait(kib, dx, 0, phase).wait_recv())

    def columns_arrived(phase, kib):
        for dy in (-1, 1):
            for dx in (0, -1, 1):
                with_peer(dx, dy, lambda where: group_wait(kib, dx, dy, phase).wait_recv())

    def gap_copy(step, i):
        return pltpu.make_async_remote_copy(
            gap_s.at[step, i], gap_r.at[step], con_send.at[0], con_recv.at[step],
            device_id=(i, gy), device_id_type=MESH,
        )

    def reach_copy(step):
        return pltpu.make_async_remote_copy(
            reach_s.at[step], reach_r.at[step, gx], con_send.at[0], con_recv.at[step],
            device_id=(front, gy), device_id_type=MESH,
        )

    def start_gap(step):
        @pl.when(is_front)
        def _():
            for i in range(n_x - 1):
                gap_copy(step, i).start()
            gap_r[step] = gap_s[step, n_x - 1]

    def start_reach(step):
        @pl.when(is_front)
        def _():
            reach_r[step, front] = reach_s[step]

        @pl.when(jnp.logical_not(is_front))
        def _():
            reach_copy(step).start()

    def end_contact(step):
        @pl.when(is_front)
        def _():
            slots = reach_r.at[step, 0 : n_x - 1]
            pltpu.make_async_remote_copy(
                slots, slots, con_send.at[0], con_recv.at[step], device_id=(0, gy), device_id_type=MESH
            ).wait_recv()
            reached = jnp.broadcast_to(reach_r[step, front], (8, 128))
            for i in range(n_x - 1):
                reached = jnp.where(sub == i, jnp.broadcast_to(reach_r[step, i], (8, 128)), reached)
            push[...] = PENALTY * jnp.maximum(gap_all[...] - reached, 0.0)

        @pl.when(jnp.logical_not(is_front))
        def _():
            gap_copy(step, 0).wait_recv()
            push[...] = jnp.zeros((8, 128), f32)

    send_columns(0, edge_s1, edge_r1)
    send_rows(0, rows_s1, rows_r1)
    start_gap(0)
    start_reach(0)

    later[0].wait()
    none = jnp.zeros((8, 128), jnp.int32)
    for s in range(9):
        for a in range(8):
            word = pick(jnp.broadcast_to(bond[8 * a : 8 * a + 8, s : s + 1], (8, 128)), lane // 16, 0)
            if s % 3 == 0:
                word = jnp.where(lane < 16, 0, word)
            if s % 3 == 2:
                word = jnp.where(lane >= 112, 0, word)
            if a == 0 and s < 3:
                row_words[0, s] = word
                word = none
            if a == 7 and s > 5:
                row_words[1, s - 6] = word
                word = none
            words[s, 8 * a : 8 * a + 8, :] = word
    col_words = []
    for side in range(2):
        tiles = bond[pl.ds(7 * side, 8, stride=8), :]
        for dx in range(3):
            s = 3 * dx + 2 * side
            word = jnp.broadcast_to(tiles[:, s : s + 1], (8, 128))
            col_words.append(pick(word, (lane & 63) // 8, 0))
    later[1].wait()
    for a in range(8):
        for c in range(2):
            vel[c, pl.ds(8 * a, 8), :] = swap_groups(v_in[c, a])

    def spread_field(field, index, out):
        for b in range(1, 9):
            x = field[index, 8 * b : 8 * b + 8, :]
            for v in range(-3, 4):
                if v:
                    out[v + 3, 8 * b : 8 * b + 8, :] = turn(x, -v)

    def ice_inside(step, field):
        last = step == 1
        sub_r = lax.broadcasted_iota(jnp.int32, (RUN, 128), 0)
        lane_r = lax.broadcasted_iota(jnp.int32, (RUN, 128), 1)
        tile_row, tile_col = sub_r & 7, lane_r & 15

        def body(a, carry):
            base = pl.multiple_of(RUN * a, RUN)
            rows = pl.ds(base, RUN)
            own = pl.ds(pl.multiple_of(base + 8, 8), RUN)

            def partner(shifted, c, u, v):
                there = pl.ds(base + (8 + u), RUN)
                if v == 0:
                    return field[(0 if shifted is shift_j else 2) + c, there, :]
                return shifted[c, v + 3, there, :]

            px = field[2, own, :]
            py = [field[3, own, :] - float(v) for v in range(-3, 4)]
            if not last:
                jx = field[0, own, :]
                jy = [field[1, own, :] - float(v) for v in range(-3, 4)]
            fx = fy = jnp.zeros((RUN, 128), f32)
            seen = None
            for n, (u, v) in enumerate(OFFSETS):
                if u != seen:
                    seen = u
                    px_u = px - float(u)
                    if not last:
                        jx_u = jx - float(u)
                        bit = bit_at(tile_row, tile_row + u)
                        flags = []
                        for dy in range(3):
                            word = words[3 + dy, rows, :]
                            if u < 0:
                                word = jnp.where(tile_row + u < 0, words[dy, rows, :], word)
                            if u > 0:
                                word = jnp.where(tile_row + u > 7, words[6 + dy, rows, :], word)
                            flags.append(intact_of(word, bit))
                if not last:
                    intact = flags[1]
                    if v < 0:
                        intact = jnp.where(tile_col + v < 0, flags[0], intact)
                    if v > 0:
                        intact = jnp.where(tile_col + v > 15, flags[2], intact)
                    rx = partner(shift_j, 0, u, v) - jx_u
                    ry = partner(shift_j, 1, u, v) - jy[v + 3]
                    near, far = bonds(intact, rx * rx + ry * ry + DELTA_SQ)
                    coef[n, 0, rows, :] = near
                    coef[n, 1, rows, :] = far
                else:
                    near = coef[n, 0, rows, :]
                    far = coef[n, 1, rows, :]
                nx = partner(shift_p, 0, u, v) - px_u
                ny = partner(shift_p, 1, u, v) - py[v + 3]
                factor = far - near * lax.rsqrt(nx * nx + ny * ny + DELTA_SQ)
                fx = fx + factor * nx
                fy = fy + factor * ny
            force[0, rows, :] = fx
            force[1, rows, :] = fy
            return carry

        lax.fori_loop(0, 64 // RUN, body, 0)

    top = sub < 4

    def row_flags():
        word = [jnp.where(top, row_words[0, dy], row_words[1, dy]) for dy in range(3)]
        seen = None
        for n, (u, v) in enumerate(ROW_OFFSETS):
            if u != seen:
                seen = u
                inside = ((sub < u) & has_up) | ((sub >= 8 - u) & has_down)
                bit = bit_at(sub, sub + jnp.where(top, -u, u))
                flags = [jnp.where(inside, intact_of(w, bit), 0.0) for w in word]
            intact = flags[1]
            if v < 0:
                intact = jnp.where((lane & 15) + v < 0, flags[0], intact)
            if v > 0:
                intact = jnp.where((lane & 15) + v > 15, flags[2], intact)
            row_coef[n, 0] = intact

    def ice_rows(step, field, rows_r):
        last = step == 1
        base = 2 if last else 0
        mine = [jnp.where(top, field[c, 8:16, :], field[c, 64:72, :]) for c in range(base, 4)]
        mine_y = [[mine[c] - float(v) for v in range(-3, 4)] for c in range(1, 4 - base, 2)]
        fx = fy = zero
        seen = None
        for n, (u, v) in enumerate(ROW_OFFSETS):
            if u != seen:
                seen = u
                beyond = [
                    jnp.where(top, slide(rows_r[0, c // 2], u + 3 * (c % 2)), slide(rows_r[1, c // 2], -u - 3 * (c % 2)))
                    for c in range(4 - base)
                ]
                by = jnp.where(top, -float(u), float(u))
                mine_x = [mine[c] - by for c in range(0, 4 - base, 2)]
            near = row_coef[n, 0]
            if not last:
                rx = turn(beyond[0], -v) - mine_x[0]
                ry = turn(beyond[1], -v) - mine_y[0][v + 3]
                near, far = bonds(near, rx * rx + ry * ry + DELTA_SQ)
                row_coef[n, 0] = near
                row_coef[n, 1] = far
            else:
                far = row_coef[n, 1]
            nx = turn(beyond[2 - base], -v) - mine_x[-1]
            ny = turn(beyond[3 - base], -v) - mine_y[-1][v + 3]
            factor = far - near * lax.rsqrt(nx * nx + ny * ny + DELTA_SQ)
            fx = fx + factor * nx
            fy = fy + factor * ny
        present = (top & has_up) | (jnp.logical_not(top) & has_down)
        return jnp.where(present, fx, 0.0), jnp.where(present, fy, 0.0)

    near_col = jnp.where(sub < 3, 0, jnp.where(sub < 5, 1, 2))
    far_col = jnp.where(sub < 3, sub + 1, jnp.where(sub < 5, sub - 2, 1))
    point_row = lane & 63

    def column_flags():
        for side in range(2):
            there = (sub < 6) & (has_right if side else has_left)
            for u in range(-3, 4):
                word = col_words[3 * side + 1]
                present = there
                if u < 0:
                    word = jnp.where((lane & 7) + u < 0, col_words[3 * side], word)
                    present = there & ((point_row + u >= 0) | has_up)
                if u > 0:
                    word = jnp.where((lane & 7) + u > 7, col_words[3 * side + 2], word)
                    present = there & ((point_row + u <= 63) | has_down)
                col_coef[side, u + 3, 0] = jnp.where(present, intact_of(word, bit_at(lane, lane + u)), 0.0)

    def ice_columns(step, edge_s, edge_r):
        last = step == 1
        parts = (0,) if last else (0, 1)
        for side in range(2):
            mine_at = 7 - near_col if side else near_col
            beyond_at = far_col - 1 if side else 8 - far_col
            shifts = [3 * p for p in parts]
            by = jnp.where(lane < 64, 0.0, (near_col + far_col).astype(f32) * (1.0 if side else -1.0))
            mine = [pick(edge_s[side, 0], mine_at - h if side else mine_at + h, 0) - by for h in shifts]
            beyond = [
                [pick(edge_r[slot, side, 0], beyond_at + h if side else beyond_at - h, 0) for slot in range(3)]
                for h in shifts
            ]
            total = zero
            for u in range(-3, 4):
                def moved(p):
                    if u == 0:
                        return beyond[p][1]
                    inside = (point_row + u >= 0) | jnp.logical_not(has_up)
                    if u > 0:
                        inside = (point_row + u <= 63) | jnp.logical_not(has_down)
                    return jnp.where(inside, turn(beyond[p][1], -u), turn(beyond[p][0 if u < 0 else 2], 64 - u))

                offset = jnp.where(lane < 64, float(u), 0.0)
                near = col_coef[side, u + 3, 0]
                if not last:
                    rest = moved(0) - (mine[0] - offset)
                    square_of = rest * rest
                    near, far = bonds(near, square_of + turn(square_of, 64) + DELTA_SQ)
                    col_coef[side, u + 3, 0] = near
                    col_coef[side, u + 3, 1] = far
                else:
                    far = col_coef[side, u + 3, 1]
                now = moved(len(parts) - 1) - (mine[-1] - offset)
                square_of = now * now
                factor = far - near * lax.rsqrt(square_of + turn(square_of, 64) + DELTA_SQ)
                total = total + factor * now
            at = 7 - sub if side else sub
            total = jnp.where(has_right if side else has_left, total, 0.0)
            square[120 * side : 120 * side + 8, :] = (
                jnp.where(at < 3, pick(total, jnp.where(at == 0, 0, jnp.where(at == 1, 3, 5)), 0), 0.0)
                + jnp.where(at < 2, pick(total, jnp.where(at == 0, 1, 4), 0), 0.0)
                + jnp.where(at == 0, pick(total, jnp.full((8, 128), 2, jnp.int32), 0), 0.0)
            )
        return jnp.transpose(square[...])

    def ice_finish(step, rows_force, columns_force):
        last = step == 1
        for a in range(8):
            rows = pl.ds(8 * a, 8)
            for c in range(2):
                total = force[c, rows, :] + columns_force[64 * c + 8 * a : 64 * c + 8 * a + 8, :]
                if a == 0:
                    total = total + jnp.where(top, rows_force[c], 0.0)
                if a == 7:
                    total = total + jnp.where(top, 0.0, rows_force[c])
                    if c == 0:
                        total = total - push[...]
                speed = vel[c, rows, :] + STEP_DT * total
                moved = disp[c, rows, :] + STEP_DT * speed
                if last:
                    v_out[c, a] = swap_groups(speed)
                    d_out[c, a] = swap_groups(moved)
                else:
                    vel[c, rows, :] = speed
                    disp[c, rows, :] = moved
                    field2[2 + c, 8 + 8 * a : 16 + 8 * a, :] = field1[c, 8 + 8 * a : 16 + 8 * a, :] + moved

    def sideways(x, first, last):
        up = [turn(c, 1) for c in x]
        down = [turn(c, -1) for c in x]
        return [
            jnp.where(lane == 0, up[k - 1] if k else first, up[k])
            + jnp.where(lane == 127, down[k + 1] if k < 3 else last, down[k])
            for k in range(4)
        ]

    def shell_inside(field, put):
        def chunks(ref, start):
            return [ref[k, pl.ds(start, 8), :] for k in range(4)]

        def once(b, carry):
            for h in range(4):
                i = pl.multiple_of(32 * b + 8 * h + 8, 8)
                f, up, down = chunks(field, i), chunks(field, i - 1), chunks(field, i + 1)
                for k, side in enumerate(sideways(f, 0.0, 0.0)):
                    bend1[k, pl.ds(i, 8), :] = (up[k] + down[k]) + side - 4.0 * f[k]
            return carry

        def twice(b, carry):
            for h in range(4):
                base = pl.multiple_of(32 * b + 8 * h, 8)
                i = pl.multiple_of(base + 8, 8)
                f, g = chunks(field, i), chunks(bend1, i)
                up, down = chunks(bend1, i - 1), chunks(bend1, i + 1)
                for k, side in enumerate(sideways(g, f[0], f[3])):
                    at = (pl.ds(base, 8), slice(128 * k, 128 * k + 128))
                    bending = (up[k] + down[k]) + side - 4.0 * g[k]
                    speed = shell_v[at] - (STEP_DT * BEND) * bending
                    shell_v[at] = speed
                    put(base, k, f[k] + STEP_DT * speed)
            return carry

        lax.fori_loop(0, 4, once, 0)
        for k in range(4):
            bend1[k, 7:8, :] = field[k, 8:9, :]
            bend1[k, 136:137, :] = field[k, 135:136, :]
        lax.fori_loop(0, 4, twice, 0)

    def rim_terms(step, side):
        above, level, below = (edge_r1[t, side, 1] if step == 0 else rim_r[t, side] for t in range(3))
        level = jnp.where(lane < 2, jnp.where(has_up, turn(above, -30), 0.0), turn(level, 2))
        rim = jnp.where(lane >= 34, jnp.where(has_down, turn(below, 34), 0.0), level)
        rim = jnp.where(has_right if side else has_left, rim, 0.0)
        first = turn(rim, 1 if side else -1)
        up, down = slide(first, 1), slide(first, -1)
        up = jnp.where(sub == 0, turn(up, 2), up)
        down = jnp.where(sub == 7, turn(down, -2), down)
        full = rim - 8.0 * first + 2.0 * (up + down)
        return jnp.where((lane & 1) == side, full, rim)

    def slab_terms(step):
        terms = []
        for k in range(2):
            slab = rows_r1[k, 2] if step == 0 else slab_r[k]
            slab = jnp.where(has_down if k else has_up, slab, 0.0)
            outer = [slide(slab, (6 if k else 0) - 2 * c) for c in range(4)]
            inner = [slide(slab, (7 if k else -1) - 2 * c) for c in range(4)]
            at = 7 - sub if k else sub
            terms.append(
                [
                    jnp.where(at < 2, o, 0.0) + jnp.where(at == 0, 2.0 * pair - 8.0 * x, 0.0)
                    for o, x, pair in zip(outer, inner, sideways(inner, 0.0, 0.0))
                ]
            )
        return terms

    outer_blocks = [(k, b) for k in range(4) for b in range(16) if k in (0, 3) or b in (0, 15)]
    inner_blocks = [(k, b) for k in (1, 2) for b in range(1, 15)]

    def loads_of(step, own):
        gaps = jnp.broadcast_to(gap_r[step], (8, 128))
        return [
            (STEP_DT * PENALTY) * jnp.maximum(pick(gaps, 32 * k + lane // 4, 1) - own[k], 0.0) for k in range(4)
        ]

    def rim_changes(step):
        slabs = slab_terms(step)
        rims = [rim_terms(step, side) for side in range(2)]
        changes = {}
        for k, b in outer_blocks:
            beyond = slabs[b // 15][k] if b in (0, 15) else None
            if k in (0, 3):
                rim = turn(rims[k // 3], (124 if k else -2) - 2 * b)
                rim = jnp.where(lane >= 126 if k else lane < 2, rim, 0.0)
                beyond = rim if beyond is None else beyond + rim
            changes[k, b] = (-STEP_DT * BEND) * beyond
        return changes

    def shell_change(blocks, load, changes, put, get, totals):
        for k, b in blocks:
            here = sub + 8 * b == targets[k]
            change = None if load is None else jnp.where(here, load[k], 0.0)
            if changes is not None:
                change = changes[k, b] if change is None else change + changes[k, b]
            at = (pl.ds(8 * b, 8), slice(128 * k, 128 * k + 128))
            shell_v[at] = shell_v[at] + change
            moved = get(8 * b, k) + STEP_DT * change
            put(8 * b, k, moved)
            if totals is not None:
                totals[k] = totals[k] + jnp.where(here, moved, 0.0)

    def put_block(base, k, moved):
        shell2[k, pl.ds(base + 8, 8), :] = moved

    def get_block(base, k):
        return shell2[k, pl.ds(base + 8, 8), :]

    def out_block(base, k, moved):
        s_out[pl.ds(base, 8), 128 * k : 128 * k + 128] = moved

    def out_get(base, k):
        return s_out[pl.ds(base, 8), 128 * k : 128 * k + 128]

    row_flags()
    column_flags()
    for c in range(2):
        spread_field(field1, c, shift_j.at[c])
        spread_field(field1, 2 + c, shift_p.at[c])
    ice_inside(0, field1)
    later[2].wait()
    shell_inside(shell1, put_block)

    rows_arrived(0, 12)
    rows_force = ice_rows(0, field1, rows_r1)
    columns_arrived(0, 8)
    columns_force = ice_columns(0, edge_s1, edge_r1)
    end_contact(0)
    ice_finish(0, rows_force, columns_force)
    put_gap(1)
    left, right = edges(field2, 2)
    edge_s2[0, 0] = left
    edge_s2[1, 0] = right
    rows_s2[0, 0], rows_s2[1, 0] = pack_rows(field2, 2)
    send_columns(1, edge_s2, edge_r2)
    send_rows(1, rows_s2, rows_r2)
    start_gap(1)

    load = loads_of(0, own)
    totals = [zero] * 4
    shell_change(outer_blocks, load, rim_changes(0), put_block, get_block, totals)
    left, right = pack_rim(shell2)
    rim_s[0] = left
    rim_s[1] = right
    slab_s[0], slab_s[1] = pack_slab(shell2)
    send_columns(2, rim_s, rim_r)
    send_rows(2, slab_s, slab_r)
    shell_change(inner_blocks, load, None, put_block, get_block, totals)
    own, points = gather_points(totals)
    reach_s[1] = points[0:1, :]
    start_reach(1)

    for c in range(2):
        spread_field(field2, 2 + c, shift_p.at[c])
    ice_inside(1, field2)
    shell_inside(shell2, out_block)

    rows_arrived(1, 4)
    rows_force = ice_rows(1, field2, rows_r2)
    end_contact(1)
    shell_change(outer_blocks + inner_blocks, loads_of(1, own), None, out_block, out_get, None)
    columns_arrived(1, 4)
    columns_force = ice_columns(1, edge_s2, edge_r2)
    ice_finish(1, rows_force, columns_force)
    rows_arrived(2, 4)
    columns_arrived(2, 4)
    shell_change(outer_blocks, None, rim_changes(1), out_block, out_get, None)

    for dx, dy in SIDES:
        with_peer(dx, dy, lambda where: group_wait(16 if dy else 20, dx, dy, 0).wait_send())

    @pl.when(is_front)
    def _():
        slots = reach_r.at[:, 0 : n_x - 1]
        pltpu.make_async_remote_copy(
            slots, slots, con_send.at[0], con_recv.at[0], device_id=(0, gy), device_id_type=MESH
        ).wait_send()

    @pl.when(jnp.logical_not(is_front))
    def _():
        pltpu.make_async_remote_copy(
            gap_r, gap_r, con_send.at[0], con_recv.at[0], device_id=(front, gy), device_id_type=MESH
        ).wait_send()


def write_out(*refs):
    copies = [pltpu.make_async_copy(refs[k], refs[4 + k], refs[8].at[k]) for k in range(4)]
    for copy in copies:
        copy.start()
    for copy in copies:
        copy.wait()


def on_device(n_x, n_y, width, d, v, j, bond, node, inter, shell, speed):
    f32, i32 = jnp.float32, jnp.int32
    vmem = pltpu.VMEM
    dma = pltpu.SemaphoreType.DMA
    shapes = [x.shape for x in (d, v, shell, speed)]
    held = pl.pallas_call(
        functools.partial(kernel, n_x, n_y, width),
        out_shape=[vmem(s, f32) for s in shapes],
        in_specs=[pl.BlockSpec(memory_space=pl.ANY)] * 8,
        out_specs=[pl.BlockSpec(memory_space=vmem)] * 4,
        scratch_shapes=[
            vmem(d.shape, f32), vmem(v.shape, f32), vmem(j.shape, f32), vmem(bond.shape, i32),
            vmem(node.shape, i32), vmem(inter.shape, f32),
            vmem((4, 80, 128), f32), vmem((4, 80, 128), f32), vmem((2, 64, 128), f32), vmem((2, 64, 128), f32),
            vmem((2, 64, 128), f32),
            vmem((2, 7, 80, 128), f32), vmem((2, 7, 80, 128), f32), vmem((9, 64, 128), i32),
            vmem((len(OFFSETS), 2, 64, 128), f32), vmem((len(ROW_OFFSETS), 2, 8, 128), f32),
            vmem((2, 7, 2, 8, 128), f32),
            vmem((2, 3, 8, 128), i32), vmem((4, 144, 128), f32), vmem((4, 144, 128), f32), vmem((4, 144, 128), f32),
            vmem((128, 128), f32),
            vmem((2, 2, 8, 128), f32), vmem((3, 2, 2, 8, 128), f32),
            vmem((2, 1, 8, 128), f32), vmem((3, 2, 1, 8, 128), f32),
            vmem((2, 3, 8, 128), f32), vmem((2, 3, 8, 128), f32), vmem((2, 1, 8, 128), f32), vmem((2, 1, 8, 128), f32),
            vmem((2, 8, 128), f32), vmem((3, 2, 8, 128), f32), vmem((2, 8, 128), f32), vmem((2, 8, 128), f32),
            vmem((8, 128), f32), vmem((2, n_x, 1, 128), f32), vmem((2, 1, 128), f32),
            vmem((2, 1, 128), f32), vmem((2, n_x, 1, 128), f32), vmem((8, 128), f32),
            dma((8,)), dma((3, 3)), dma((3, 3, 3)), dma((1,)), dma((2,)),
        ],
        compiler_params=pltpu.CompilerParams(collective_id=0, has_side_effects=True),
    )(d, v, j, bond, node, inter, shell, speed)
    return pl.pallas_call(
        write_out,
        out_shape=[jax.ShapeDtypeStruct(s, f32) for s in shapes],
        in_specs=[pl.BlockSpec(memory_space=vmem)] * 4,
        out_specs=[pl.BlockSpec(memory_space=pl.ANY)] * 4,
        scratch_shapes=[dma((4,))],
    )(*[pltpu.with_memory_space_constraint(x, vmem) for x in held])


def solution(mesh):
    n_x, n_y = mesh.shape["gx"], mesh.shape["gy"]
    ice, plate = P(None, "gx", "gy", None), P("gx", "gy")

    def step(d, v, j, bond, *rest):
        width = rest[2].shape[1] * n_y
        return on_device(n_x, n_y, width, d, v, j, bond.reshape(-1, bond.shape[2]), *rest)

    return jax.shard_map(
        step,
        mesh=mesh,
        in_specs=(ice, ice, ice, P("gx", "gy", None), P("gy", None), P("gy", None), plate, plate),
        out_specs=(ice, ice, plate, plate),
        check_vma=False,
    )
```

```python
import functools

import jax
import jax.numpy as jnp
from jax import lax
from jax.experimental import pallas as pl
from jax.experimental.pallas import tpu as pltpu
from jax.sharding import PartitionSpec as P

MESH = pl.DeviceIdType.MESH

HORIZON = 3.5
DELTA_SQ = 0.25
PENALTY = 4.0
BEND = 0.5
STEP_DT = 0.2
RUN = 32

OFFSETS = [
    (u, v)
    for u in range(-3, 4)
    for v in range(-3, 4)
    if (u, v) != (0, 0) and max(abs(u) - 0.4, 0) ** 2 + max(abs(v) - 0.4, 0) ** 2 < HORIZON**2 - DELTA_SQ
]
ROW_OFFSETS = [(u, v) for u, v in OFFSETS if u > 0]
SIDES = [(dx, dy) for dx in (-1, 0, 1) for dy in (-1, 0, 1) if (dx, dy) != (0, 0)]


def iota(axis):
    return lax.broadcasted_iota(jnp.int32, (8, 128), axis)


def pick(x, index, axis):
    return jnp.take_along_axis(x, index, axis=axis, mode="promise_in_bounds")


def swap_groups(x):
    sub, group = iota(0), iota(1) // 16
    x = pltpu.roll(x, 0, 1, stride=16, stride_axis=0)
    x = pick(x, (group - sub) & 7, 0)
    return pick(x, ((group + sub) & 7) * 16 + (iota(1) & 15), 1)


def turn(x, shift):
    shift = shift % 128
    return pltpu.roll(x, shift, 1) if shift else x


def slide(x, shift):
    return pltpu.roll(x, shift % 8, 0)


def bonds(intact, square):
    inverse = lax.rsqrt(square)
    reach = jnp.maximum(HORIZON - square * inverse, 0.0)
    near = intact * (reach * reach)
    return near, near * inverse


def intact_of(word, bit):
    return jnp.where((word & bit) != 0, 1.0 / HORIZON**2, 0.0)


def bit_at(row, beyond):
    return jnp.left_shift(1, 4 * (row & 7) + ((beyond & 7) >> 1))


def kernel(
    n_x, n_y, width,
    d_hbm, v_hbm, j_hbm, bond_hbm, node_hbm, inter_hbm, s_hbm, w_hbm,
    d_out, v_out, s_out, shell_v,
    d_in, v_in, j_in, bond, node, inter,
    field1, field2, disp, vel, force, shift_j, shift_p, words, coef, row_coef, col_coef,
    row_words, shell1, shell2, bend1, square,
    edge_s1, edge_r1, edge_s2, edge_r2, rows_s1, rows_r1, rows_s2, rows_r2,
    gap_all, gap_s, gap_r, reach_s, reach_r, push,
    in_sem, send_sem, recv_sem, con_send, con_recv,
):
    f32 = jnp.float32
    gx, gy = lax.axis_index("gx"), lax.axis_index("gy")
    front = n_x - 1
    is_front = gx == front
    has_up, has_down, has_left, has_right = gx > 0, gx < n_x - 1, gy > 0, gy < n_y - 1
    sub, lane = iota(0), iota(1)
    zero = jnp.zeros((8, 128), f32)

    across = {-1: has_left, 1: has_right}
    along = {-1: has_up, 1: has_down}

    def with_peer(dx, dy, run):
        there = along[dx] & across[dy] if dx and dy else along[dx] if dx else across[dy]

        @pl.when(there)
        def _():
            run((gx + dx, gy + dy))

    barrier = pltpu.get_barrier_semaphore()

    def greet(where):
        pl.semaphore_signal(barrier, inc=1, device_id=where, device_id_type=MESH)

    for dx, dy in SIDES:
        with_peer(dx, dy, greet)

    @pl.when(is_front)
    def _():
        for i in range(n_x - 2):
            greet((i, gy))

    @pl.when(gx < n_x - 2)
    def _():
        greet((front, gy))

    def load(src, dst, k):
        return pltpu.make_async_copy(src, dst, in_sem.at[k])

    def span(kib):
        return coef.at[0 : kib // 4, 0, 0:8, :]

    first = [load(j_hbm, j_in, 0), load(d_hbm, d_in, 1), load(node_hbm, node, 2), load(inter_hbm, inter, 3)]
    plate = [load(s_hbm.at[:, 128 * k : 128 * k + 128], shell1.at[k, 8:136, :], 4) for k in range(4)]
    later = [load(bond_hbm, bond, 5), load(v_hbm, v_in, 6), load(w_hbm, shell_v, 7)]
    for copy in first + plate + later:
        copy.start()

    for r in (0, 72):
        for c in range(2):
            for v in range(7):
                shift_j[c, v, r : r + 8, :] = zero
                shift_p[c, v, r : r + 8, :] = zero
        for c in range(4):
            field1[c, r : r + 8, :] = zero
            field2[c, r : r + 8, :] = zero
    for field in (shell1, shell2):
        for r in (0, 136):
            for k in range(4):
                field[k, r : r + 8, :] = zero
    for b in range(1, 15):
        square[8 * b : 8 * b + 8, :] = zero

    first[0].wait()
    first[1].wait()
    for a in range(8):
        rows = pl.ds(8 + 8 * a, 8)
        for c in range(2):
            jit = swap_groups(j_in[c, a])
            dis = swap_groups(d_in[c, a])
            field1[c, rows, :] = jit
            field1[2 + c, rows, :] = jit + dis
            disp[c, pl.ds(8 * a, 8), :] = dis

    def edges(field, base):
        stack = jnp.concatenate([field[base, 8:72, :], field[base + 1, 8:72, :]], axis=0)
        across = jnp.transpose(stack)
        return across[0:8, :], across[120:128, :]

    jit_left, jit_right = edges(field1, 0)
    pos_left, pos_right = edges(field1, 2)
    edge_s1[0, 0] = jnp.where(sub < 3, jit_left, slide(pos_left, 3))
    edge_s1[1, 0] = jnp.where(sub > 4, jit_right, slide(pos_right, -3))

    def pack_rows(field, base):
        x, y = field[base, 8:16, :], field[base + 1, 8:16, :]
        first_rows = jnp.where(sub < 3, x, slide(y, 3))
        x, y = field[base, 64:72, :], field[base + 1, 64:72, :]
        return first_rows, jnp.where(sub > 4, x, slide(y, -3))

    for part, base in enumerate((0, 2)):
        rows_s1[0, part], rows_s1[1, part] = pack_rows(field1, base)

    def pack_slab(field):
        ends = []
        for start, at in ((8, 0), (128, 6)):
            total = zero
            for c in range(4):
                total = jnp.where(sub // 2 == c, slide(field[c, start : start + 8, :], 2 * c - at), total)
            ends.append(total)
        return ends

    first[2].wait()
    first[3].wait()
    inter[...] = swap_groups(inter[...])
    node[...] = swap_groups(node[...])

    def put_gap(step):
        gap = disp[0, 56:64, :] + inter[...]
        gap_all[...] = gap
        for i in range(8):
            gap_s[step, i] = gap[i : i + 1, :]

    put_gap(0)

    mine = jnp.broadcast_to(node[pl.ds(gx, 1), :], (8, 128))
    targets = []
    for k in range(4):
        n = pick(mine, 32 * k + lane // 4, 1)
        row = lax.shift_right_logical(n, width.bit_length() - 1) & 127
        targets.append(jnp.where((n & 3) == (lane & 3), row, -1))

    def gather_points(totals):
        own = []
        points = zero
        for k, total in enumerate(totals):
            for s in (4, 2, 1):
                total = total + slide(total, s)
            own.append(total)
            total = total + turn(total, -1)
            total = total + turn(total, -2)
            points = jnp.where(lane // 32 == k, pick(total, (lane & 31) * 4, 1), points)
        return own, points

    def touched(field):
        totals = []
        for k in range(4):
            total = zero
            for b in range(16):
                x = field[k, 8 + 8 * b : 16 + 8 * b, :]
                total = total + jnp.where(sub + 8 * b == targets[k], x, 0.0)
            totals.append(total)
        return totals

    def pack_rim(field):
        left = right = zero
        for b in range(16):
            here = lane // 2 == b
            left = jnp.where(here, turn(field[0, 8 + 8 * b : 16 + 8 * b, :], 2 * b), left)
            right = jnp.where(here, turn(field[3, 8 + 8 * b : 16 + 8 * b, :], 2 * b + 2), right)
        return left, right

    load(shell1.at[:, 8:136, :], shell1.at[:, 8:136, :], 4).wait()
    own, points = gather_points(touched(shell1))
    reach_s[0] = points[0:1, :]
    left, right = pack_rim(shell1)
    edge_s1[0, 1] = left
    edge_s1[1, 1] = right
    rows_s1[0, 2], rows_s1[1, 2] = pack_slab(shell1)

    n_along = has_up.astype(jnp.int32) + has_down.astype(jnp.int32)
    n_across = has_left.astype(jnp.int32) + has_right.astype(jnp.int32)
    extra = jnp.where(is_front, n_x - 2, jnp.where(gx < n_x - 2, 1, 0))
    pl.semaphore_wait(barrier, n_along + n_across + n_along * n_across + extra)

    def send(src, dst, phase, dx, dy):
        with_peer(dx, dy, lambda where: pltpu.make_async_remote_copy(
            src, dst, send_sem.at[1 - dx, 1 - dy], recv_sem.at[phase, 1 - dx, 1 - dy],
            device_id=where, device_id_type=MESH,
        ).start())

    def send_columns(phase, src, dst):
        for dx in (-1, 1, 0):
            for dy in (-1, 1):
                side = (dy + 1) // 2
                send(src.at[side], dst.at[1 - dx, 1 - side], phase, dx, dy)

    def send_rows(phase, src, dst):
        for k, dx in enumerate((-1, 1)):
            send(src.at[k], dst.at[1 - k], phase, dx, 0)

    def group_wait(kib, dx, dy, phase):
        return pltpu.make_async_remote_copy(
            span(kib), span(kib), send_sem.at[1 - dx, 1 - dy], recv_sem.at[phase, 1 + dx, 1 + dy],
            device_id=(0, 0), device_id_type=MESH,
        )

    def rows_arrived(phase, kib):
        for dx in (-1, 1):
            with_peer(dx, 0, lambda where: group_wait(kib, dx, 0, phase).wait_recv())

    def columns_arrived(phase, kib):
        for dy in (-1, 1):
            for dx in (0, -1, 1):
                with_peer(dx, dy, lambda where: group_wait(kib, dx, dy, phase).wait_recv())

    def gap_copy(step, i):
        return pltpu.make_async_remote_copy(
            gap_s.at[step, i], gap_r.at[step], con_send.at[0], con_recv.at[step],
            device_id=(i, gy), device_id_type=MESH,
        )

    def reach_copy(step):
        return pltpu.make_async_remote_copy(
            reach_s.at[step], reach_r.at[step, gx], con_send.at[0], con_recv.at[step],
            device_id=(front, gy), device_id_type=MESH,
        )

    def start_gap(step):
        @pl.when(is_front)
        def _():
            for i in range(n_x - 1):
                gap_copy(step, i).start()
            gap_r[step] = gap_s[step, n_x - 1]

    def start_reach(step):
        @pl.when(is_front)
        def _():
            reach_r[step, front] = reach_s[step]

        @pl.when(jnp.logical_not(is_front))
        def _():
            reach_copy(step).start()

    def end_contact(step):
        @pl.when(is_front)
        def _():
            slots = reach_r.at[step, 0 : n_x - 1]
            pltpu.make_async_remote_copy(
                slots, slots, con_send.at[0], con_recv.at[step], device_id=(0, gy), device_id_type=MESH
            ).wait_recv()
            reached = jnp.broadcast_to(reach_r[step, front], (8, 128))
            for i in range(n_x - 1):
                reached = jnp.where(sub == i, jnp.broadcast_to(reach_r[step, i], (8, 128)), reached)
            push[...] = PENALTY * jnp.maximum(gap_all[...] - reached, 0.0)

        @pl.when(jnp.logical_not(is_front))
        def _():
            gap_copy(step, 0).wait_recv()
            push[...] = jnp.zeros((8, 128), f32)

    send_columns(0, edge_s1, edge_r1)
    send_rows(0, rows_s1, rows_r1)
    start_gap(0)
    start_reach(0)

    later[0].wait()
    none = jnp.zeros((8, 128), jnp.int32)
    for s in range(9):
        for a in range(8):
            word = pick(jnp.broadcast_to(bond[8 * a : 8 * a + 8, s : s + 1], (8, 128)), lane // 16, 0)
            if s % 3 == 0:
                word = jnp.where(lane < 16, 0, word)
            if s % 3 == 2:
                word = jnp.where(lane >= 112, 0, word)
            if a == 0 and s < 3:
                row_words[0, s] = word
                word = none
            if a == 7 and s > 5:
                row_words[1, s - 6] = word
                word = none
            words[s, 8 * a : 8 * a + 8, :] = word
    col_words = []
    for side in range(2):
        tiles = bond[pl.ds(7 * side, 8, stride=8), :]
        for dx in range(3):
            s = 3 * dx + 2 * side
            word = jnp.broadcast_to(tiles[:, s : s + 1], (8, 128))
            col_words.append(pick(word, (lane & 63) // 8, 0))
    later[1].wait()
    for a in range(8):
        for c in range(2):
            vel[c, pl.ds(8 * a, 8), :] = swap_groups(v_in[c, a])

    def spread_field(field, index, out):
        for b in range(1, 9):
            x = field[index, 8 * b : 8 * b + 8, :]
            for v in range(-3, 4):
                if v:
                    out[v + 3, 8 * b : 8 * b + 8, :] = turn(x, -v)

    def ice_inside(step, field):
        last = step == 1
        sub_r = lax.broadcasted_iota(jnp.int32, (RUN, 128), 0)
        lane_r = lax.broadcasted_iota(jnp.int32, (RUN, 128), 1)
        tile_row, tile_col = sub_r & 7, lane_r & 15

        def body(a, carry):
            base = pl.multiple_of(RUN * a, RUN)
            rows = pl.ds(base, RUN)
            own = pl.ds(pl.multiple_of(base + 8, 8), RUN)

            def partner(shifted, c, u, v):
                there = pl.ds(base + (8 + u), RUN)
                if v == 0:
                    return field[(0 if shifted is shift_j else 2) + c, there, :]
                return shifted[c, v + 3, there, :]

            px = field[2, own, :]
            py = [field[3, own, :] - float(v) for v in range(-3, 4)]
            if not last:
                jx = field[0, own, :]
                jy = [field[1, own, :] - float(v) for v in range(-3, 4)]
            fx = fy = jnp.zeros((RUN, 128), f32)
            seen = None
            for n, (u, v) in enumerate(OFFSETS):
                if u != seen:
                    seen = u
                    px_u = px - float(u)
                    if not last:
                        jx_u = jx - float(u)
                        bit = bit_at(tile_row, tile_row + u)
                        flags = []
                        for dy in range(3):
                            word = words[3 + dy, rows, :]
                            if u < 0:
                                word = jnp.where(tile_row + u < 0, words[dy, rows, :], word)
                            if u > 0:
                                word = jnp.where(tile_row + u > 7, words[6 + dy, rows, :], word)
                            flags.append(intact_of(word, bit))
                if not last:
                    intact = flags[1]
                    if v < 0:
                        intact = jnp.where(tile_col + v < 0, flags[0], intact)
                    if v > 0:
                        intact = jnp.where(tile_col + v > 15, flags[2], intact)
                    rx = partner(shift_j, 0, u, v) - jx_u
                    ry = partner(shift_j, 1, u, v) - jy[v + 3]
                    near, far = bonds(intact, rx * rx + ry * ry + DELTA_SQ)
                    coef[n, 0, rows, :] = near
                    coef[n, 1, rows, :] = far
                else:
                    near = coef[n, 0, rows, :]
                    far = coef[n, 1, rows, :]
                nx = partner(shift_p, 0, u, v) - px_u
                ny = partner(shift_p, 1, u, v) - py[v + 3]
                factor = far - near * lax.rsqrt(nx * nx + ny * ny + DELTA_SQ)
                fx = fx + factor * nx
                fy = fy + factor * ny
            force[0, rows, :] = fx
            force[1, rows, :] = fy
            return carry

        lax.fori_loop(0, 64 // RUN, body, 0)

    top = sub < 4

    def row_flags():
        word = [jnp.where(top, row_words[0, dy], row_words[1, dy]) for dy in range(3)]
        seen = None
        for n, (u, v) in enumerate(ROW_OFFSETS):
            if u != seen:
                seen = u
                inside = ((sub < u) & has_up) | ((sub >= 8 - u) & has_down)
                bit = bit_at(sub, sub + jnp.where(top, -u, u))
                flags = [jnp.where(inside, intact_of(w, bit), 0.0) for w in word]
            intact = flags[1]
            if v < 0:
                intact = jnp.where((lane & 15) + v < 0, flags[0], intact)
            if v > 0:
                intact = jnp.where((lane & 15) + v > 15, flags[2], intact)
            row_coef[n, 0] = intact

    def ice_rows(step, field, rows_r):
        last = step == 1
        base = 2 if last else 0
        mine = [jnp.where(top, field[c, 8:16, :], field[c, 64:72, :]) for c in range(base, 4)]
        mine_y = [[mine[c] - float(v) for v in range(-3, 4)] for c in range(1, 4 - base, 2)]
        fx = fy = zero
        seen = None
        for n, (u, v) in enumerate(ROW_OFFSETS):
            if u != seen:
                seen = u
                beyond = [
                    jnp.where(top, slide(rows_r[0, c // 2], u + 3 * (c % 2)), slide(rows_r[1, c // 2], -u - 3 * (c % 2)))
                    for c in range(4 - base)
                ]
                by = jnp.where(top, -float(u), float(u))
                mine_x = [mine[c] - by for c in range(0, 4 - base, 2)]
            near = row_coef[n, 0]
            if not last:
                rx = turn(beyond[0], -v) - mine_x[0]
                ry = turn(beyond[1], -v) - mine_y[0][v + 3]
                near, far = bonds(near, rx * rx + ry * ry + DELTA_SQ)
                row_coef[n, 0] = near
                row_coef[n, 1] = far
            else:
                far = row_coef[n, 1]
            nx = turn(beyond[2 - base], -v) - mine_x[-1]
            ny = turn(beyond[3 - base], -v) - mine_y[-1][v + 3]
            factor = far - near * lax.rsqrt(nx * nx + ny * ny + DELTA_SQ)
            fx = fx + factor * nx
            fy = fy + factor * ny
        present = (top & has_up) | (jnp.logical_not(top) & has_down)
        return jnp.where(present, fx, 0.0), jnp.where(present, fy, 0.0)

    near_col = jnp.where(sub < 3, 0, jnp.where(sub < 5, 1, 2))
    far_col = jnp.where(sub < 3, sub + 1, jnp.where(sub < 5, sub - 2, 1))
    point_row = lane & 63

    def column_flags():
        for side in range(2):
            there = (sub < 6) & (has_right if side else has_left)
            for u in range(-3, 4):
                word = col_words[3 * side + 1]
                present = there
                if u < 0:
                    word = jnp.where((lane & 7) + u < 0, col_words[3 * side], word)
                    present = there & ((point_row + u >= 0) | has_up)
                if u > 0:
                    word = jnp.where((lane & 7) + u > 7, col_words[3 * side + 2], word)
                    present = there & ((point_row + u <= 63) | has_down)
                col_coef[side, u + 3, 0] = jnp.where(present, intact_of(word, bit_at(lane, lane + u)), 0.0)

    def ice_columns(step, edge_s, edge_r):
        last = step == 1
        parts = (0,) if last else (0, 1)
        sides = []
        for side in range(2):
            mine_at = 7 - near_col if side else near_col
            beyond_at = far_col - 1 if side else 8 - far_col
            shifts = [3 * p for p in parts]
            by = jnp.where(lane < 64, 0.0, (near_col + far_col).astype(f32) * (1.0 if side else -1.0))
            mine = [pick(edge_s[side, 0], mine_at - h if side else mine_at + h, 0) - by for h in shifts]
            beyond = [
                [pick(edge_r[slot, side, 0], beyond_at + h if side else beyond_at - h, 0) for slot in range(3)]
                for h in shifts
            ]
            total = zero
            for u in range(-3, 4):
                def moved(p):
                    if u == 0:
                        return beyond[p][1]
                    inside = (point_row + u >= 0) | jnp.logical_not(has_up)
                    if u > 0:
                        inside = (point_row + u <= 63) | jnp.logical_not(has_down)
                    return jnp.where(inside, turn(beyond[p][1], -u), turn(beyond[p][0 if u < 0 else 2], 64 - u))

                offset = jnp.where(lane < 64, float(u), 0.0)
                near = col_coef[side, u + 3, 0]
                if not last:
                    rest = moved(0) - (mine[0] - offset)
                    square_of = rest * rest
                    near, far = bonds(near, square_of + turn(square_of, 64) + DELTA_SQ)
                    col_coef[side, u + 3, 0] = near
                    col_coef[side, u + 3, 1] = far
                else:
                    far = col_coef[side, u + 3, 1]
                now = moved(len(parts) - 1) - (mine[-1] - offset)
                square_of = now * now
                factor = far - near * lax.rsqrt(square_of + turn(square_of, 64) + DELTA_SQ)
                total = total + factor * now
            at = 7 - sub if side else sub
            total = jnp.where(has_right if side else has_left, total, 0.0)
            sides.append(
                jnp.where(at < 3, pick(total, jnp.where(at == 0, 0, jnp.where(at == 1, 3, 5)), 0), 0.0)
                + jnp.where(at < 2, pick(total, jnp.where(at == 0, 1, 4), 0), 0.0)
                + jnp.where(at == 0, pick(total, jnp.full((8, 128), 2, jnp.int32), 0), 0.0)
            )
            square[120 * side : 120 * side + 8, :] = sides[side]
        return sides

    def ice_partial(step, rows_force):
        for a in range(8):
            rows = pl.ds(8 * a, 8)
            for c in range(2):
                total = force[c, rows, :]
                if a == 0:
                    total = total + jnp.where(top, rows_force[c], 0.0)
                if a == 7:
                    total = total + jnp.where(top, 0.0, rows_force[c])
                    if c == 0:
                        total = total - push[...]
                speed = vel[c, rows, :] + STEP_DT * total
                moved = disp[c, rows, :] + STEP_DT * speed
                if step == 1:
                    v_out[c, a] = swap_groups(speed)
                    d_out[c, a] = swap_groups(moved)
                else:
                    vel[c, rows, :] = speed
                    disp[c, rows, :] = moved
                    field2[2 + c, 8 + 8 * a : 16 + 8 * a, :] = field1[c, 8 + 8 * a : 16 + 8 * a, :] + moved

    def ice_complete(step):
        sides_force = jnp.transpose(square[...])
        for a in range(8):
            rows = pl.ds(8 * a, 8)
            for c in range(2):
                push_on = STEP_DT * sides_force[64 * c + 8 * a : 64 * c + 8 * a + 8, :]
                if step == 1:
                    push_on = swap_groups(push_on)
                    v_out[c, a] = v_out[c, a] + push_on
                    d_out[c, a] = d_out[c, a] + STEP_DT * push_on
                else:
                    vel[c, rows, :] = vel[c, rows, :] + push_on
                    shift = STEP_DT * push_on
                    disp[c, rows, :] = disp[c, rows, :] + shift
                    there = slice(8 + 8 * a, 16 + 8 * a)
                    field2[2 + c, there, :] = field2[2 + c, there, :] + shift

    def sideways(x, first, last):
        up = [turn(c, 1) for c in x]
        down = [turn(c, -1) for c in x]
        return [
            jnp.where(lane == 0, up[k - 1] if k else first, up[k])
            + jnp.where(lane == 127, down[k + 1] if k < 3 else last, down[k])
            for k in range(4)
        ]

    def shell_inside(field, put):
        def chunks(ref, start):
            return [ref[k, pl.ds(start, 8), :] for k in range(4)]

        def once(b, carry):
            for h in range(4):
                i = pl.multiple_of(32 * b + 8 * h + 8, 8)
                f, up, down = chunks(field, i), chunks(field, i - 1), chunks(field, i + 1)
                for k, side in enumerate(sideways(f, 0.0, 0.0)):
                    bend1[k, pl.ds(i, 8), :] = (up[k] + down[k]) + side - 4.0 * f[k]
            return carry

        def twice(b, carry):
            for h in range(4):
                base = pl.multiple_of(32 * b + 8 * h, 8)
                i = pl.multiple_of(base + 8, 8)
                f, g = chunks(field, i), chunks(bend1, i)
                up, down = chunks(bend1, i - 1), chunks(bend1, i + 1)
                for k, side in enumerate(sideways(g, f[0], f[3])):
                    at = (pl.ds(base, 8), slice(128 * k, 128 * k + 128))
                    bending = (up[k] + down[k]) + side - 4.0 * g[k]
                    speed = shell_v[at] - (STEP_DT * BEND) * bending
                    shell_v[at] = speed
                    put(base, k, f[k] + STEP_DT * speed)
            return carry

        lax.fori_loop(0, 4, once, 0)
        for k in range(4):
            bend1[k, 7:8, :] = field[k, 8:9, :]
            bend1[k, 136:137, :] = field[k, 135:136, :]
        lax.fori_loop(0, 4, twice, 0)

    def rim_terms(step, side):
        edge_r = edge_r2 if step else edge_r1
        above, level, below = (edge_r[t, side, 1] for t in range(3))
        level = jnp.where(lane < 2, jnp.where(has_up, turn(above, -30), 0.0), turn(level, 2))
        rim = jnp.where(lane >= 34, jnp.where(has_down, turn(below, 34), 0.0), level)
        rim = jnp.where(has_right if side else has_left, rim, 0.0)
        first = turn(rim, 1 if side else -1)
        up, down = slide(first, 1), slide(first, -1)
        up = jnp.where(sub == 0, turn(up, 2), up)
        down = jnp.where(sub == 7, turn(down, -2), down)
        full = rim - 8.0 * first + 2.0 * (up + down)
        return jnp.where((lane & 1) == side, full, rim)

    def slab_terms(step):
        terms = []
        for k in range(2):
            slab = rows_r1[k, 2] if step == 0 else rows_r2[k, 1]
            slab = jnp.where(has_down if k else has_up, slab, 0.0)
            outer = [slide(slab, (6 if k else 0) - 2 * c) for c in range(4)]
            inner = [slide(slab, (7 if k else -1) - 2 * c) for c in range(4)]
            at = 7 - sub if k else sub
            terms.append(
                [
                    jnp.where(at < 2, o, 0.0) + jnp.where(at == 0, 2.0 * pair - 8.0 * x, 0.0)
                    for o, x, pair in zip(outer, inner, sideways(inner, 0.0, 0.0))
                ]
            )
        return terms

    all_blocks = [(k, b) for k in range(4) for b in range(16)]
    end_blocks = [(k, b) for k in range(4) for b in (0, 15)]
    side_blocks = [(k, b) for k in (0, 3) for b in range(16)]

    def loads_of(step, own):
        gaps = jnp.broadcast_to(gap_r[step], (8, 128))
        return [
            (STEP_DT * PENALTY) * jnp.maximum(pick(gaps, 32 * k + lane // 4, 1) - own[k], 0.0) for k in range(4)
        ]

    def slab_changes(step):
        slabs = slab_terms(step)
        return {(k, b): (-STEP_DT * BEND) * slabs[b // 15][k] for k, b in end_blocks}

    def rim_changes(rims):
        changes = {}
        for k, b in side_blocks:
            rim = turn(rims[k // 3], (124 if k else -2) - 2 * b)
            changes[k, b] = (-STEP_DT * BEND) * jnp.where(lane >= 126 if k else lane < 2, rim, 0.0)
        return changes

    def shell_change(blocks, load, changes, put, get):
        for k, b in blocks:
            change = None if load is None else jnp.where(sub + 8 * b == targets[k], load[k], 0.0)
            if (k, b) in changes:
                change = changes[k, b] if change is None else change + changes[k, b]
            at = (pl.ds(8 * b, 8), slice(128 * k, 128 * k + 128))
            shell_v[at] = shell_v[at] + change
            put(8 * b, k, get(8 * b, k) + STEP_DT * change)

    def put_block(base, k, moved):
        shell2[k, pl.ds(base + 8, 8), :] = moved

    def get_block(base, k):
        return shell2[k, pl.ds(base + 8, 8), :]

    def out_block(base, k, moved):
        s_out[pl.ds(base, 8), 128 * k : 128 * k + 128] = moved

    def out_get(base, k):
        return s_out[pl.ds(base, 8), 128 * k : 128 * k + 128]

    row_flags()
    column_flags()
    for c in range(2):
        spread_field(field1, c, shift_j.at[c])
        spread_field(field1, 2 + c, shift_p.at[c])
    ice_inside(0, field1)
    later[2].wait()
    shell_inside(shell1, put_block)

    rows_arrived(0, 12)
    rows_force = ice_rows(0, field1, rows_r1)
    end_contact(0)
    ice_partial(0, rows_force)
    edge_left, edge_right = edges(field2, 2)
    shell_change(all_blocks, loads_of(0, own), slab_changes(0), put_block, get_block)
    rim_left, rim_right = pack_rim(shell2)

    columns_arrived(0, 8)
    sides_left, sides_right = ice_columns(0, edge_s1, edge_r1)
    edge_s2[0, 0] = edge_left + STEP_DT**2 * sides_left
    edge_s2[1, 0] = edge_right + STEP_DT**2 * sides_right
    rims = [rim_terms(0, side) for side in range(2)]
    edge_s2[0, 1] = rim_left - (STEP_DT**2 * BEND) * turn(rims[0], -2)
    edge_s2[1, 1] = rim_right - (STEP_DT**2 * BEND) * turn(rims[1], -2)
    send_columns(1, edge_s2, edge_r2)

    ice_complete(0)
    rows_s2[0, 0], rows_s2[1, 0] = pack_rows(field2, 2)
    put_gap(1)
    start_gap(1)
    shell_change(side_blocks, None, rim_changes(rims), put_block, get_block)
    rows_s2[0, 1], rows_s2[1, 1] = pack_slab(shell2)
    send_rows(1, rows_s2, rows_r2)
    own, points = gather_points(touched(shell2))
    reach_s[1] = points[0:1, :]
    start_reach(1)

    for c in range(2):
        spread_field(field2, 2 + c, shift_p.at[c])
    ice_inside(1, field2)
    shell_inside(shell2, out_block)

    rows_arrived(1, 8)
    rows_force = ice_rows(1, field2, rows_r2)
    end_contact(1)
    ice_partial(1, rows_force)
    shell_change(all_blocks, loads_of(1, own), slab_changes(1), out_block, out_get)
    columns_arrived(1, 8)
    ice_columns(1, edge_s2, edge_r2)
    ice_complete(1)
    shell_change(side_blocks, None, rim_changes([rim_terms(1, side) for side in range(2)]), out_block, out_get)

    for dx, dy in SIDES:
        with_peer(dx, dy, lambda where: group_wait(16 if dy else 20, dx, dy, 0).wait_send())

    @pl.when(is_front)
    def _():
        slots = reach_r.at[:, 0 : n_x - 1]
        pltpu.make_async_remote_copy(
            slots, slots, con_send.at[0], con_recv.at[0], device_id=(0, gy), device_id_type=MESH
        ).wait_send()

    @pl.when(jnp.logical_not(is_front))
    def _():
        pltpu.make_async_remote_copy(
            gap_r, gap_r, con_send.at[0], con_recv.at[0], device_id=(front, gy), device_id_type=MESH
        ).wait_send()


def write_out(*refs):
    copies = [pltpu.make_async_copy(refs[k], refs[4 + k], refs[8].at[k]) for k in range(4)]
    for copy in copies:
        copy.start()
    for copy in copies:
        copy.wait()


def on_device(n_x, n_y, width, d, v, j, bond, node, inter, shell, speed):
    f32, i32 = jnp.float32, jnp.int32
    vmem = pltpu.VMEM
    dma = pltpu.SemaphoreType.DMA
    shapes = [x.shape for x in (d, v, shell, speed)]
    held = pl.pallas_call(
        functools.partial(kernel, n_x, n_y, width),
        out_shape=[vmem(s, f32) for s in shapes],
        in_specs=[pl.BlockSpec(memory_space=pl.ANY)] * 8,
        out_specs=[pl.BlockSpec(memory_space=vmem)] * 4,
        scratch_shapes=[
            vmem(d.shape, f32), vmem(v.shape, f32), vmem(j.shape, f32), vmem(bond.shape, i32),
            vmem(node.shape, i32), vmem(inter.shape, f32),
            vmem((4, 80, 128), f32), vmem((4, 80, 128), f32), vmem((2, 64, 128), f32), vmem((2, 64, 128), f32),
            vmem((2, 64, 128), f32),
            vmem((2, 7, 80, 128), f32), vmem((2, 7, 80, 128), f32), vmem((9, 64, 128), i32),
            vmem((len(OFFSETS), 2, 64, 128), f32), vmem((len(ROW_OFFSETS), 2, 8, 128), f32),
            vmem((2, 7, 2, 8, 128), f32),
            vmem((2, 3, 8, 128), i32), vmem((4, 144, 128), f32), vmem((4, 144, 128), f32), vmem((4, 144, 128), f32),
            vmem((128, 128), f32),
            vmem((2, 2, 8, 128), f32), vmem((3, 2, 2, 8, 128), f32),
            vmem((2, 2, 8, 128), f32), vmem((3, 2, 2, 8, 128), f32),
            vmem((2, 3, 8, 128), f32), vmem((2, 3, 8, 128), f32), vmem((2, 2, 8, 128), f32), vmem((2, 2, 8, 128), f32),
            vmem((8, 128), f32), vmem((2, n_x, 1, 128), f32), vmem((2, 1, 128), f32),
            vmem((2, 1, 128), f32), vmem((2, n_x, 1, 128), f32), vmem((8, 128), f32),
            dma((8,)), dma((3, 3)), dma((2, 3, 3)), dma((1,)), dma((2,)),
        ],
        compiler_params=pltpu.CompilerParams(collective_id=0, has_side_effects=True),
    )(d, v, j, bond, node, inter, shell, speed)
    return pl.pallas_call(
        write_out,
        out_shape=[jax.ShapeDtypeStruct(s, f32) for s in shapes],
        in_specs=[pl.BlockSpec(memory_space=vmem)] * 4,
        out_specs=[pl.BlockSpec(memory_space=pl.ANY)] * 4,
        scratch_shapes=[dma((4,))],
    )(*[pltpu.with_memory_space_constraint(x, vmem) for x in held])


def solution(mesh):
    n_x, n_y = mesh.shape["gx"], mesh.shape["gy"]
    ice, plate = P(None, "gx", "gy", None), P("gx", "gy")

    def step(d, v, j, bond, *rest):
        width = rest[2].shape[1] * n_y
        return on_device(n_x, n_y, width, d, v, j, bond.reshape(-1, bond.shape[2]), *rest)

    return jax.shard_map(
        step,
        mesh=mesh,
        in_specs=(ice, ice, ice, P("gx", "gy", None), P("gy", None), P("gy", None), plate, plate),
        out_specs=(ice, ice, plate, plate),
        check_vma=False,
    )
```

```python
import functools

import jax
import jax.numpy as jnp
from jax import lax
from jax.experimental import pallas as pl
from jax.experimental.pallas import tpu as pltpu
from jax.sharding import PartitionSpec as P

MESH = pl.DeviceIdType.MESH

HORIZON = 3.5
DELTA_SQ = 0.25
PENALTY = 4.0
BEND = 0.5
STEP_DT = 0.2
RUN = 32

OFFSETS = [
    (u, v)
    for u in range(-3, 4)
    for v in range(-3, 4)
    if (u, v) != (0, 0) and max(abs(u) - 0.4, 0) ** 2 + max(abs(v) - 0.4, 0) ** 2 < HORIZON**2 - DELTA_SQ
]
ROW_OFFSETS = [(u, v) for u, v in OFFSETS if u > 0]
SIDES = [(dx, dy) for dx in (-1, 0, 1) for dy in (-1, 0, 1) if (dx, dy) != (0, 0)]


def iota(axis):
    return lax.broadcasted_iota(jnp.int32, (8, 128), axis)


def pick(x, index, axis):
    return jnp.take_along_axis(x, index, axis=axis, mode="promise_in_bounds")


def swap_groups(x):
    sub, group = iota(0), iota(1) // 16
    x = pltpu.roll(x, 0, 1, stride=16, stride_axis=0)
    x = pick(x, (group - sub) & 7, 0)
    return pick(x, ((group + sub) & 7) * 16 + (iota(1) & 15), 1)


def turn(x, shift):
    shift = shift % 128
    return pltpu.roll(x, shift, 1) if shift else x


def slide(x, shift):
    return pltpu.roll(x, shift % 8, 0)


def bonds(intact, square):
    inverse = lax.rsqrt(square)
    reach = jnp.maximum(HORIZON - square * inverse, 0.0)
    near = intact * (reach * reach)
    return near, near * inverse


def intact_of(word, bit):
    return jnp.where((word & bit) != 0, 1.0 / HORIZON**2, 0.0)


def bit_at(row, beyond):
    return jnp.left_shift(1, 4 * (row & 7) + ((beyond & 7) >> 1))


def kernel(
    n_x, n_y, width,
    d_hbm, v_hbm, j_hbm, bond_hbm, node_hbm, inter_hbm, s_hbm, w_hbm,
    d_out, v_out, s_out, shell_v,
    d_in, v_in, j_in, bond, node, inter,
    field1, field2, disp, vel, force, shift_j, shift_p, words, coef, row_coef, col_coef,
    row_words, shell1, shell2, bend1, square,
    edge_s1, edge_r1, edge_s2, edge_r2, rows_s1, rows_r1, rows_s2, rows_r2,
    gap_all, gap_s, gap_r, reach_s, reach_r, push,
    in_sem, send_sem, recv_sem, con_send, con_recv,
):
    f32 = jnp.float32
    gx, gy = lax.axis_index("gx"), lax.axis_index("gy")
    front = n_x - 1
    is_front = gx == front
    has_up, has_down, has_left, has_right = gx > 0, gx < n_x - 1, gy > 0, gy < n_y - 1
    sub, lane = iota(0), iota(1)
    zero = jnp.zeros((8, 128), f32)

    across = {-1: has_left, 1: has_right}
    along = {-1: has_up, 1: has_down}

    def with_peer(dx, dy, run):
        there = along[dx] & across[dy] if dx and dy else along[dx] if dx else across[dy]

        @pl.when(there)
        def _():
            run((gx + dx, gy + dy))

    barrier = pltpu.get_barrier_semaphore()

    def greet(where):
        pl.semaphore_signal(barrier, inc=1, device_id=where, device_id_type=MESH)

    for dx, dy in SIDES:
        with_peer(dx, dy, greet)

    @pl.when(is_front)
    def _():
        for i in range(n_x - 2):
            greet((i, gy))

    @pl.when(gx < n_x - 2)
    def _():
        greet((front, gy))

    def load(src, dst, k):
        return pltpu.make_async_copy(src, dst, in_sem.at[k])

    def span(kib):
        return coef.at[0 : kib // 4, 0, 0:8, :]

    first = [load(j_hbm, j_in, 0), load(d_hbm, d_in, 1), load(node_hbm, node, 2), load(inter_hbm, inter, 3)]
    plate = [load(s_hbm.at[:, 128 * k : 128 * k + 128], shell1.at[k, 8:136, :], 4) for k in range(4)]
    later = [load(bond_hbm, bond, 5), load(v_hbm, v_in, 6), load(w_hbm, shell_v, 7)]
    for copy in first + plate + later:
        copy.start()

    for r in (0, 72):
        for c in range(2):
            for v in range(7):
                shift_j[c, v, r : r + 8, :] = zero
                shift_p[c, v, r : r + 8, :] = zero
        for c in range(4):
            field1[c, r : r + 8, :] = zero
            field2[c, r : r + 8, :] = zero
    for field in (shell1, shell2):
        for r in (0, 136):
            for k in range(4):
                field[k, r : r + 8, :] = zero
    for b in range(1, 15):
        square[8 * b : 8 * b + 8, :] = zero

    first[0].wait()
    first[1].wait()
    for a in range(8):
        rows = pl.ds(8 + 8 * a, 8)
        for c in range(2):
            jit = swap_groups(j_in[c, a])
            dis = swap_groups(d_in[c, a])
            field1[c, rows, :] = jit
            field1[2 + c, rows, :] = jit + dis
            disp[c, pl.ds(8 * a, 8), :] = dis

    def edges(field, base):
        stack = jnp.concatenate([field[base, 8:72, :], field[base + 1, 8:72, :]], axis=0)
        across = jnp.transpose(stack)
        return across[0:8, :], across[120:128, :]

    jit_left, jit_right = edges(field1, 0)
    pos_left, pos_right = edges(field1, 2)
    edge_s1[0, 0] = jnp.where(sub < 3, jit_left, slide(pos_left, 3))
    edge_s1[1, 0] = jnp.where(sub > 4, jit_right, slide(pos_right, -3))

    def pack_rows(field, base):
        x, y = field[base, 8:16, :], field[base + 1, 8:16, :]
        first_rows = jnp.where(sub < 3, x, slide(y, 3))
        x, y = field[base, 64:72, :], field[base + 1, 64:72, :]
        return first_rows, jnp.where(sub > 4, x, slide(y, -3))

    for part, base in enumerate((0, 2)):
        rows_s1[0, part], rows_s1[1, part] = pack_rows(field1, base)

    def pack_slab(field):
        ends = []
        for start, at in ((8, 0), (128, 6)):
            total = zero
            for c in range(4):
                total = jnp.where(sub // 2 == c, slide(field[c, start : start + 8, :], 2 * c - at), total)
            ends.append(total)
        return ends

    first[2].wait()
    first[3].wait()
    inter[...] = swap_groups(inter[...])
    node[...] = swap_groups(node[...])

    def put_gap(step):
        gap = disp[0, 56:64, :] + inter[...]
        gap_all[...] = gap
        for i in range(8):
            gap_s[step, i] = gap[i : i + 1, :]

    put_gap(0)

    mine = jnp.broadcast_to(node[pl.ds(gx, 1), :], (8, 128))
    targets = []
    for k in range(4):
        n = pick(mine, 32 * k + lane // 4, 1)
        row = lax.shift_right_logical(n, width.bit_length() - 1) & 127
        targets.append(jnp.where((n & 3) == (lane & 3), row, -1))

    def gather_points(totals):
        own = []
        points = zero
        for k, total in enumerate(totals):
            for s in (4, 2, 1):
                total = total + slide(total, s)
            own.append(total)
            total = total + turn(total, -1)
            total = total + turn(total, -2)
            points = jnp.where(lane // 32 == k, pick(total, (lane & 31) * 4, 1), points)
        return own, points

    def touched(field):
        totals = []
        for k in range(4):
            total = zero
            for b in range(16):
                x = field[k, 8 + 8 * b : 16 + 8 * b, :]
                total = total + jnp.where(sub + 8 * b == targets[k], x, 0.0)
            totals.append(total)
        return totals

    def pack_rim(field):
        left = right = zero
        for b in range(16):
            here = lane // 2 == b
            left = jnp.where(here, turn(field[0, 8 + 8 * b : 16 + 8 * b, :], 2 * b), left)
            right = jnp.where(here, turn(field[3, 8 + 8 * b : 16 + 8 * b, :], 2 * b + 2), right)
        return left, right

    load(shell1.at[:, 8:136, :], shell1.at[:, 8:136, :], 4).wait()
    own, points = gather_points(touched(shell1))
    reach_s[0] = points[0:1, :]
    left, right = pack_rim(shell1)
    edge_s1[0, 1] = left
    edge_s1[1, 1] = right
    rows_s1[0, 2], rows_s1[1, 2] = pack_slab(shell1)

    n_along = has_up.astype(jnp.int32) + has_down.astype(jnp.int32)
    n_across = has_left.astype(jnp.int32) + has_right.astype(jnp.int32)
    extra = jnp.where(is_front, n_x - 2, jnp.where(gx < n_x - 2, 1, 0))
    pl.semaphore_wait(barrier, n_along + n_across + n_along * n_across + extra)

    def send(src, dst, phase, dx, dy):
        with_peer(dx, dy, lambda where: pltpu.make_async_remote_copy(
            src, dst, send_sem.at[1 - dx, 1 - dy], recv_sem.at[phase, 1 - dx, 1 - dy],
            device_id=where, device_id_type=MESH,
        ).start())

    def send_columns(phase, src, dst):
        for dx in (-1, 1, 0):
            for dy in (-1, 1):
                side = (dy + 1) // 2
                send(src.at[side], dst.at[1 - dx, 1 - side], phase, dx, dy)

    def send_rows(phase, src, dst):
        for k, dx in enumerate((-1, 1)):
            send(src.at[k], dst.at[1 - k], phase, dx, 0)

    def group_wait(kib, dx, dy, phase):
        return pltpu.make_async_remote_copy(
            span(kib), span(kib), send_sem.at[1 - dx, 1 - dy], recv_sem.at[phase, 1 + dx, 1 + dy],
            device_id=(0, 0), device_id_type=MESH,
        )

    def rows_arrived(phase, kib):
        for dx in (-1, 1):
            with_peer(dx, 0, lambda where: group_wait(kib, dx, 0, phase).wait_recv())

    def columns_arrived(phase, kib):
        for dy in (-1, 1):
            for dx in (0, -1, 1):
                with_peer(dx, dy, lambda where: group_wait(kib, dx, dy, phase).wait_recv())

    def gap_copy(step, i):
        return pltpu.make_async_remote_copy(
            gap_s.at[step, i], gap_r.at[step], con_send.at[0], con_recv.at[step],
            device_id=(i, gy), device_id_type=MESH,
        )

    def reach_copy(step):
        return pltpu.make_async_remote_copy(
            reach_s.at[step], reach_r.at[step, gx], con_send.at[0], con_recv.at[step],
            device_id=(front, gy), device_id_type=MESH,
        )

    def start_gap(step):
        @pl.when(is_front)
        def _():
            for i in range(n_x - 1):
                gap_copy(step, i).start()
            gap_r[step] = gap_s[step, n_x - 1]

    def start_reach(step):
        @pl.when(is_front)
        def _():
            reach_r[step, front] = reach_s[step]

        @pl.when(jnp.logical_not(is_front))
        def _():
            reach_copy(step).start()

    def end_contact(step):
        @pl.when(is_front)
        def _():
            slots = reach_r.at[step, 0 : n_x - 1]
            pltpu.make_async_remote_copy(
                slots, slots, con_send.at[0], con_recv.at[step], device_id=(0, gy), device_id_type=MESH
            ).wait_recv()
            reached = jnp.broadcast_to(reach_r[step, front], (8, 128))
            for i in range(n_x - 1):
                reached = jnp.where(sub == i, jnp.broadcast_to(reach_r[step, i], (8, 128)), reached)
            push[...] = PENALTY * jnp.maximum(gap_all[...] - reached, 0.0)

        @pl.when(jnp.logical_not(is_front))
        def _():
            gap_copy(step, 0).wait_recv()
            push[...] = jnp.zeros((8, 128), f32)

    send_columns(0, edge_s1, edge_r1)
    send_rows(0, rows_s1, rows_r1)
    start_gap(0)
    start_reach(0)

    later[0].wait()
    none = jnp.zeros((8, 128), jnp.int32)
    for s in range(9):
        for a in range(8):
            word = pick(jnp.broadcast_to(bond[8 * a : 8 * a + 8, s : s + 1], (8, 128)), lane // 16, 0)
            if s % 3 == 0:
                word = jnp.where(lane < 16, 0, word)
            if s % 3 == 2:
                word = jnp.where(lane >= 112, 0, word)
            if a == 0 and s < 3:
                row_words[0, s] = word
                word = none
            if a == 7 and s > 5:
                row_words[1, s - 6] = word
                word = none
            words[s, 8 * a : 8 * a + 8, :] = word
    col_words = []
    for side in range(2):
        tiles = bond[pl.ds(7 * side, 8, stride=8), :]
        for dx in range(3):
            s = 3 * dx + 2 * side
            word = jnp.broadcast_to(tiles[:, s : s + 1], (8, 128))
            col_words.append(pick(word, (lane & 63) // 8, 0))
    later[1].wait()
    for a in range(8):
        for c in range(2):
            vel[c, pl.ds(8 * a, 8), :] = swap_groups(v_in[c, a])

    def spread_field(field, index, out):
        for b in range(1, 9):
            x = field[index, 8 * b : 8 * b + 8, :]
            for v in range(-3, 4):
                if v:
                    out[v + 3, 8 * b : 8 * b + 8, :] = turn(x, -v)

    def ice_inside(step, field):
        last = step == 1
        sub_r = lax.broadcasted_iota(jnp.int32, (RUN, 128), 0)
        lane_r = lax.broadcasted_iota(jnp.int32, (RUN, 128), 1)
        tile_row, tile_col = sub_r & 7, lane_r & 15

        def body(a, carry):
            base = pl.multiple_of(RUN * a, RUN)
            rows = pl.ds(base, RUN)
            own = pl.ds(pl.multiple_of(base + 8, 8), RUN)

            def partner(shifted, c, u, v):
                there = pl.ds(base + (8 + u), RUN)
                if v == 0:
                    return field[(0 if shifted is shift_j else 2) + c, there, :]
                return shifted[c, v + 3, there, :]

            px = field[2, own, :]
            py = [field[3, own, :] - float(v) for v in range(-3, 4)]
            if not last:
                jx = field[0, own, :]
                jy = [field[1, own, :] - float(v) for v in range(-3, 4)]
            fx = fy = jnp.zeros((RUN, 128), f32)
            seen = None
            for n, (u, v) in enumerate(OFFSETS):
                if u != seen:
                    seen = u
                    px_u = px - float(u)
                    if not last:
                        jx_u = jx - float(u)
                        bit = bit_at(tile_row, tile_row + u)
                        flags = []
                        for dy in range(3):
                            word = words[3 + dy, rows, :]
                            if u < 0:
                                word = jnp.where(tile_row + u < 0, words[dy, rows, :], word)
                            if u > 0:
                                word = jnp.where(tile_row + u > 7, words[6 + dy, rows, :], word)
                            flags.append(intact_of(word, bit))
                if not last:
                    intact = flags[1]
                    if v < 0:
                        intact = jnp.where(tile_col + v < 0, flags[0], intact)
                    if v > 0:
                        intact = jnp.where(tile_col + v > 15, flags[2], intact)
                    rx = partner(shift_j, 0, u, v) - jx_u
                    ry = partner(shift_j, 1, u, v) - jy[v + 3]
                    near, far = bonds(intact, rx * rx + ry * ry + DELTA_SQ)
                    coef[n, 0, rows, :] = near
                    coef[n, 1, rows, :] = far
                else:
                    near = coef[n, 0, rows, :]
                    far = coef[n, 1, rows, :]
                nx = partner(shift_p, 0, u, v) - px_u
                ny = partner(shift_p, 1, u, v) - py[v + 3]
                factor = far - near * lax.rsqrt(nx * nx + ny * ny + DELTA_SQ)
                fx = fx + factor * nx
                fy = fy + factor * ny
            force[0, rows, :] = fx
            force[1, rows, :] = fy
            return carry

        lax.fori_loop(0, 64 // RUN, body, 0)

    top = sub < 4

    def row_flags():
        word = [jnp.where(top, row_words[0, dy], row_words[1, dy]) for dy in range(3)]
        seen = None
        for n, (u, v) in enumerate(ROW_OFFSETS):
            if u != seen:
                seen = u
                inside = ((sub < u) & has_up) | ((sub >= 8 - u) & has_down)
                bit = bit_at(sub, sub + jnp.where(top, -u, u))
                flags = [jnp.where(inside, intact_of(w, bit), 0.0) for w in word]
            intact = flags[1]
            if v < 0:
                intact = jnp.where((lane & 15) + v < 0, flags[0], intact)
            if v > 0:
                intact = jnp.where((lane & 15) + v > 15, flags[2], intact)
            row_coef[n, 0] = intact

    def ice_rows(step, field, rows_r):
        last = step == 1
        base = 2 if last else 0
        mine = [jnp.where(top, field[c, 8:16, :], field[c, 64:72, :]) for c in range(base, 4)]
        mine_y = [[mine[c] - float(v) for v in range(-3, 4)] for c in range(1, 4 - base, 2)]
        fx = fy = zero
        seen = None
        for n, (u, v) in enumerate(ROW_OFFSETS):
            if u != seen:
                seen = u
                beyond = [
                    jnp.where(top, slide(rows_r[0, c // 2], u + 3 * (c % 2)), slide(rows_r[1, c // 2], -u - 3 * (c % 2)))
                    for c in range(4 - base)
                ]
                by = jnp.where(top, -float(u), float(u))
                mine_x = [mine[c] - by for c in range(0, 4 - base, 2)]
            near = row_coef[n, 0]
            if not last:
                rx = turn(beyond[0], -v) - mine_x[0]
                ry = turn(beyond[1], -v) - mine_y[0][v + 3]
                near, far = bonds(near, rx * rx + ry * ry + DELTA_SQ)
                row_coef[n, 0] = near
                row_coef[n, 1] = far
            else:
                far = row_coef[n, 1]
            nx = turn(beyond[2 - base], -v) - mine_x[-1]
            ny = turn(beyond[3 - base], -v) - mine_y[-1][v + 3]
            factor = far - near * lax.rsqrt(nx * nx + ny * ny + DELTA_SQ)
            fx = fx + factor * nx
            fy = fy + factor * ny
        present = (top & has_up) | (jnp.logical_not(top) & has_down)
        return jnp.where(present, fx, 0.0), jnp.where(present, fy, 0.0)

    near_col = jnp.where(sub < 3, 0, jnp.where(sub < 5, 1, 2))
    far_col = jnp.where(sub < 3, sub + 1, jnp.where(sub < 5, sub - 2, 1))
    point_row = lane & 63

    def column_flags():
        for side in range(2):
            there = (sub < 6) & (has_right if side else has_left)
            for u in range(-3, 4):
                word = col_words[3 * side + 1]
                present = there
                if u < 0:
                    word = jnp.where((lane & 7) + u < 0, col_words[3 * side], word)
                    present = there & ((point_row + u >= 0) | has_up)
                if u > 0:
                    word = jnp.where((lane & 7) + u > 7, col_words[3 * side + 2], word)
                    present = there & ((point_row + u <= 63) | has_down)
                col_coef[side, u + 3, 0] = jnp.where(present, intact_of(word, bit_at(lane, lane + u)), 0.0)

    def ice_columns(step, edge_s, edge_r):
        last = step == 1
        parts = (0,) if last else (0, 1)
        sides = []
        for side in range(2):
            mine_at = 7 - near_col if side else near_col
            beyond_at = far_col - 1 if side else 8 - far_col
            shifts = [3 * p for p in parts]
            by = jnp.where(lane < 64, 0.0, (near_col + far_col).astype(f32) * (1.0 if side else -1.0))
            mine = [pick(edge_s[side, 0], mine_at - h if side else mine_at + h, 0) - by for h in shifts]
            beyond = [
                [pick(edge_r[slot, side, 0], beyond_at + h if side else beyond_at - h, 0) for slot in range(3)]
                for h in shifts
            ]
            total = zero
            for u in range(-3, 4):
                def moved(p):
                    if u == 0:
                        return beyond[p][1]
                    inside = (point_row + u >= 0) | jnp.logical_not(has_up)
                    if u > 0:
                        inside = (point_row + u <= 63) | jnp.logical_not(has_down)
                    return jnp.where(inside, turn(beyond[p][1], -u), turn(beyond[p][0 if u < 0 else 2], 64 - u))

                offset = jnp.where(lane < 64, float(u), 0.0)
                near = col_coef[side, u + 3, 0]
                if not last:
                    rest = moved(0) - (mine[0] - offset)
                    square_of = rest * rest
                    near, far = bonds(near, square_of + turn(square_of, 64) + DELTA_SQ)
                    col_coef[side, u + 3, 0] = near
                    col_coef[side, u + 3, 1] = far
                else:
                    far = col_coef[side, u + 3, 1]
                now = moved(len(parts) - 1) - (mine[-1] - offset)
                square_of = now * now
                factor = far - near * lax.rsqrt(square_of + turn(square_of, 64) + DELTA_SQ)
                total = total + factor * now
            at = 7 - sub if side else sub
            total = jnp.where(has_right if side else has_left, total, 0.0)
            sides.append(
                jnp.where(at < 3, pick(total, jnp.where(at == 0, 0, jnp.where(at == 1, 3, 5)), 0), 0.0)
                + jnp.where(at < 2, pick(total, jnp.where(at == 0, 1, 4), 0), 0.0)
                + jnp.where(at == 0, pick(total, jnp.full((8, 128), 2, jnp.int32), 0), 0.0)
            )
            square[120 * side : 120 * side + 8, :] = sides[side]
        return sides

    def ice_partial(step, rows_force):
        for a in range(8):
            rows = pl.ds(8 * a, 8)
            for c in range(2):
                total = force[c, rows, :]
                if a == 0:
                    total = total + jnp.where(top, rows_force[c], 0.0)
                if a == 7:
                    total = total + jnp.where(top, 0.0, rows_force[c])
                    if c == 0:
                        total = total - push[...]
                speed = vel[c, rows, :] + STEP_DT * total
                moved = disp[c, rows, :] + STEP_DT * speed
                if step == 1:
                    v_out[c, a] = speed
                    d_out[c, a] = moved
                else:
                    vel[c, rows, :] = speed
                    disp[c, rows, :] = moved
                    field2[2 + c, 8 + 8 * a : 16 + 8 * a, :] = field1[c, 8 + 8 * a : 16 + 8 * a, :] + moved

    def ice_complete(step):
        sides_force = jnp.transpose(square[...])
        for a in range(8):
            rows = pl.ds(8 * a, 8)
            for c in range(2):
                push_on = STEP_DT * sides_force[64 * c + 8 * a : 64 * c + 8 * a + 8, :]
                if step == 1:
                    v_out[c, a] = v_out[c, a] + push_on
                    d_out[c, a] = d_out[c, a] + STEP_DT * push_on
                else:
                    vel[c, rows, :] = vel[c, rows, :] + push_on
                    shift = STEP_DT * push_on
                    disp[c, rows, :] = disp[c, rows, :] + shift
                    there = slice(8 + 8 * a, 16 + 8 * a)
                    field2[2 + c, there, :] = field2[2 + c, there, :] + shift

    def sideways(x, first, last):
        up = [turn(c, 1) for c in x]
        down = [turn(c, -1) for c in x]
        return [
            jnp.where(lane == 0, up[k - 1] if k else first, up[k])
            + jnp.where(lane == 127, down[k + 1] if k < 3 else last, down[k])
            for k in range(4)
        ]

    def shell_inside(field, put):
        def chunks(ref, start):
            return [ref[k, pl.ds(start, 8), :] for k in range(4)]

        def once(b, carry):
            for h in range(4):
                i = pl.multiple_of(32 * b + 8 * h + 8, 8)
                f, up, down = chunks(field, i), chunks(field, i - 1), chunks(field, i + 1)
                for k, side in enumerate(sideways(f, 0.0, 0.0)):
                    bend1[k, pl.ds(i, 8), :] = (up[k] + down[k]) + side - 4.0 * f[k]
            return carry

        def twice(b, carry):
            for h in range(4):
                base = pl.multiple_of(32 * b + 8 * h, 8)
                i = pl.multiple_of(base + 8, 8)
                f, g = chunks(field, i), chunks(bend1, i)
                up, down = chunks(bend1, i - 1), chunks(bend1, i + 1)
                for k, side in enumerate(sideways(g, f[0], f[3])):
                    at = (pl.ds(base, 8), slice(128 * k, 128 * k + 128))
                    bending = (up[k] + down[k]) + side - 4.0 * g[k]
                    speed = shell_v[at] - (STEP_DT * BEND) * bending
                    shell_v[at] = speed
                    put(base, k, f[k] + STEP_DT * speed)
            return carry

        lax.fori_loop(0, 4, once, 0)
        for k in range(4):
            bend1[k, 7:8, :] = field[k, 8:9, :]
            bend1[k, 136:137, :] = field[k, 135:136, :]
        lax.fori_loop(0, 4, twice, 0)

    def rim_terms(step, side):
        edge_r = edge_r2 if step else edge_r1
        above, level, below = (edge_r[t, side, 1] for t in range(3))
        level = jnp.where(lane < 2, jnp.where(has_up, turn(above, -30), 0.0), turn(level, 2))
        rim = jnp.where(lane >= 34, jnp.where(has_down, turn(below, 34), 0.0), level)
        rim = jnp.where(has_right if side else has_left, rim, 0.0)
        first = turn(rim, 1 if side else -1)
        up, down = slide(first, 1), slide(first, -1)
        up = jnp.where(sub == 0, turn(up, 2), up)
        down = jnp.where(sub == 7, turn(down, -2), down)
        full = rim - 8.0 * first + 2.0 * (up + down)
        return jnp.where((lane & 1) == side, full, rim)

    def slab_terms(step):
        terms = []
        for k in range(2):
            slab = rows_r1[k, 2] if step == 0 else rows_r2[k, 1]
            slab = jnp.where(has_down if k else has_up, slab, 0.0)
            outer = [slide(slab, (6 if k else 0) - 2 * c) for c in range(4)]
            inner = [slide(slab, (7 if k else -1) - 2 * c) for c in range(4)]
            at = 7 - sub if k else sub
            terms.append(
                [
                    jnp.where(at < 2, o, 0.0) + jnp.where(at == 0, 2.0 * pair - 8.0 * x, 0.0)
                    for o, x, pair in zip(outer, inner, sideways(inner, 0.0, 0.0))
                ]
            )
        return terms

    all_blocks = [(k, b) for k in range(4) for b in range(16)]
    end_blocks = [(k, b) for k in range(4) for b in (0, 15)]
    side_blocks = [(k, b) for k in (0, 3) for b in range(16)]

    def loads_of(step, own):
        gaps = jnp.broadcast_to(gap_r[step], (8, 128))
        return [
            (STEP_DT * PENALTY) * jnp.maximum(pick(gaps, 32 * k + lane // 4, 1) - own[k], 0.0) for k in range(4)
        ]

    def slab_changes(step):
        slabs = slab_terms(step)
        return {(k, b): (-STEP_DT * BEND) * slabs[b // 15][k] for k, b in end_blocks}

    def rim_changes(rims):
        changes = {}
        for k, b in side_blocks:
            rim = turn(rims[k // 3], (124 if k else -2) - 2 * b)
            changes[k, b] = (-STEP_DT * BEND) * jnp.where(lane >= 126 if k else lane < 2, rim, 0.0)
        return changes

    def shell_change(blocks, load, changes, put, get):
        for k, b in blocks:
            change = None if load is None else jnp.where(sub + 8 * b == targets[k], load[k], 0.0)
            if (k, b) in changes:
                change = changes[k, b] if change is None else change + changes[k, b]
            at = (pl.ds(8 * b, 8), slice(128 * k, 128 * k + 128))
            shell_v[at] = shell_v[at] + change
            put(8 * b, k, get(8 * b, k) + STEP_DT * change)

    def put_block(base, k, moved):
        shell2[k, pl.ds(base + 8, 8), :] = moved

    def get_block(base, k):
        return shell2[k, pl.ds(base + 8, 8), :]

    def out_block(base, k, moved):
        s_out[pl.ds(base, 8), 128 * k : 128 * k + 128] = moved

    def out_get(base, k):
        return s_out[pl.ds(base, 8), 128 * k : 128 * k + 128]

    row_flags()
    column_flags()
    for c in range(2):
        spread_field(field1, c, shift_j.at[c])
        spread_field(field1, 2 + c, shift_p.at[c])
    ice_inside(0, field1)
    later[2].wait()
    shell_inside(shell1, put_block)

    rows_arrived(0, 12)
    rows_force = ice_rows(0, field1, rows_r1)
    end_contact(0)
    ice_partial(0, rows_force)
    edge_left, edge_right = edges(field2, 2)
    shell_change(all_blocks, loads_of(0, own), slab_changes(0), put_block, get_block)
    rim_left, rim_right = pack_rim(shell2)

    columns_arrived(0, 8)
    sides_left, sides_right = ice_columns(0, edge_s1, edge_r1)
    edge_s2[0, 0] = edge_left + STEP_DT**2 * sides_left
    edge_s2[1, 0] = edge_right + STEP_DT**2 * sides_right
    rims = [rim_terms(0, side) for side in range(2)]
    edge_s2[0, 1] = rim_left - (STEP_DT**2 * BEND) * turn(rims[0], -2)
    edge_s2[1, 1] = rim_right - (STEP_DT**2 * BEND) * turn(rims[1], -2)
    send_columns(1, edge_s2, edge_r2)

    ice_complete(0)
    rows_s2[0, 0], rows_s2[1, 0] = pack_rows(field2, 2)
    put_gap(1)
    start_gap(1)
    shell_change(side_blocks, None, rim_changes(rims), put_block, get_block)
    rows_s2[0, 1], rows_s2[1, 1] = pack_slab(shell2)
    send_rows(1, rows_s2, rows_r2)
    own, points = gather_points(touched(shell2))
    reach_s[1] = points[0:1, :]
    start_reach(1)

    for c in range(2):
        spread_field(field2, 2 + c, shift_p.at[c])
    ice_inside(1, field2)
    shell_inside(shell2, out_block)

    rows_arrived(1, 8)
    rows_force = ice_rows(1, field2, rows_r2)
    end_contact(1)
    ice_partial(1, rows_force)
    shell_change(all_blocks, loads_of(1, own), slab_changes(1), out_block, out_get)
    columns_arrived(1, 8)
    ice_columns(1, edge_s2, edge_r2)
    ice_complete(1)
    shell_change(side_blocks, None, rim_changes([rim_terms(1, side) for side in range(2)]), out_block, out_get)

    for dx, dy in SIDES:
        with_peer(dx, dy, lambda where: group_wait(16 if dy else 20, dx, dy, 0).wait_send())

    @pl.when(is_front)
    def _():
        slots = reach_r.at[:, 0 : n_x - 1]
        pltpu.make_async_remote_copy(
            slots, slots, con_send.at[0], con_recv.at[0], device_id=(0, gy), device_id_type=MESH
        ).wait_send()

    @pl.when(jnp.logical_not(is_front))
    def _():
        pltpu.make_async_remote_copy(
            gap_r, gap_r, con_send.at[0], con_recv.at[0], device_id=(front, gy), device_id_type=MESH
        ).wait_send()


def write_out(d, v, shell, speed, d_hbm, v_hbm, shell_hbm, speed_hbm, d_own, v_own, sem):
    copies = [
        pltpu.make_async_copy(shell, shell_hbm, sem.at[0]),
        pltpu.make_async_copy(speed, speed_hbm, sem.at[1]),
    ]
    for copy in copies:
        copy.start()
    for k, (held, own, out) in enumerate(((d, d_own, d_hbm), (v, v_own, v_hbm))):
        for c in range(2):
            for a in range(8):
                own[c, a] = swap_groups(held[c, a])
        copies.append(pltpu.make_async_copy(own, out, sem.at[2 + k]))
        copies[-1].start()
    for copy in copies:
        copy.wait()


def on_device(n_x, n_y, width, d, v, j, bond, node, inter, shell, speed):
    f32, i32 = jnp.float32, jnp.int32
    vmem = pltpu.VMEM
    dma = pltpu.SemaphoreType.DMA
    shapes = [x.shape for x in (d, v, shell, speed)]
    held = pl.pallas_call(
        functools.partial(kernel, n_x, n_y, width),
        out_shape=[vmem(s, f32) for s in shapes],
        in_specs=[pl.BlockSpec(memory_space=pl.ANY)] * 8,
        out_specs=[pl.BlockSpec(memory_space=vmem)] * 4,
        scratch_shapes=[
            vmem(d.shape, f32), vmem(v.shape, f32), vmem(j.shape, f32), vmem(bond.shape, i32),
            vmem(node.shape, i32), vmem(inter.shape, f32),
            vmem((4, 80, 128), f32), vmem((4, 80, 128), f32), vmem((2, 64, 128), f32), vmem((2, 64, 128), f32),
            vmem((2, 64, 128), f32),
            vmem((2, 7, 80, 128), f32), vmem((2, 7, 80, 128), f32), vmem((9, 64, 128), i32),
            vmem((len(OFFSETS), 2, 64, 128), f32), vmem((len(ROW_OFFSETS), 2, 8, 128), f32),
            vmem((2, 7, 2, 8, 128), f32),
            vmem((2, 3, 8, 128), i32), vmem((4, 144, 128), f32), vmem((4, 144, 128), f32), vmem((4, 144, 128), f32),
            vmem((128, 128), f32),
            vmem((2, 2, 8, 128), f32), vmem((3, 2, 2, 8, 128), f32),
            vmem((2, 2, 8, 128), f32), vmem((3, 2, 2, 8, 128), f32),
            vmem((2, 3, 8, 128), f32), vmem((2, 3, 8, 128), f32), vmem((2, 2, 8, 128), f32), vmem((2, 2, 8, 128), f32),
            vmem((8, 128), f32), vmem((2, n_x, 1, 128), f32), vmem((2, 1, 128), f32),
            vmem((2, 1, 128), f32), vmem((2, n_x, 1, 128), f32), vmem((8, 128), f32),
            dma((8,)), dma((3, 3)), dma((2, 3, 3)), dma((1,)), dma((2,)),
        ],
        compiler_params=pltpu.CompilerParams(collective_id=0, has_side_effects=True),
    )(d, v, j, bond, node, inter, shell, speed)
    return pl.pallas_call(
        write_out,
        out_shape=[jax.ShapeDtypeStruct(s, f32) for s in shapes],
        in_specs=[pl.BlockSpec(memory_space=vmem)] * 4,
        out_specs=[pl.BlockSpec(memory_space=pl.ANY)] * 4,
        scratch_shapes=[vmem(shapes[0], f32), vmem(shapes[1], f32), dma((4,))],
    )(*[pltpu.with_memory_space_constraint(x, vmem) for x in held])


def solution(mesh):
    n_x, n_y = mesh.shape["gx"], mesh.shape["gy"]
    ice, plate = P(None, "gx", "gy", None), P("gx", "gy")

    def step(d, v, j, bond, *rest):
        width = rest[2].shape[1] * n_y
        return on_device(n_x, n_y, width, d, v, j, bond.reshape(-1, bond.shape[2]), *rest)

    return jax.shard_map(
        step,
        mesh=mesh,
        in_specs=(ice, ice, ice, P("gx", "gy", None), P("gy", None), P("gy", None), plate, plate),
        out_specs=(ice, ice, plate, plate),
        check_vma=False,
    )
```

```python
import functools

import jax
import jax.numpy as jnp
from jax import lax
from jax.experimental import pallas as pl
from jax.experimental.pallas import tpu as pltpu
from jax.sharding import PartitionSpec as P

MESH = pl.DeviceIdType.MESH

HORIZON = 3.5
DELTA_SQ = 0.25
PENALTY = 4.0
BEND = 0.5
STEP_DT = 0.2
RUN = 32

OFFSETS = [
    (u, v)
    for u in range(-3, 4)
    for v in range(-3, 4)
    if (u, v) != (0, 0) and max(abs(u) - 0.4, 0) ** 2 + max(abs(v) - 0.4, 0) ** 2 < HORIZON**2 - DELTA_SQ
]
ROW_OFFSETS = [(u, v) for u, v in OFFSETS if u > 0]
SIDES = [(dx, dy) for dx in (-1, 0, 1) for dy in (-1, 0, 1) if (dx, dy) != (0, 0)]


def iota(axis):
    return lax.broadcasted_iota(jnp.int32, (8, 128), axis)


def pick(x, index, axis):
    return jnp.take_along_axis(x, index, axis=axis, mode="promise_in_bounds")


def swap_groups(x):
    sub, group = iota(0), iota(1) // 16
    x = pltpu.roll(x, 0, 1, stride=16, stride_axis=0)
    x = pick(x, (group - sub) & 7, 0)
    return pick(x, ((group + sub) & 7) * 16 + (iota(1) & 15), 1)


def turn(x, shift):
    shift = shift % 128
    return pltpu.roll(x, shift, 1) if shift else x


def slide(x, shift):
    return pltpu.roll(x, shift % 8, 0)


def bonds(intact, square):
    inverse = lax.rsqrt(square)
    reach = jnp.maximum(HORIZON - square * inverse, 0.0)
    near = intact * (reach * reach)
    return near, near * inverse


def intact_of(word, bit):
    return jnp.where((word & bit) != 0, 1.0 / HORIZON**2, 0.0)


def bit_at(row, beyond):
    return jnp.left_shift(1, 4 * (row & 7) + ((beyond & 7) >> 1))


def kernel(
    n_x, n_y, width,
    d_hbm, v_hbm, j_hbm, bond_hbm, node_hbm, inter_hbm, s_hbm, w_hbm,
    d_out, v_out, s_out, shell_v, square, rim_out,
    d_in, v_in, j_in, bond, node, inter,
    field1, field2, disp, vel, force, shift_j, shift_p, words, coef, row_coef, col_coef,
    row_words, shell1, shell2, bend1,
    edge_s1, edge_r1, edge_s2, edge_r2, rows_s1, rows_r1, rows_s2, rows_r2,
    gap_all, gap_s, gap_r, reach_s, reach_r, push,
    in_sem, send_sem, recv_sem, con_send, con_recv,
):
    f32 = jnp.float32
    gx, gy = lax.axis_index("gx"), lax.axis_index("gy")
    front = n_x - 1
    is_front = gx == front
    has_up, has_down, has_left, has_right = gx > 0, gx < n_x - 1, gy > 0, gy < n_y - 1
    sub, lane = iota(0), iota(1)
    zero = jnp.zeros((8, 128), f32)

    across = {-1: has_left, 1: has_right}
    along = {-1: has_up, 1: has_down}

    def with_peer(dx, dy, run):
        there = along[dx] & across[dy] if dx and dy else along[dx] if dx else across[dy]

        @pl.when(there)
        def _():
            run((gx + dx, gy + dy))

    barrier = pltpu.get_barrier_semaphore()

    def greet(where):
        pl.semaphore_signal(barrier, inc=1, device_id=where, device_id_type=MESH)

    for dx, dy in SIDES:
        with_peer(dx, dy, greet)

    @pl.when(is_front)
    def _():
        for i in range(n_x - 2):
            greet((i, gy))

    @pl.when(gx < n_x - 2)
    def _():
        greet((front, gy))

    def load(src, dst, k):
        return pltpu.make_async_copy(src, dst, in_sem.at[k])

    def span(kib):
        return coef.at[0 : kib // 4, 0, 0:8, :]

    first = [load(j_hbm, j_in, 0), load(d_hbm, d_in, 1), load(node_hbm, node, 2), load(inter_hbm, inter, 3)]
    plate = [load(s_hbm.at[:, 128 * k : 128 * k + 128], shell1.at[k, 8:136, :], 4) for k in range(4)]
    later = [load(bond_hbm, bond, 5), load(v_hbm, v_in, 6), load(w_hbm, shell_v, 7)]
    for copy in first + plate + later:
        copy.start()

    for r in (0, 72):
        for c in range(2):
            for v in range(7):
                shift_j[c, v, r : r + 8, :] = zero
                shift_p[c, v, r : r + 8, :] = zero
        for c in range(4):
            field1[c, r : r + 8, :] = zero
            field2[c, r : r + 8, :] = zero
    for field in (shell1, shell2):
        for r in (0, 136):
            for k in range(4):
                field[k, r : r + 8, :] = zero
    for b in range(1, 15):
        square[8 * b : 8 * b + 8, :] = zero

    first[0].wait()
    first[1].wait()
    for a in range(8):
        rows = pl.ds(8 + 8 * a, 8)
        for c in range(2):
            jit = swap_groups(j_in[c, a])
            dis = swap_groups(d_in[c, a])
            field1[c, rows, :] = jit
            field1[2 + c, rows, :] = jit + dis
            disp[c, pl.ds(8 * a, 8), :] = dis

    def edges(field, base):
        stack = jnp.concatenate([field[base, 8:72, :], field[base + 1, 8:72, :]], axis=0)
        across = jnp.transpose(stack)
        return across[0:8, :], across[120:128, :]

    jit_left, jit_right = edges(field1, 0)
    pos_left, pos_right = edges(field1, 2)
    edge_s1[0, 0] = jnp.where(sub < 3, jit_left, slide(pos_left, 3))
    edge_s1[1, 0] = jnp.where(sub > 4, jit_right, slide(pos_right, -3))

    def pack_rows(field, base):
        x, y = field[base, 8:16, :], field[base + 1, 8:16, :]
        first_rows = jnp.where(sub < 3, x, slide(y, 3))
        x, y = field[base, 64:72, :], field[base + 1, 64:72, :]
        return first_rows, jnp.where(sub > 4, x, slide(y, -3))

    for part, base in enumerate((0, 2)):
        rows_s1[0, part], rows_s1[1, part] = pack_rows(field1, base)

    def pack_slab(field):
        ends = []
        for start, at in ((8, 0), (128, 6)):
            total = zero
            for c in range(4):
                total = jnp.where(sub // 2 == c, slide(field[c, start : start + 8, :], 2 * c - at), total)
            ends.append(total)
        return ends

    first[2].wait()
    first[3].wait()
    inter[...] = swap_groups(inter[...])
    node[...] = swap_groups(node[...])

    def put_gap(step):
        gap = disp[0, 56:64, :] + inter[...]
        gap_all[...] = gap
        for i in range(8):
            gap_s[step, i] = gap[i : i + 1, :]

    put_gap(0)

    mine = jnp.broadcast_to(node[pl.ds(gx, 1), :], (8, 128))
    targets = []
    for k in range(4):
        n = pick(mine, 32 * k + lane // 4, 1)
        row = lax.shift_right_logical(n, width.bit_length() - 1) & 127
        targets.append(jnp.where((n & 3) == (lane & 3), row, -1))

    def gather_points(totals):
        own = []
        points = zero
        for k, total in enumerate(totals):
            for s in (4, 2, 1):
                total = total + slide(total, s)
            own.append(total)
            total = total + turn(total, -1)
            total = total + turn(total, -2)
            points = jnp.where(lane // 32 == k, pick(total, (lane & 31) * 4, 1), points)
        return own, points

    def touched(field):
        totals = []
        for k in range(4):
            total = zero
            for b in range(16):
                x = field[k, 8 + 8 * b : 16 + 8 * b, :]
                total = total + jnp.where(sub + 8 * b == targets[k], x, 0.0)
            totals.append(total)
        return totals

    def pack_rim(field):
        left = right = zero
        for b in range(16):
            here = lane // 2 == b
            left = jnp.where(here, turn(field[0, 8 + 8 * b : 16 + 8 * b, :], 2 * b), left)
            right = jnp.where(here, turn(field[3, 8 + 8 * b : 16 + 8 * b, :], 2 * b + 2), right)
        return left, right

    load(shell1.at[:, 8:136, :], shell1.at[:, 8:136, :], 4).wait()
    own, points = gather_points(touched(shell1))
    reach_s[0] = points[0:1, :]
    left, right = pack_rim(shell1)
    edge_s1[0, 1] = left
    edge_s1[1, 1] = right
    rows_s1[0, 2], rows_s1[1, 2] = pack_slab(shell1)

    n_along = has_up.astype(jnp.int32) + has_down.astype(jnp.int32)
    n_across = has_left.astype(jnp.int32) + has_right.astype(jnp.int32)
    extra = jnp.where(is_front, n_x - 2, jnp.where(gx < n_x - 2, 1, 0))
    pl.semaphore_wait(barrier, n_along + n_across + n_along * n_across + extra)

    def send(src, dst, phase, dx, dy):
        with_peer(dx, dy, lambda where: pltpu.make_async_remote_copy(
            src, dst, send_sem.at[1 - dx, 1 - dy], recv_sem.at[phase, 1 - dx, 1 - dy],
            device_id=where, device_id_type=MESH,
        ).start())

    def send_columns(phase, src, dst):
        for dx in (-1, 1, 0):
            for dy in (-1, 1):
                side = (dy + 1) // 2
                send(src.at[side], dst.at[1 - dx, 1 - side], phase, dx, dy)

    def send_rows(phase, src, dst):
        for k, dx in enumerate((-1, 1)):
            send(src.at[k], dst.at[1 - k], phase, dx, 0)

    def group_wait(kib, dx, dy, phase):
        return pltpu.make_async_remote_copy(
            span(kib), span(kib), send_sem.at[1 - dx, 1 - dy], recv_sem.at[phase, 1 + dx, 1 + dy],
            device_id=(0, 0), device_id_type=MESH,
        )

    def rows_arrived(phase, kib):
        for dx in (-1, 1):
            with_peer(dx, 0, lambda where: group_wait(kib, dx, 0, phase).wait_recv())

    def columns_arrived(phase, kib):
        for dy in (-1, 1):
            for dx in (0, -1, 1):
                with_peer(dx, dy, lambda where: group_wait(kib, dx, dy, phase).wait_recv())

    def gap_copy(step, i):
        return pltpu.make_async_remote_copy(
            gap_s.at[step, i], gap_r.at[step], con_send.at[0], con_recv.at[step],
            device_id=(i, gy), device_id_type=MESH,
        )

    def reach_copy(step):
        return pltpu.make_async_remote_copy(
            reach_s.at[step], reach_r.at[step, gx], con_send.at[0], con_recv.at[step],
            device_id=(front, gy), device_id_type=MESH,
        )

    def start_gap(step):
        @pl.when(is_front)
        def _():
            for i in range(n_x - 1):
                gap_copy(step, i).start()
            gap_r[step] = gap_s[step, n_x - 1]

    def start_reach(step):
        @pl.when(is_front)
        def _():
            reach_r[step, front] = reach_s[step]

        @pl.when(jnp.logical_not(is_front))
        def _():
            reach_copy(step).start()

    def end_contact(step):
        @pl.when(is_front)
        def _():
            slots = reach_r.at[step, 0 : n_x - 1]
            pltpu.make_async_remote_copy(
                slots, slots, con_send.at[0], con_recv.at[step], device_id=(0, gy), device_id_type=MESH
            ).wait_recv()
            reached = jnp.broadcast_to(reach_r[step, front], (8, 128))
            for i in range(n_x - 1):
                reached = jnp.where(sub == i, jnp.broadcast_to(reach_r[step, i], (8, 128)), reached)
            push[...] = PENALTY * jnp.maximum(gap_all[...] - reached, 0.0)

        @pl.when(jnp.logical_not(is_front))
        def _():
            gap_copy(step, 0).wait_recv()
            push[...] = jnp.zeros((8, 128), f32)

    send_columns(0, edge_s1, edge_r1)
    send_rows(0, rows_s1, rows_r1)
    start_gap(0)
    start_reach(0)

    later[0].wait()
    none = jnp.zeros((8, 128), jnp.int32)
    for s in range(9):
        for a in range(8):
            word = pick(jnp.broadcast_to(bond[8 * a : 8 * a + 8, s : s + 1], (8, 128)), lane // 16, 0)
            if s % 3 == 0:
                word = jnp.where(lane < 16, 0, word)
            if s % 3 == 2:
                word = jnp.where(lane >= 112, 0, word)
            if a == 0 and s < 3:
                row_words[0, s] = word
                word = none
            if a == 7 and s > 5:
                row_words[1, s - 6] = word
                word = none
            words[s, 8 * a : 8 * a + 8, :] = word
    col_words = []
    for side in range(2):
        tiles = bond[pl.ds(7 * side, 8, stride=8), :]
        for dx in range(3):
            s = 3 * dx + 2 * side
            word = jnp.broadcast_to(tiles[:, s : s + 1], (8, 128))
            col_words.append(pick(word, (lane & 63) // 8, 0))
    later[1].wait()
    for a in range(8):
        for c in range(2):
            vel[c, pl.ds(8 * a, 8), :] = swap_groups(v_in[c, a])

    def spread_field(field, index, out):
        for b in range(1, 9):
            x = field[index, 8 * b : 8 * b + 8, :]
            for v in range(-3, 4):
                if v:
                    out[v + 3, 8 * b : 8 * b + 8, :] = turn(x, -v)

    def ice_inside(step, field):
        last = step == 1
        sub_r = lax.broadcasted_iota(jnp.int32, (RUN, 128), 0)
        lane_r = lax.broadcasted_iota(jnp.int32, (RUN, 128), 1)
        tile_row, tile_col = sub_r & 7, lane_r & 15

        def body(a, carry):
            base = pl.multiple_of(RUN * a, RUN)
            rows = pl.ds(base, RUN)
            own = pl.ds(pl.multiple_of(base + 8, 8), RUN)

            def partner(shifted, c, u, v):
                there = pl.ds(base + (8 + u), RUN)
                if v == 0:
                    return field[(0 if shifted is shift_j else 2) + c, there, :]
                return shifted[c, v + 3, there, :]

            px = field[2, own, :]
            py = [field[3, own, :] - float(v) for v in range(-3, 4)]
            if not last:
                jx = field[0, own, :]
                jy = [field[1, own, :] - float(v) for v in range(-3, 4)]
            fx = fy = jnp.zeros((RUN, 128), f32)
            seen = None
            for n, (u, v) in enumerate(OFFSETS):
                if u != seen:
                    seen = u
                    px_u = px - float(u)
                    if not last:
                        jx_u = jx - float(u)
                        bit = bit_at(tile_row, tile_row + u)
                        flags = []
                        for dy in range(3):
                            word = words[3 + dy, rows, :]
                            if u < 0:
                                word = jnp.where(tile_row + u < 0, words[dy, rows, :], word)
                            if u > 0:
                                word = jnp.where(tile_row + u > 7, words[6 + dy, rows, :], word)
                            flags.append(intact_of(word, bit))
                if not last:
                    intact = flags[1]
                    if v < 0:
                        intact = jnp.where(tile_col + v < 0, flags[0], intact)
                    if v > 0:
                        intact = jnp.where(tile_col + v > 15, flags[2], intact)
                    rx = partner(shift_j, 0, u, v) - jx_u
                    ry = partner(shift_j, 1, u, v) - jy[v + 3]
                    near, far = bonds(intact, rx * rx + ry * ry + DELTA_SQ)
                    coef[n, 0, rows, :] = near
                    coef[n, 1, rows, :] = far
                else:
                    near = coef[n, 0, rows, :]
                    far = coef[n, 1, rows, :]
                nx = partner(shift_p, 0, u, v) - px_u
                ny = partner(shift_p, 1, u, v) - py[v + 3]
                factor = far - near * lax.rsqrt(nx * nx + ny * ny + DELTA_SQ)
                fx = fx + factor * nx
                fy = fy + factor * ny
            force[0, rows, :] = fx
            force[1, rows, :] = fy
            return carry

        lax.fori_loop(0, 64 // RUN, body, 0)

    top = sub < 4

    def row_flags():
        word = [jnp.where(top, row_words[0, dy], row_words[1, dy]) for dy in range(3)]
        seen = None
        for n, (u, v) in enumerate(ROW_OFFSETS):
            if u != seen:
                seen = u
                inside = ((sub < u) & has_up) | ((sub >= 8 - u) & has_down)
                bit = bit_at(sub, sub + jnp.where(top, -u, u))
                flags = [jnp.where(inside, intact_of(w, bit), 0.0) for w in word]
            intact = flags[1]
            if v < 0:
                intact = jnp.where((lane & 15) + v < 0, flags[0], intact)
            if v > 0:
                intact = jnp.where((lane & 15) + v > 15, flags[2], intact)
            row_coef[n, 0] = intact

    def ice_rows(step, field, rows_r):
        last = step == 1
        base = 2 if last else 0
        mine = [jnp.where(top, field[c, 8:16, :], field[c, 64:72, :]) for c in range(base, 4)]
        mine_y = [[mine[c] - float(v) for v in range(-3, 4)] for c in range(1, 4 - base, 2)]
        fx = fy = zero
        seen = None
        for n, (u, v) in enumerate(ROW_OFFSETS):
            if u != seen:
                seen = u
                beyond = [
                    jnp.where(top, slide(rows_r[0, c // 2], u + 3 * (c % 2)), slide(rows_r[1, c // 2], -u - 3 * (c % 2)))
                    for c in range(4 - base)
                ]
                by = jnp.where(top, -float(u), float(u))
                mine_x = [mine[c] - by for c in range(0, 4 - base, 2)]
            near = row_coef[n, 0]
            if not last:
                rx = turn(beyond[0], -v) - mine_x[0]
                ry = turn(beyond[1], -v) - mine_y[0][v + 3]
                near, far = bonds(near, rx * rx + ry * ry + DELTA_SQ)
                row_coef[n, 0] = near
                row_coef[n, 1] = far
            else:
                far = row_coef[n, 1]
            nx = turn(beyond[2 - base], -v) - mine_x[-1]
            ny = turn(beyond[3 - base], -v) - mine_y[-1][v + 3]
            factor = far - near * lax.rsqrt(nx * nx + ny * ny + DELTA_SQ)
            fx = fx + factor * nx
            fy = fy + factor * ny
        present = (top & has_up) | (jnp.logical_not(top) & has_down)
        return jnp.where(present, fx, 0.0), jnp.where(present, fy, 0.0)

    near_col = jnp.where(sub < 3, 0, jnp.where(sub < 5, 1, 2))
    far_col = jnp.where(sub < 3, sub + 1, jnp.where(sub < 5, sub - 2, 1))
    point_row = lane & 63

    def column_flags():
        for side in range(2):
            there = (sub < 6) & (has_right if side else has_left)
            for u in range(-3, 4):
                word = col_words[3 * side + 1]
                present = there
                if u < 0:
                    word = jnp.where((lane & 7) + u < 0, col_words[3 * side], word)
                    present = there & ((point_row + u >= 0) | has_up)
                if u > 0:
                    word = jnp.where((lane & 7) + u > 7, col_words[3 * side + 2], word)
                    present = there & ((point_row + u <= 63) | has_down)
                col_coef[side, u + 3, 0] = jnp.where(present, intact_of(word, bit_at(lane, lane + u)), 0.0)

    def ice_columns(step, edge_s, edge_r):
        last = step == 1
        parts = (0,) if last else (0, 1)
        sides = []
        for side in range(2):
            mine_at = 7 - near_col if side else near_col
            beyond_at = far_col - 1 if side else 8 - far_col
            shifts = [3 * p for p in parts]
            by = jnp.where(lane < 64, 0.0, (near_col + far_col).astype(f32) * (1.0 if side else -1.0))
            mine = [pick(edge_s[side, 0], mine_at - h if side else mine_at + h, 0) - by for h in shifts]
            beyond = [
                [pick(edge_r[slot, side, 0], beyond_at + h if side else beyond_at - h, 0) for slot in range(3)]
                for h in shifts
            ]
            total = zero
            for u in range(-3, 4):
                def moved(p):
                    if u == 0:
                        return beyond[p][1]
                    inside = (point_row + u >= 0) | jnp.logical_not(has_up)
                    if u > 0:
                        inside = (point_row + u <= 63) | jnp.logical_not(has_down)
                    return jnp.where(inside, turn(beyond[p][1], -u), turn(beyond[p][0 if u < 0 else 2], 64 - u))

                offset = jnp.where(lane < 64, float(u), 0.0)
                near = col_coef[side, u + 3, 0]
                if not last:
                    rest = moved(0) - (mine[0] - offset)
                    square_of = rest * rest
                    near, far = bonds(near, square_of + turn(square_of, 64) + DELTA_SQ)
                    col_coef[side, u + 3, 0] = near
                    col_coef[side, u + 3, 1] = far
                else:
                    far = col_coef[side, u + 3, 1]
                now = moved(len(parts) - 1) - (mine[-1] - offset)
                square_of = now * now
                factor = far - near * lax.rsqrt(square_of + turn(square_of, 64) + DELTA_SQ)
                total = total + factor * now
            at = 7 - sub if side else sub
            total = jnp.where(has_right if side else has_left, total, 0.0)
            sides.append(
                jnp.where(at < 3, pick(total, jnp.where(at == 0, 0, jnp.where(at == 1, 3, 5)), 0), 0.0)
                + jnp.where(at < 2, pick(total, jnp.where(at == 0, 1, 4), 0), 0.0)
                + jnp.where(at == 0, pick(total, jnp.full((8, 128), 2, jnp.int32), 0), 0.0)
            )
            square[120 * side : 120 * side + 8, :] = sides[side]
        return sides

    def ice_partial(step, rows_force):
        for a in range(8):
            rows = pl.ds(8 * a, 8)
            for c in range(2):
                total = force[c, rows, :]
                if a == 0:
                    total = total + jnp.where(top, rows_force[c], 0.0)
                if a == 7:
                    total = total + jnp.where(top, 0.0, rows_force[c])
                    if c == 0:
                        total = total - push[...]
                speed = vel[c, rows, :] + STEP_DT * total
                moved = disp[c, rows, :] + STEP_DT * speed
                if step == 1:
                    v_out[c, a] = speed
                    d_out[c, a] = moved
                else:
                    vel[c, rows, :] = speed
                    disp[c, rows, :] = moved
                    field2[2 + c, 8 + 8 * a : 16 + 8 * a, :] = field1[c, 8 + 8 * a : 16 + 8 * a, :] + moved

    def ice_complete():
        sides_force = jnp.transpose(square[...])
        for a in range(8):
            rows = pl.ds(8 * a, 8)
            for c in range(2):
                push_on = STEP_DT * sides_force[64 * c + 8 * a : 64 * c + 8 * a + 8, :]
                vel[c, rows, :] = vel[c, rows, :] + push_on
                shift = STEP_DT * push_on
                disp[c, rows, :] = disp[c, rows, :] + shift
                there = slice(8 + 8 * a, 16 + 8 * a)
                field2[2 + c, there, :] = field2[2 + c, there, :] + shift

    def sideways(x, first, last):
        up = [turn(c, 1) for c in x]
        down = [turn(c, -1) for c in x]
        return [
            jnp.where(lane == 0, up[k - 1] if k else first, up[k])
            + jnp.where(lane == 127, down[k + 1] if k < 3 else last, down[k])
            for k in range(4)
        ]

    def shell_inside(field, put):
        def chunks(ref, start):
            return [ref[k, pl.ds(start, 8), :] for k in range(4)]

        def once(b, carry):
            for h in range(4):
                i = pl.multiple_of(32 * b + 8 * h + 8, 8)
                f, up, down = chunks(field, i), chunks(field, i - 1), chunks(field, i + 1)
                for k, side in enumerate(sideways(f, 0.0, 0.0)):
                    bend1[k, pl.ds(i, 8), :] = (up[k] + down[k]) + side - 4.0 * f[k]
            return carry

        def twice(b, carry):
            for h in range(4):
                base = pl.multiple_of(32 * b + 8 * h, 8)
                i = pl.multiple_of(base + 8, 8)
                f, g = chunks(field, i), chunks(bend1, i)
                up, down = chunks(bend1, i - 1), chunks(bend1, i + 1)
                for k, side in enumerate(sideways(g, f[0], f[3])):
                    at = (pl.ds(base, 8), slice(128 * k, 128 * k + 128))
                    bending = (up[k] + down[k]) + side - 4.0 * g[k]
                    speed = shell_v[at] - (STEP_DT * BEND) * bending
                    shell_v[at] = speed
                    put(base, k, f[k] + STEP_DT * speed)
            return carry

        lax.fori_loop(0, 4, once, 0)
        for k in range(4):
            bend1[k, 7:8, :] = field[k, 8:9, :]
            bend1[k, 136:137, :] = field[k, 135:136, :]
        lax.fori_loop(0, 4, twice, 0)

    def rim_terms(step, side):
        edge_r = edge_r2 if step else edge_r1
        above, level, below = (edge_r[t, side, 1] for t in range(3))
        level = jnp.where(lane < 2, jnp.where(has_up, turn(above, -30), 0.0), turn(level, 2))
        rim = jnp.where(lane >= 34, jnp.where(has_down, turn(below, 34), 0.0), level)
        rim = jnp.where(has_right if side else has_left, rim, 0.0)
        first = turn(rim, 1 if side else -1)
        up, down = slide(first, 1), slide(first, -1)
        up = jnp.where(sub == 0, turn(up, 2), up)
        down = jnp.where(sub == 7, turn(down, -2), down)
        full = rim - 8.0 * first + 2.0 * (up + down)
        return jnp.where((lane & 1) == side, full, rim)

    def slab_terms(step):
        terms = []
        for k in range(2):
            slab = rows_r1[k, 2] if step == 0 else rows_r2[k, 1]
            slab = jnp.where(has_down if k else has_up, slab, 0.0)
            outer = [slide(slab, (6 if k else 0) - 2 * c) for c in range(4)]
            inner = [slide(slab, (7 if k else -1) - 2 * c) for c in range(4)]
            at = 7 - sub if k else sub
            terms.append(
                [
                    jnp.where(at < 2, o, 0.0) + jnp.where(at == 0, 2.0 * pair - 8.0 * x, 0.0)
                    for o, x, pair in zip(outer, inner, sideways(inner, 0.0, 0.0))
                ]
            )
        return terms

    all_blocks = [(k, b) for k in range(4) for b in range(16)]
    end_blocks = [(k, b) for k in range(4) for b in (0, 15)]
    side_blocks = [(k, b) for k in (0, 3) for b in range(16)]

    def loads_of(step, own):
        gaps = jnp.broadcast_to(gap_r[step], (8, 128))
        return [
            (STEP_DT * PENALTY) * jnp.maximum(pick(gaps, 32 * k + lane // 4, 1) - own[k], 0.0) for k in range(4)
        ]

    def slab_changes(step):
        slabs = slab_terms(step)
        return {(k, b): (-STEP_DT * BEND) * slabs[b // 15][k] for k, b in end_blocks}

    def rim_changes(rims):
        changes = {}
        for k, b in side_blocks:
            rim = turn(rims[k // 3], (124 if k else -2) - 2 * b)
            changes[k, b] = (-STEP_DT * BEND) * jnp.where(lane >= 126 if k else lane < 2, rim, 0.0)
        return changes

    def shell_change(blocks, load, changes, put, get):
        for k, b in blocks:
            change = None if load is None else jnp.where(sub + 8 * b == targets[k], load[k], 0.0)
            if (k, b) in changes:
                change = changes[k, b] if change is None else change + changes[k, b]
            at = (pl.ds(8 * b, 8), slice(128 * k, 128 * k + 128))
            shell_v[at] = shell_v[at] + change
            put(8 * b, k, get(8 * b, k) + STEP_DT * change)

    def put_block(base, k, moved):
        shell2[k, pl.ds(base + 8, 8), :] = moved

    def get_block(base, k):
        return shell2[k, pl.ds(base + 8, 8), :]

    def out_block(base, k, moved):
        s_out[pl.ds(base, 8), 128 * k : 128 * k + 128] = moved

    def out_get(base, k):
        return s_out[pl.ds(base, 8), 128 * k : 128 * k + 128]

    row_flags()
    column_flags()
    for c in range(2):
        spread_field(field1, c, shift_j.at[c])
        spread_field(field1, 2 + c, shift_p.at[c])
    ice_inside(0, field1)
    later[2].wait()
    shell_inside(shell1, put_block)

    rows_arrived(0, 12)
    rows_force = ice_rows(0, field1, rows_r1)
    end_contact(0)
    ice_partial(0, rows_force)
    edge_left, edge_right = edges(field2, 2)
    shell_change(all_blocks, loads_of(0, own), slab_changes(0), put_block, get_block)
    rim_left, rim_right = pack_rim(shell2)

    columns_arrived(0, 8)
    sides_left, sides_right = ice_columns(0, edge_s1, edge_r1)
    edge_s2[0, 0] = edge_left + STEP_DT**2 * sides_left
    edge_s2[1, 0] = edge_right + STEP_DT**2 * sides_right
    rims = [rim_terms(0, side) for side in range(2)]
    edge_s2[0, 1] = rim_left - (STEP_DT**2 * BEND) * turn(rims[0], -2)
    edge_s2[1, 1] = rim_right - (STEP_DT**2 * BEND) * turn(rims[1], -2)
    send_columns(1, edge_s2, edge_r2)

    ice_complete()
    rows_s2[0, 0], rows_s2[1, 0] = pack_rows(field2, 2)
    put_gap(1)
    start_gap(1)
    shell_change(side_blocks, None, rim_changes(rims), put_block, get_block)
    rows_s2[0, 1], rows_s2[1, 1] = pack_slab(shell2)
    send_rows(1, rows_s2, rows_r2)
    own, points = gather_points(touched(shell2))
    reach_s[1] = points[0:1, :]
    start_reach(1)

    for c in range(2):
        spread_field(field2, 2 + c, shift_p.at[c])
    ice_inside(1, field2)
    shell_inside(shell2, out_block)

    rows_arrived(1, 8)
    rows_force = ice_rows(1, field2, rows_r2)
    end_contact(1)
    ice_partial(1, rows_force)
    shell_change(all_blocks, loads_of(1, own), slab_changes(1), out_block, out_get)
    columns_arrived(1, 8)
    ice_columns(1, edge_s2, edge_r2)
    for side in range(2):
        rim_out[side] = rim_terms(1, side)

    for dx, dy in SIDES:
        with_peer(dx, dy, lambda where: group_wait(16 if dy else 20, dx, dy, 0).wait_send())

    @pl.when(is_front)
    def _():
        slots = reach_r.at[:, 0 : n_x - 1]
        pltpu.make_async_remote_copy(
            slots, slots, con_send.at[0], con_recv.at[0], device_id=(0, gy), device_id_type=MESH
        ).wait_send()

    @pl.when(jnp.logical_not(is_front))
    def _():
        pltpu.make_async_remote_copy(
            gap_r, gap_r, con_send.at[0], con_recv.at[0], device_id=(front, gy), device_id_type=MESH
        ).wait_send()


def write_out(
    d, v, shell, speed, square, rims, d_hbm, v_hbm, shell_hbm, speed_hbm, d_own, v_own, shell_own, speed_own, sem
):
    lane = iota(1)
    copies = []

    def put(src, dst):
        copies.append(pltpu.make_async_copy(src, dst, sem.at[len(copies)]))
        copies[-1].start()

    put(shell.at[:, 128:384], shell_hbm.at[:, 128:384])
    put(speed.at[:, 128:384], speed_hbm.at[:, 128:384])
    for side in range(2):
        at = slice(384 * side, 384 * side + 128)
        for b in range(16):
            rows = slice(8 * b, 8 * b + 8)
            rim = turn(rims[side], (124 if side else -2) - 2 * b)
            change = (-STEP_DT * BEND) * jnp.where(lane >= 126 if side else lane < 2, rim, 0.0)
            speed_own[side, rows, :] = speed[rows, at] + change
            shell_own[side, rows, :] = shell[rows, at] + STEP_DT * change
        put(speed_own.at[side], speed_hbm.at[:, at])
        put(shell_own.at[side], shell_hbm.at[:, at])
    sides_force = jnp.transpose(square[...])
    for c in range(2):
        for a in range(8):
            push_on = STEP_DT * sides_force[64 * c + 8 * a : 64 * c + 8 * a + 8, :]
            v_own[c, a] = swap_groups(v[c, a] + push_on)
            d_own[c, a] = swap_groups(d[c, a] + STEP_DT * push_on)
    put(v_own, v_hbm)
    put(d_own, d_hbm)
    for copy in copies:
        copy.wait()


def on_device(n_x, n_y, width, d, v, j, bond, node, inter, shell, speed):
    f32, i32 = jnp.float32, jnp.int32
    vmem = pltpu.VMEM
    dma = pltpu.SemaphoreType.DMA
    shapes = [x.shape for x in (d, v, shell, speed)]
    held = pl.pallas_call(
        functools.partial(kernel, n_x, n_y, width),
        out_shape=[vmem(s, f32) for s in shapes + [(128, 128), (2, 8, 128)]],
        in_specs=[pl.BlockSpec(memory_space=pl.ANY)] * 8,
        out_specs=[pl.BlockSpec(memory_space=vmem)] * 6,
        scratch_shapes=[
            vmem(d.shape, f32), vmem(v.shape, f32), vmem(j.shape, f32), vmem(bond.shape, i32),
            vmem(node.shape, i32), vmem(inter.shape, f32),
            vmem((4, 80, 128), f32), vmem((4, 80, 128), f32), vmem((2, 64, 128), f32), vmem((2, 64, 128), f32),
            vmem((2, 64, 128), f32),
            vmem((2, 7, 80, 128), f32), vmem((2, 7, 80, 128), f32), vmem((9, 64, 128), i32),
            vmem((len(OFFSETS), 2, 64, 128), f32), vmem((len(ROW_OFFSETS), 2, 8, 128), f32),
            vmem((2, 7, 2, 8, 128), f32),
            vmem((2, 3, 8, 128), i32), vmem((4, 144, 128), f32), vmem((4, 144, 128), f32), vmem((4, 144, 128), f32),
            vmem((2, 2, 8, 128), f32), vmem((3, 2, 2, 8, 128), f32),
            vmem((2, 2, 8, 128), f32), vmem((3, 2, 2, 8, 128), f32),
            vmem((2, 3, 8, 128), f32), vmem((2, 3, 8, 128), f32), vmem((2, 2, 8, 128), f32), vmem((2, 2, 8, 128), f32),
            vmem((8, 128), f32), vmem((2, n_x, 1, 128), f32), vmem((2, 1, 128), f32),
            vmem((2, 1, 128), f32), vmem((2, n_x, 1, 128), f32), vmem((8, 128), f32),
            dma((8,)), dma((3, 3)), dma((2, 3, 3)), dma((1,)), dma((2,)),
        ],
        compiler_params=pltpu.CompilerParams(collective_id=0, has_side_effects=True),
    )(d, v, j, bond, node, inter, shell, speed)
    return pl.pallas_call(
        write_out,
        out_shape=[jax.ShapeDtypeStruct(s, f32) for s in shapes],
        in_specs=[pl.BlockSpec(memory_space=vmem)] * 6,
        out_specs=[pl.BlockSpec(memory_space=pl.ANY)] * 4,
        scratch_shapes=[
            vmem(shapes[0], f32), vmem(shapes[1], f32), vmem((2, 128, 128), f32), vmem((2, 128, 128), f32), dma((8,)),
        ],
    )(*[pltpu.with_memory_space_constraint(x, vmem) for x in held])


def solution(mesh):
    n_x, n_y = mesh.shape["gx"], mesh.shape["gy"]
    ice, plate = P(None, "gx", "gy", None), P("gx", "gy")

    def step(d, v, j, bond, *rest):
        width = rest[2].shape[1] * n_y
        return on_device(n_x, n_y, width, d, v, j, bond.reshape(-1, bond.shape[2]), *rest)

    return jax.shard_map(
        step,
        mesh=mesh,
        in_specs=(ice, ice, ice, P("gx", "gy", None), P("gy", None), P("gy", None), plate, plate),
        out_specs=(ice, ice, plate, plate),
        check_vma=False,
    )
```
